32 devices in a mesh: seq: 8 (over z, core), ctx: 4 (over y, x).
Axes of the slice: x: 2, y: 2, z: 4, core: 2. Of those that a mesh axis runs over, the one named last changes fastest.
Arguments:
- hidden: bfloat16 [16, 1024, 768], P('seq', 'ctx'), may hold values from -6 to 6
- segment: int32 [16, 1024], P('seq', 'ctx'), may hold values from 0 to 3, never falling along the last dimension, each value on 1 to 640 neighbouring positions
- cotangent: bfloat16 [16, 1024, 768], P('seq', 'ctx'), may hold values from -6 to 6
- w_query: bfloat16 [768, 768], P(('seq', 'ctx')), may hold values from -0.21875 to 0.21875
- b_query: bfloat16 [768], P(('seq', 'ctx')), may hold values from -2 to 2
- w_key: bfloat16 [768, 768], P(('seq', 'ctx')), may hold values from -0.21875 to 0.21875
- w_value: bfloat16 [768, 768], P(('seq', 'ctx')), may hold values from -0.21875 to 0.21875
- b_value: bfloat16 [768], P(('seq', 'ctx')), may hold values from -2 to 2
- w_output: bfloat16 [768, 768], P(('seq', 'ctx')), may hold values from -3.5 to 3.5
- b_output: bfloat16 [768], P(('seq', 'ctx')), may hold values from -2 to 2
- attn_gain: bfloat16 [768], P(('seq', 'ctx')), may hold values from 0.099609375 to 1.8984375
- attn_shift: bfloat16 [768], P(('seq', 'ctx')), may hold values from -2 to 2
- w_inner: bfloat16 [768, 3072], P(('seq', 'ctx')), may hold values from -0.21875 to 0.21875
- b_inner: bfloat16 [3072], P(('seq', 'ctx')), may hold values from -2 to 2
- w_outer: bfloat16 [3072, 768], P(('seq', 'ctx')), may hold values from -0.109375 to 0.109375
- b_outer: bfloat16 [768], P(('seq', 'ctx')), may hold values from -2 to 2
- ffn_gain: bfloat16 [768], P(('seq', 'ctx')), may hold values from 0.099609375 to 1.8984375
- ffn_shift: bfloat16 [768], P(('seq', 'ctx')), may hold values from -2 to 2
Outputs:
- output: bfloat16 [16, 1024, 768], P('seq', 'ctx')
- grad_input: float32 [16, 1024, 768], P('seq', 'ctx')
- grad_w_query: float32 [768, 768], P(('seq', 'ctx'))
- grad_b_query: float32 [768], P(('seq', 'ctx'))
- grad_w_key: float32 [768, 768], P(('seq', 'ctx'))
- grad_w_value: float32 [768, 768], P(('seq', 'ctx'))
- grad_b_value: float32 [768], P(('seq', 'ctx'))
- grad_w_output: float32 [768, 768], P(('seq', 'ctx'))
- grad_b_output: float32 [768], P(('seq', 'ctx'))
- grad_attn_gain: float32 [768], P(('seq', 'ctx'))
- grad_attn_shift: float32 [768], P(('seq', 'ctx'))
- grad_w_inner: float32 [768, 3072], P(('seq', 'ctx'))
- grad_b_inner: float32 [3072], P(('seq', 'ctx'))
- grad_w_outer: float32 [3072, 768], P(('seq', 'ctx'))
- grad_b_outer: float32 [768], P(('seq', 'ctx'))
- grad_ffn_gain: float32 [768], P(('seq', 'ctx'))
- grad_ffn_shift: float32 [768], P(('seq', 'ctx'))
The draws below stay inside these ranges and needn't reach their ends.
Inputs may be any that keep to these rules, and one draw needn't show every extreme that they name: `segment`: along each sequence the document numbers never fall; every number from 0 appears, each document has 1 to 640 tokens and one has exactly 640.
All inputs are finite; a program needn't handle non-finite values.
Results may differ from the reference program's by a relative error of at most 0.023.
Values may be sent and summed in bfloat16 or wider, within the bound.
No kernel may reach another device: no remote copies, remote signals or barrier semaphores. Data moves between devices by JAX's collectives and lax.ppermute only.
A program may use at most 192 MiB of HBM per device.

```python
import math
import jax
import jax.numpy as jnp
import numpy as np
from jax import lax

D = 768
H = 12
DH = 64
FF = 3072
LENGTH = 1024
SEQS = 16
DOCS = 4
DOC_MOST = 640


def level_of(own_key, shape, cuts, least, high):
    loudness = 1.0
    for position, shards_of in cuts:
        draws = jax.random.uniform(jax.random.fold_in(jax.random.fold_in(own_key, 6), position), (shards_of,), jnp.float32, least / len(cuts), high / len(cuts))
        loudness = loudness * jnp.repeat(jnp.exp(draws), shape[position] // shards_of).reshape((-1,) + (1,) * (len(shape) - 1 - position))
    return loudness


def profile(amount, total, limit, skew):
    portions = [(1 << 20) // math.isqrt(rank ** skew) + 1 for rank in range(2, amount + 1)]
    spare, holding = total - limit - (amount - 1), [1] * (amount - 1)
    while spare > 0:
        free = [i for i in range(amount - 1) if holding[i] < limit]
        pool, budget = sum([portions[i] for i in free]), spare
        for i in free:
            addition = min(limit - holding[i], max(1, budget * portions[i] // pool), spare)
            holding[i] = holding[i] + addition
            spare = spare - addition
    return np.array([limit] + holding)


def uneven(key, number_of, total, reach, lean):
    if number_of == 2:
        one = jax.random.randint(key, (), max(1, total - reach), min(reach, total - 1) + 1)
        return jnp.stack([one, total - one])
    lengths = jnp.asarray(profile(number_of, total, reach, lean), jnp.int32)
    couples = (number_of - 1) // 2
    source_of, sink = lengths[1:1 + 2 * couples:2], lengths[2:2 + 2 * couples:2]
    room = jnp.minimum(source_of - 1, reach - sink)
    shifted = jax.random.randint(jax.random.fold_in(key, 1), (couples,), 0, 1 << 20) % (room + 1)
    lengths = lengths.at[1:1 + 2 * couples:2].set(source_of - shifted).at[2:2 + 2 * couples:2].set(sink + shifted)
    return lengths[jax.random.permutation(jax.random.fold_in(key, 2), number_of)]


def scatter_about(stream_key, extent, width, limit, split=(), held_as=jnp.bfloat16):
    entries = width * jax.random.normal(stream_key, extent, jnp.float32)
    if split:
        entries = entries * level_of(stream_key, extent, split, -0.22, 0.18)
    return jnp.clip(entries, -limit, limit).astype(held_as)


def setup_inputs(seed: int = 0) -> dict:
    streams_of = jax.random.split(jax.random.key(seed), 19)
    return {
        "hidden": scatter_about(streams_of[0], (SEQS, LENGTH, D), 1.0, 6.0, ((0, 8), (1, 4))),
        "segment": jax.vmap(lambda own: jnp.searchsorted(jnp.cumsum(uneven(own, DOCS, LENGTH, DOC_MOST, 0)), jnp.arange(LENGTH), side="right"))(jax.random.split(streams_of[1], SEQS)).reshape((SEQS, LENGTH)).astype(jnp.int32),
        "cotangent": scatter_about(streams_of[2], (SEQS, LENGTH, D), 1.0, 6.0, ((0, 8), (1, 4))),
        "w_query": scatter_about(streams_of[3], (D, D), D ** -0.5, 0.21875, ((0, 32),)),
        "b_query": scatter_about(streams_of[4], (D,), 0.3, 2.0, ((0, 32),)),
        "w_key": scatter_about(streams_of[5], (D, D), D ** -0.5, 0.21875, ((0, 32),)),
        "w_value": scatter_about(streams_of[6], (D, D), D ** -0.5, 0.21875, ((0, 32),)),
        "b_value": scatter_about(streams_of[7], (D,), 0.3, 2.0, ((0, 32),)),
        "w_output": scatter_about(streams_of[8], (D, D), (D // 256) ** -0.5, 3.5, ((0, 32),)),
        "b_output": scatter_about(streams_of[9], (D,), 0.3, 2.0, ((0, 32),)),
        "attn_gain": jnp.clip(1.0 + 0.18 * jax.random.normal(streams_of[10], (D,), jnp.float32), 0.099609375, 1.8984375).astype(jnp.bfloat16),
        "attn_shift": scatter_about(streams_of[11], (D,), 0.3, 2.0, ((0, 32),)),
        "w_inner": scatter_about(streams_of[12], (D, FF), D ** -0.5, 0.21875, ((0, 32),)),
        "b_inner": scatter_about(streams_of[13], (FF,), 0.3, 2.0, ((0, 32),)),
        "w_outer": scatter_about(streams_of[14], (FF, D), FF ** -0.5, 0.109375, ((0, 32),)),
        "b_outer": scatter_about(streams_of[15], (D,), 0.3, 2.0, ((0, 32),)),
        "ffn_gain": jnp.clip(1.0 + 0.18 * jax.random.normal(streams_of[16], (D,), jnp.float32), 0.099609375, 1.8984375).astype(jnp.bfloat16),
        "ffn_shift": scatter_about(streams_of[17], (D,), 0.3, 2.0, ((0, 32),)),
    }


@jax.custom_vjp
def low(v):
    return lax.optimization_barrier(v.astype(jnp.bfloat16)).astype(jnp.float32)

@jax.custom_vjp
def low_back(v):
    return v

def low_keep(v):
    return (low(v), None)

def low_pass(kept, grad):
    return (grad,)

def back_keep(v):
    return (v, None)

def back_low(kept, grad):
    return (low(grad),)
low.defvjp(low_keep, low_pass)
low_back.defvjp(back_keep, back_low)
highest = lax.Precision.HIGHEST
epsilon = 1e-06

def matmul(left_side, right_side):
    return jnp.dot(left_side, right_side, precision=highest)

def normalize(values, gain_row, shift_row):
    average = lax.optimization_barrier(jnp.mean(values, axis=-1, keepdims=True))
    centered = values - average
    spread = lax.optimization_barrier(jnp.mean(centered * centered, axis=-1, keepdims=True))
    return centered * lax.rsqrt(spread + epsilon) * gain_row + shift_row

def attend_rows(item, key_heads, value_heads, key_segments):
    query_heads, query_segments = item
    scores = jnp.einsum('qhd,khd->hqk', query_heads, key_heads, precision=highest) * 0.125
    visible = query_segments[:, None] == key_segments[None, :]
    scores = low_back(jnp.where(visible[None], scores, -1e+30))
    row_max = lax.optimization_barrier(jnp.max(scores, axis=-1, keepdims=True))
    weights = jnp.exp(scores - row_max)
    probs = weights / lax.optimization_barrier(jnp.sum(weights, axis=-1, keepdims=True))
    return jnp.einsum('hqk,khd->qhd', low(probs), value_heads, precision=highest)

def layer(token_rows, params, segments):
    w_query, b_query, w_key, w_value, b_value, w_output, b_output, attn_gain, attn_shift, w_inner, b_inner, w_outer, b_outer, ffn_gain, ffn_shift = params
    length = token_rows.shape[0]
    low_rows = low(token_rows)
    queries = low_back(low(matmul(low_rows, w_query) + b_query))
    key_rows = low_back(low(matmul(low_rows, w_key)))
    value_rows = low_back(low(matmul(low_rows, w_value) + b_value))
    block_rows = min(512, length)
    block_count = length // block_rows
    key_heads = key_rows.reshape(length, H, DH)
    value_heads = value_rows.reshape(length, H, DH)
    query_blocks = queries.reshape(block_count, block_rows, H, DH)
    segment_blocks = segments.reshape(block_count, block_rows)
    attend = jax.checkpoint(attend_rows)
    mixed = lax.map(lambda item: attend(item, key_heads, value_heads, segments), (query_blocks, segment_blocks))
    mixed = low_back(low(mixed.reshape(length, H * DH)))
    branch = low_back(matmul(mixed, w_output) + b_output)
    normed = normalize(token_rows + branch, attn_gain, attn_shift)
    pre_act = low_back(matmul(low(normed), w_inner) + b_inner)
    activated = low(jax.nn.gelu(pre_act, approximate=False))
    outer_sum = low_back(matmul(activated, w_outer) + b_outer)
    return normalize(normed + outer_sum, ffn_gain, ffn_shift)

def reference(hidden, segment, cotangent, w_query, b_query, w_key, w_value, b_value, w_output, b_output, attn_gain, attn_shift, w_inner, b_inner, w_outer, b_outer, ffn_gain, ffn_shift):
    params = tuple((item.astype(jnp.float32) for item in (w_query, b_query, w_key, w_value, b_value, w_output, b_output, attn_gain, attn_shift, w_inner, b_inner, w_outer, b_outer, ffn_gain, ffn_shift)))

    def one_sequence(totals, item):
        token_rows, seg_ids, tangent = item

        def forward(inputs, weights):
            return layer(inputs, weights, seg_ids)
        result, pull = jax.vjp(forward, token_rows.astype(jnp.float32), params)
        grad_rows, grad_params = pull(tangent.astype(jnp.float32))
        totals = jax.tree.map(jnp.add, totals, grad_params)
        return (totals, (result.astype(jnp.bfloat16), grad_rows))
    zeros = jax.tree.map(jnp.zeros_like, params)
    totals, (output, grad_input) = lax.scan(one_sequence, zeros, (hidden, segment, cotangent))
    return (output, grad_input, totals[0], totals[1], totals[2], totals[3], totals[4], totals[5], totals[6], totals[7], totals[8], totals[9], totals[10], totals[11], totals[12], totals[13], totals[14])
```

```python
import functools

import jax
import jax.numpy as jnp
from jax import lax
from jax.experimental import pallas as pl
from jax.experimental.pallas import tpu as pltpu
from jax.sharding import PartitionSpec as P

H = 12
DH = 64


epsilon = 1e-06
root_half = 0.7071067811865476
inv_root_tau = 0.3989422804014327


def matmul(left_side, right_side):
    return jnp.dot(left_side, right_side, preferred_element_type=jnp.float32)


def outer_dot(left_side, right_side):
    return lax.dot_general(
        left_side, right_side, (((0,), (0,)), ((), ())), preferred_element_type=jnp.float32
    )


def back_dot(left_side, right_side):
    return lax.dot_general(
        left_side, right_side, (((1,), (1,)), ((), ())), preferred_element_type=jnp.float32
    )


def forward_norm(values, gain_row, shift_row):
    average = jnp.mean(values, axis=-1, keepdims=True)
    centered = values - average
    spread = jnp.mean(centered * centered, axis=-1, keepdims=True)
    inv_scale = lax.rsqrt(spread + epsilon)
    unit_rows = centered * inv_scale
    return (unit_rows * gain_row + shift_row, unit_rows, inv_scale)


def backward_norm(grad_rows, unit_rows, inv_scale, gain_row):
    scaled = grad_rows * gain_row
    plain_mean = jnp.mean(scaled, axis=-1, keepdims=True)
    cross_mean = jnp.mean(scaled * unit_rows, axis=-1, keepdims=True)
    grad_values = inv_scale * (scaled - plain_mean - unit_rows * cross_mean)
    return (grad_values, jnp.sum(grad_rows * unit_rows, axis=0), jnp.sum(grad_rows, axis=0))


def as_float(weights):
    return tuple((item.astype(jnp.float32) if item.ndim == 1 else item for item in weights))


def forward_pass(token_rows, seg_ids, weights):
    (
        w_query,
        b_query,
        w_key,
        w_value,
        b_value,
        w_output,
        b_output,
        attn_gain,
        attn_shift,
        w_inner,
        b_inner,
        w_outer,
        b_outer,
        ffn_gain,
        ffn_shift,
    ) = as_float(weights)
    tokens = token_rows.shape[0]
    model_width = token_rows.shape[1]
    queries = (matmul(token_rows, w_query) + b_query).astype(jnp.bfloat16)
    key_rows = matmul(token_rows, w_key).astype(jnp.bfloat16)
    value_rows = (matmul(token_rows, w_value) + b_value).astype(jnp.bfloat16)
    seg_low = seg_ids.astype(jnp.bfloat16)
    query_heads = queries.reshape(tokens, H, DH)
    piece_keys = lax.all_gather(key_rows, "ctx", axis=0, tiled=True)
    piece_values = lax.all_gather(value_rows, "ctx", axis=0, tiled=True)
    piece_seg = lax.all_gather(seg_low, "ctx", axis=0, tiled=True)
    piece_len = piece_keys.shape[0]
    row_max = jnp.full((H, tokens), -1e30, jnp.float32)
    weighted = jnp.zeros((tokens, H, DH), jnp.float32)
    scores = (
        jnp.einsum(
            "qhd,khd->hqk",
            query_heads,
            piece_keys.reshape(piece_len, H, DH),
            preferred_element_type=jnp.float32,
        )
        * 0.125
    )
    visible = (seg_low[:, None] == piece_seg[None, :])[None]
    masked = jnp.where(visible, scores, -1e30)
    new_max = jnp.maximum(row_max, jnp.max(masked, axis=-1))
    weights_now = jnp.where(visible, jnp.exp(masked - new_max[:, :, None]), 0.0)
    rescale = jnp.exp(row_max - new_max)
    row_sum = jnp.sum(weights_now, axis=-1)
    added = jnp.einsum(
        "hqk,khd->qhd",
        weights_now.astype(jnp.bfloat16),
        piece_values.reshape(piece_len, H, DH),
        preferred_element_type=jnp.float32,
    )
    weighted = rescale.T[:, :, None] * weighted + added
    row_max, row_sum, weighted = (new_max, row_sum, weighted)
    mixed_full = (weighted / row_sum.T[:, :, None]).reshape(tokens, model_width)
    log_sum = row_max + jnp.log(row_sum)
    mixed = mixed_full.astype(jnp.bfloat16)
    branch = matmul(mixed, w_output) + b_output
    normed, unit_one, inv_one = forward_norm(
        token_rows.astype(jnp.float32) + branch, attn_gain, attn_shift
    )
    normed_low = normed.astype(jnp.bfloat16)
    pre_act = matmul(normed_low, w_inner) + b_inner
    activated = jax.nn.gelu(pre_act, approximate=False).astype(jnp.bfloat16)
    outer_sum = matmul(activated, w_outer) + b_outer
    result, unit_two, inv_two = forward_norm(normed + outer_sum, ffn_gain, ffn_shift)
    kept = (
        token_rows,
        seg_low,
        queries,
        key_rows,
        value_rows,
        mixed_full,
        mixed,
        log_sum,
        unit_one,
        inv_one,
        normed_low,
        pre_act,
        activated,
        unit_two,
        inv_two,
    )
    return (kept, result.astype(jnp.bfloat16))


def backward_pass(tangent, kept, weights):
    (
        w_query,
        b_query,
        w_key,
        w_value,
        b_value,
        w_output,
        b_output,
        attn_gain,
        attn_shift,
        w_inner,
        b_inner,
        w_outer,
        b_outer,
        ffn_gain,
        ffn_shift,
    ) = as_float(weights)
    (
        token_rows,
        seg_low,
        queries,
        key_rows,
        value_rows,
        mixed_full,
        mixed,
        log_sum,
        unit_one,
        inv_one,
        normed_low,
        pre_act,
        activated,
        unit_two,
        inv_two,
    ) = kept
    tokens = token_rows.shape[0]
    model_width = token_rows.shape[1]
    grad_second, grad_ffn_gain, grad_ffn_shift = backward_norm(
        tangent.astype(jnp.float32), unit_two, inv_two, ffn_gain
    )
    grad_outer = grad_second.astype(jnp.bfloat16)
    grad_b_outer = jnp.sum(grad_outer.astype(jnp.float32), axis=0)
    grad_w_outer = outer_dot(activated, grad_outer)
    grad_act = back_dot(grad_outer, w_outer)
    normal_cdf = 0.5 * (1.0 + lax.erf(pre_act * root_half))
    density = jnp.exp(-0.5 * pre_act * pre_act) * inv_root_tau
    grad_pre = (grad_act * (normal_cdf + pre_act * density)).astype(jnp.bfloat16)
    grad_b_inner = jnp.sum(grad_pre.astype(jnp.float32), axis=0)
    grad_w_inner = outer_dot(normed_low, grad_pre)
    grad_normed = grad_second + back_dot(grad_pre, w_inner)
    grad_mid, grad_attn_gain, grad_attn_shift = backward_norm(
        grad_normed, unit_one, inv_one, attn_gain
    )
    grad_branch = grad_mid.astype(jnp.bfloat16)
    grad_b_output = jnp.sum(grad_branch.astype(jnp.float32), axis=0)
    grad_w_output = outer_dot(mixed, grad_branch)
    grad_mixed = back_dot(grad_branch, w_output).astype(jnp.bfloat16)
    mixed_heads = grad_mixed.reshape(tokens, H, DH)
    query_heads = queries.reshape(tokens, H, DH)
    row_dot = jnp.sum(
        grad_mixed.astype(jnp.float32).reshape(tokens, H, DH) * mixed_full.reshape(tokens, H, DH),
        axis=-1,
    ).T
    whole_keys, whole_values, whole_seg = (
        lax.all_gather(key_rows, "ctx", axis=0, tiled=True),
        lax.all_gather(value_rows, "ctx", axis=0, tiled=True),
        lax.all_gather(seg_low, "ctx", axis=0, tiled=True),
    )
    length = whole_keys.shape[0]
    key_block = min(512, length)
    block_count = length // key_block

    def visit(block_index, carry_now):
        offset = block_index * key_block
        block_keys = lax.dynamic_slice_in_dim(whole_keys, offset, key_block, 0).reshape(
            key_block, H, DH
        )
        block_values = lax.dynamic_slice_in_dim(whole_values, offset, key_block, 0).reshape(
            key_block, H, DH
        )
        block_seg = lax.dynamic_slice_in_dim(whole_seg, offset, key_block, 0)
        grad_query_sum, key_terms, value_terms = carry_now
        scores = (
            jnp.einsum("qhd,khd->hqk", query_heads, block_keys, preferred_element_type=jnp.float32)
            * 0.125
        )
        visible = (seg_low[:, None] == block_seg[None, :])[None]
        probs = jnp.where(visible, jnp.exp(scores - log_sum[:, :, None]), 0.0)
        grad_probs = jnp.einsum(
            "qhd,khd->hqk", mixed_heads, block_values, preferred_element_type=jnp.float32
        )
        grad_scores = (probs * (grad_probs - row_dot[:, :, None])).astype(jnp.bfloat16)
        grad_query_sum = grad_query_sum + jnp.einsum(
            "hqk,khd->qhd", grad_scores, block_keys, preferred_element_type=jnp.float32
        )
        key_part = (
            jnp.einsum(
                "hqk,qhd->khd", grad_scores, query_heads, preferred_element_type=jnp.float32
            ).reshape(key_block, model_width)
            * 0.125
        )
        value_part = jnp.einsum(
            "hqk,qhd->khd",
            probs.astype(jnp.bfloat16),
            mixed_heads,
            preferred_element_type=jnp.float32,
        ).reshape(key_block, model_width)
        key_terms = lax.dynamic_update_slice_in_dim(key_terms, key_part, offset, 0)
        value_terms = lax.dynamic_update_slice_in_dim(value_terms, value_part, offset, 0)
        return (grad_query_sum, key_terms, value_terms)

    initial = (
        jnp.zeros((tokens, H, DH), jnp.float32),
        jnp.zeros((length, model_width), jnp.float32),
        jnp.zeros((length, model_width), jnp.float32),
    )
    grad_query_sum, key_terms, value_terms = lax.fori_loop(0, block_count, visit, initial)
    grad_key_sum, grad_value_sum = (
        lax.psum_scatter(
            key_terms.astype(jnp.bfloat16), "ctx", scatter_dimension=0, tiled=True
        ).astype(jnp.float32),
        lax.psum_scatter(
            value_terms.astype(jnp.bfloat16), "ctx", scatter_dimension=0, tiled=True
        ).astype(jnp.float32),
    )
    grad_queries = (grad_query_sum.reshape(tokens, model_width) * 0.125).astype(jnp.bfloat16)
    grad_keys = grad_key_sum.astype(jnp.bfloat16)
    grad_values = grad_value_sum.astype(jnp.bfloat16)
    grad_w_query = outer_dot(token_rows, grad_queries)
    grad_b_query = jnp.sum(grad_queries.astype(jnp.float32), axis=0)
    grad_w_key = outer_dot(token_rows, grad_keys)
    grad_w_value = outer_dot(token_rows, grad_values)
    grad_b_value = jnp.sum(grad_values.astype(jnp.float32), axis=0)
    grad_rows = (
        grad_mid
        + back_dot(grad_queries, w_query)
        + back_dot(grad_keys, w_key)
        + back_dot(grad_values, w_value)
    )
    grads = (
        grad_w_query,
        grad_b_query,
        grad_w_key,
        grad_w_value,
        grad_b_value,
        grad_w_output,
        grad_b_output,
        grad_attn_gain,
        grad_attn_shift,
        grad_w_inner,
        grad_b_inner,
        grad_w_outer,
        grad_b_outer,
        grad_ffn_gain,
        grad_ffn_shift,
    )
    return (grad_rows, grads)


def on_device(
    hidden,
    segment,
    cotangent,
    w_query,
    b_query,
    w_key,
    w_value,
    b_value,
    w_output,
    b_output,
    attn_gain,
    attn_shift,
    w_inner,
    b_inner,
    w_outer,
    b_outer,
    ffn_gain,
    ffn_shift,
):
    micro_count = hidden.shape[0]
    totals = None
    results = []
    input_grads = []
    for micro_index in range(micro_count):
        forward_weights = (
            lax.all_gather(w_query, ("seq", "ctx"), axis=0, tiled=True),
            lax.all_gather(b_query, ("seq", "ctx"), axis=0, tiled=True),
            lax.all_gather(w_key, ("seq", "ctx"), axis=0, tiled=True),
            lax.all_gather(w_value, ("seq", "ctx"), axis=0, tiled=True),
            lax.all_gather(b_value, ("seq", "ctx"), axis=0, tiled=True),
            lax.all_gather(w_output, ("seq", "ctx"), axis=0, tiled=True),
            lax.all_gather(b_output, ("seq", "ctx"), axis=0, tiled=True),
            lax.all_gather(attn_gain, ("seq", "ctx"), axis=0, tiled=True),
            lax.all_gather(attn_shift, ("seq", "ctx"), axis=0, tiled=True),
            lax.all_gather(w_inner, ("seq", "ctx"), axis=0, tiled=True),
            lax.all_gather(b_inner, ("seq", "ctx"), axis=0, tiled=True),
            lax.all_gather(w_outer, ("seq", "ctx"), axis=0, tiled=True),
            lax.all_gather(b_outer, ("seq", "ctx"), axis=0, tiled=True),
            lax.all_gather(ffn_gain, ("seq", "ctx"), axis=0, tiled=True),
            lax.all_gather(ffn_shift, ("seq", "ctx"), axis=0, tiled=True),
        )
        kept, result = forward_pass(hidden[micro_index], segment[micro_index], forward_weights)
        results.append(result)
        backward_weights = (
            lax.all_gather(w_query, ("seq", "ctx"), axis=0, tiled=True),
            lax.all_gather(b_query, ("seq", "ctx"), axis=0, tiled=True),
            lax.all_gather(w_key, ("seq", "ctx"), axis=0, tiled=True),
            lax.all_gather(w_value, ("seq", "ctx"), axis=0, tiled=True),
            lax.all_gather(b_value, ("seq", "ctx"), axis=0, tiled=True),
            lax.all_gather(w_output, ("seq", "ctx"), axis=0, tiled=True),
            lax.all_gather(b_output, ("seq", "ctx"), axis=0, tiled=True),
            lax.all_gather(attn_gain, ("seq", "ctx"), axis=0, tiled=True),
            lax.all_gather(attn_shift, ("seq", "ctx"), axis=0, tiled=True),
            lax.all_gather(w_inner, ("seq", "ctx"), axis=0, tiled=True),
            lax.all_gather(b_inner, ("seq", "ctx"), axis=0, tiled=True),
            lax.all_gather(w_outer, ("seq", "ctx"), axis=0, tiled=True),
            lax.all_gather(b_outer, ("seq", "ctx"), axis=0, tiled=True),
            lax.all_gather(ffn_gain, ("seq", "ctx"), axis=0, tiled=True),
            lax.all_gather(ffn_shift, ("seq", "ctx"), axis=0, tiled=True),
        )
        grad_rows, grads = backward_pass(cotangent[micro_index], kept, backward_weights)
        input_grads.append(grad_rows)
        if totals is None:
            totals = grads
        else:
            totals = jax.tree.map(jnp.add, totals, grads)
    owned = (
        lax.psum_scatter(totals[0], ("seq", "ctx"), scatter_dimension=0, tiled=True),
        lax.psum_scatter(totals[1], ("seq", "ctx"), scatter_dimension=0, tiled=True),
        lax.psum_scatter(totals[2], ("seq", "ctx"), scatter_dimension=0, tiled=True),
        lax.psum_scatter(totals[3], ("seq", "ctx"), scatter_dimension=0, tiled=True),
        lax.psum_scatter(totals[4], ("seq", "ctx"), scatter_dimension=0, tiled=True),
        lax.psum_scatter(totals[5], ("seq", "ctx"), scatter_dimension=0, tiled=True),
        lax.psum_scatter(totals[6], ("seq", "ctx"), scatter_dimension=0, tiled=True),
        lax.psum_scatter(totals[7], ("seq", "ctx"), scatter_dimension=0, tiled=True),
        lax.psum_scatter(totals[8], ("seq", "ctx"), scatter_dimension=0, tiled=True),
        lax.psum_scatter(totals[9], ("seq", "ctx"), scatter_dimension=0, tiled=True),
        lax.psum_scatter(totals[10], ("seq", "ctx"), scatter_dimension=0, tiled=True),
        lax.psum_scatter(totals[11], ("seq", "ctx"), scatter_dimension=0, tiled=True),
        lax.psum_scatter(totals[12], ("seq", "ctx"), scatter_dimension=0, tiled=True),
        lax.psum_scatter(totals[13], ("seq", "ctx"), scatter_dimension=0, tiled=True),
        lax.psum_scatter(totals[14], ("seq", "ctx"), scatter_dimension=0, tiled=True),
    )
    return (jnp.stack(results), jnp.stack(input_grads)) + tuple(owned)


AXES = ("seq", "ctx")
LOG2E = 1.4426950408889634
SCORE_UNIT = 0.125 * LOG2E
HIDDEN_SCORE = -1e30
VMEM_BYTES = 62 << 20
SLAB = 128


def place_of(index, me):
    mz, mc, my, mx = me
    bx, by, bc, bz = index & 1, (index >> 1) & 1, (index >> 2) & 1, index >> 3
    kx, ky, kz = bx ^ mx, by ^ my, bz ^ mz
    even = bc == 0
    first = jnp.where(even, kx, ky)
    second = jnp.where(even, ky, kx)
    return bc == mc, first, second, kz


def read_me(me_ref):
    return me_ref[0], me_ref[1], me_ref[2], me_ref[3]


def start_load(me, pieces, columns, target, rows, count, sem):
    def body(index, carry):
        own, first, second, kz = place_of(index, me)
        spot = target.at[pl.ds(pl.multiple_of(index * rows, 8), rows), :]
        for number, piece in enumerate(pieces):
            mine = own if number < 2 else jnp.logical_not(own)

            @pl.when(jnp.logical_and(mine, second == number % 2))
            def _(piece=piece):
                source = piece.at[first, kz]
                if columns is not None:
                    source = source.at[:, pl.ds(columns[0], columns[1])]
                pltpu.make_async_copy(source, spot, sem).start()

        return carry

    lax.fori_loop(0, count, body, 0)


def end_load(target, sem):
    pltpu.make_async_copy(target, target, sem).wait()


def store_blocks(me, value_ref, keep_ref, send_ref, first_block, count, rows, column, width):
    def body(step, carry):
        own, first, second, kz = place_of(first_block + step, me)
        value = value_ref[pl.ds(pl.multiple_of(step * rows, 8), rows), :].astype(jnp.bfloat16)

        @pl.when(own)
        def _():
            keep_ref[first, second, kz, :, pl.ds(column, width)] = value

        @pl.when(jnp.logical_not(own))
        def _():
            send_ref[first, second, kz, :, pl.ds(column, width)] = value

        return carry

    lax.fori_loop(0, count, body, 0)


def lanes_of(shape):
    return lax.broadcasted_iota(jnp.int32, shape, len(shape) - 1)


def nn(a, b):
    return jnp.dot(a, b, preferred_element_type=jnp.float32)


def nt(a, b):
    return lax.dot_general(a, b, (((1,), (1,)), ((), ())), preferred_element_type=jnp.float32)


def tn(a, b):
    return lax.dot_general(a, b, (((0,), (0,)), ((), ())), preferred_element_type=jnp.float32)


def row_sum(values):
    return jnp.sum(values, axis=0, keepdims=True)


def pack_weights_kernel(wq_ref, wk_ref, wv_ref, *rest):
    vectors, inner_ref, out_ref = rest[:8], rest[8], rest[9]
    rows, width = wq_ref.shape
    out_ref[:, 0:width] = wq_ref[...]
    out_ref[:, width : 2 * width] = wk_ref[...]
    out_ref[:, 2 * width : 3 * width] = wv_ref[...]
    share = inner_ref.shape[1]
    lines = [ref[...].astype(jnp.float32) for ref in vectors]
    lines = [jnp.concatenate([line, jnp.zeros((1, SLAB - rows), jnp.float32)], axis=1) for line in lines]
    last = jnp.concatenate(
        [inner_ref[...].astype(jnp.float32), jnp.zeros((1, SLAB - share), jnp.float32)], axis=1
    )
    slab = jnp.concatenate(lines + [last, jnp.zeros((rows - 9, SLAB), jnp.float32)], axis=0)
    out_ref[:, 3 * width : 3 * width + SLAB] = slab.astype(jnp.bfloat16)


def pack_rows_kernel(me_ref, hidden_ref, segment_ref, near_ref, far_ref):
    x = me_ref[3]
    quarter, width = hidden_ref.shape[1], hidden_ref.shape[2]
    for ref, pick in ((near_ref, x), (far_ref, 1 - x)):
        ref[0:quarter, :] = hidden_ref[pick]
        both = segment_ref[...].astype(jnp.float32)
        line = jnp.where(pick == 0, both[0:1, :], both[1:2, :]).astype(jnp.bfloat16)
        ref[quarter : quarter + 8, 0:quarter] = jnp.broadcast_to(line, (8, quarter))
        ref[quarter : quarter + 8, quarter:width] = jnp.zeros((8, width - quarter), jnp.bfloat16)


def pick_rows_kernel(me_ref, rows_ref, near_ref, far_ref):
    x = me_ref[3]
    near_ref[...] = rows_ref[x]
    far_ref[...] = rows_ref[1 - x]


def settle_kernel(me_ref, near_ref, far_ref, out_ref):
    x = me_ref[3]
    out_ref[x] = near_ref[...].astype(out_ref.dtype)
    out_ref[1 - x] = far_ref[...].astype(out_ref.dtype)


def spread_lanes(block, share, offset, tiles, tile):
    lane = lanes_of(block.shape)
    moved = pltpu.roll(block, offset, axis=1) if offset else block
    tiles[tile] = jnp.where(
        jnp.logical_and(lane >= offset, lane < offset + share), moved, tiles[tile]
    )
    if offset + share > 128:
        tiles[tile + 1] = jnp.where(lane < offset + share - 128, moved, tiles[tile + 1])


def project_kernel(
    me_ref, r0, r1, r2, r3, p0, p1, p2, p3,
    q_ref, k_ref, v_ref, vec_ref, bias_ref, x_ref, segrow_ref, segcol_ref, w_ref, slab_ref, sem,
):
    me = read_me(me_ref)
    tokens, width = q_ref.shape
    blocks = 32
    rows = width // blocks
    start_load(me, (p0, p1, p2, p3), None, w_ref, rows, blocks, sem)
    quarter = tokens // 2
    for number, ref in enumerate((r0, r1, r2, r3)):
        span = pl.ds(number * quarter, quarter)
        x_ref[span, :] = ref[0:quarter, :]
        line = ref[quarter : quarter + 8, 0:quarter].astype(jnp.float32)
        segrow_ref[:, span] = line
        segcol_ref[span, :] = jnp.broadcast_to(line[0:1, :], (128, quarter)).T
    end_load(w_ref, sem)
    slab_ref[...] = w_ref[:, 3 * width : 3 * width + SLAB].astype(jnp.float32)
    tiles = [jnp.zeros((8, 128), jnp.float32) for _ in range(width // 128 + 1)]
    for index in range(blocks):
        start = rows * index
        spread_lanes(slab_ref[start : start + 8, :], rows, start % 128, tiles, start // 128)
    vectors = jnp.concatenate(tiles[: width // 128], axis=1)
    vec_ref[...] = vectors
    share = bias_ref.shape[1] // blocks
    tiles = [jnp.zeros((8, 128), jnp.float32) for _ in range(4)]
    for turn in range(4):
        lines = slab_ref[pl.ds(rows * turn + 8, 8, stride=4 * rows), :]
        spread_lanes(lines, share, share * turn % 128, tiles, share * turn // 128)
    for group in range(8):
        for tile in range(3):
            bias_ref[0:1, pl.ds(group * 384 + tile * 128, 128)] = tiles[tile][group : group + 1, :]
    b_query, b_value = vectors[0:1, :], vectors[1:2, :]
    q_ref[...] = (nn(x_ref[0:tokens, :], w_ref[:, 0:width]) + b_query).astype(jnp.bfloat16)
    for part in range(2):
        span = pl.ds(part * tokens, tokens)
        k_ref[span, :] = nn(x_ref[span, :], w_ref[:, width : 2 * width]).astype(jnp.bfloat16)
        v_ref[span, :] = (nn(x_ref[span, :], w_ref[:, 2 * width : 3 * width]) + b_value).astype(
            jnp.bfloat16
        )


def attend_kernel(q_ref, k_ref, v_ref, segcol_ref, segrow_ref, mixed_ref, lse_ref, bias_ref):
    tokens = q_ref.shape[0]
    keys = k_ref.shape[0]
    tile = 256

    @pl.when(pl.program_id(0) == 0)
    def _():
        visible = segcol_ref[0:tokens, 0:1] == segrow_ref[0:1, :]
        bias_ref[...] = jnp.where(visible, 0.0, HIDDEN_SCORE)

    low_half = lanes_of((1, 128)) < 64
    key_rows = k_ref[...]
    value_rows = v_ref[...]
    one = jnp.ones((), jnp.bfloat16)
    zero = jnp.zeros((), jnp.bfloat16)
    for part in range(tokens // tile):
        span = pl.ds(part * tile, tile)
        query = q_ref[span, :]
        bias = bias_ref[span, :]
        outs, sums = [], []
        for head in range(2):
            mine = low_half if head == 0 else jnp.logical_not(low_half)
            scores = nt(jnp.where(mine, query, zero), key_rows) + bias
            top = jnp.max(scores, axis=-1, keepdims=True)
            weights = jnp.exp2((scores - top) * SCORE_UNIT).astype(jnp.bfloat16)
            product = nn(weights, jnp.where(mine, value_rows, one))
            total = product[:, 64:65] if head == 0 else product[:, 0:1]
            outs.append(product / total)
            sums.append(top * SCORE_UNIT + jnp.log2(total))
        mixed_ref[span, :] = jnp.where(low_half, outs[0], outs[1])
        lane = lanes_of((tile, 128))
        both = jnp.where(lane == 0, sums[0], jnp.where(lane == 1, sums[1], 0.0))
        lse_ref[0, :, span] = both.T[0:8, :]


def attend_back_kernel(
    q_ref, k_ref, v_ref, gm_ref, mixed_ref, lse_ref, segcol_ref, segrow_ref,
    dq_ref, dk_ref, dv_ref, bias_ref,
):
    tokens = q_ref.shape[0]
    keys = k_ref.shape[0]
    tile = 256

    @pl.when(pl.program_id(0) == 0)
    def _():
        visible = segcol_ref[:, 0:1] == segrow_ref[0:1, 0:tokens]
        bias_ref[...] = jnp.where(visible, 0.0, HIDDEN_SCORE)

    low_half = lanes_of((1, 128)) < 64
    zero = jnp.zeros((), jnp.bfloat16)
    query = q_ref[...]
    grad = gm_ref[...]
    product = (grad.astype(jnp.float32) * mixed_ref[...]).T
    row_dots = [row_sum(product[0:64, :]), row_sum(product[64:128, :])]
    masks = (low_half, jnp.logical_not(low_half))
    queries = [jnp.where(mine, query, zero) for mine in masks]
    grads = [jnp.where(mine, grad, zero) for mine in masks]
    grad_query = jnp.zeros((tokens, 128), jnp.float32)
    for part in range(keys // tile):
        span = pl.ds(part * tile, tile)
        key_rows = k_ref[span, :]
        value_rows = v_ref[span, :]
        bias = bias_ref[span, :]
        grad_key = jnp.zeros((tile, 128), jnp.float32)
        grad_value = jnp.zeros((tile, 128), jnp.float32)
        for head in range(2):
            scores = nt(key_rows, queries[head])
            probs = jnp.exp2(scores * SCORE_UNIT + (bias - lse_ref[0, head : head + 1, :]))
            grad_probs = nt(value_rows, grads[head])
            grad_scores = (probs * (grad_probs - row_dots[head])).astype(jnp.bfloat16)
            grad_key = grad_key + nn(grad_scores, queries[head])
            grad_value = grad_value + nn(probs.astype(jnp.bfloat16), grads[head])
            grad_query = grad_query + tn(grad_scores, jnp.where(masks[head], key_rows, zero))
        dk_ref[span, :] = (grad_key * 0.125).astype(jnp.bfloat16)
        dv_ref[span, :] = grad_value.astype(jnp.bfloat16)
    dq_ref[...] = (grad_query * 0.125).astype(jnp.bfloat16)


def normalize(values):
    average = jnp.mean(values, axis=-1, keepdims=True)
    centered = values - average
    spread = jnp.mean(centered * centered, axis=-1, keepdims=True)
    inverse = lax.rsqrt(spread + epsilon)
    return centered * inverse, inverse


def normalize_back(grad, unit, inverse, gain):
    scaled = grad * gain
    plain = jnp.mean(scaled, axis=-1, keepdims=True)
    cross = jnp.mean(scaled * unit, axis=-1, keepdims=True)
    return inverse * (scaled - plain - unit * cross)


def feed_in_kernel(
    me_ref, mixed_a_ref, mixed_b_ref, x_ref, vec_ref, bias_ref, a0, a1, a2, a3,
    low_ref, act_ref, slope_ref, unit_ref, inverse_ref, rest_ref, wo_ref, wi_ref, sem_o, sem_i,
):
    me = read_me(me_ref)
    tokens, width = low_ref.shape
    inner = wi_ref.shape[1]
    blocks = 32
    start_load(me, (a0, a1, a2, a3), (0, width), wo_ref, width // blocks, blocks, sem_o)
    start_load(me, (a0, a1, a2, a3), (width, inner), wi_ref, width // blocks, blocks, sem_i)
    b_output, attn_gain, attn_shift = vec_ref[2:3, :], vec_ref[3:4, :], vec_ref[4:5, :]
    b_outer = vec_ref[5:6, :]
    end_load(wo_ref, sem_o)
    part = mixed_a_ref.shape[1]
    branch = b_output + nn(mixed_a_ref[...].astype(jnp.bfloat16), wo_ref[0:part, :])
    branch = branch + nn(mixed_b_ref[...].astype(jnp.bfloat16), wo_ref[part:width, :])
    unit_one, inverse_one = normalize(x_ref[0:tokens, :].astype(jnp.float32) + branch)
    normed = unit_one * attn_gain + attn_shift
    unit_ref[...] = unit_one
    inverse_ref[...] = jnp.broadcast_to(inverse_one, inverse_ref.shape)
    low_ref[...] = normed.astype(jnp.bfloat16)
    rest_ref[...] = normed + b_outer
    end_load(wi_ref, sem_i)
    step = 512

    @pl.loop(0, inner // step)
    def _(turn):
        span = pl.ds(pl.multiple_of(turn * step, step), step)
        pre_act = nn(low_ref[...], wi_ref[:, span]) + bias_ref[0:1, span]
        normal_cdf = 0.5 * (1.0 + lax.erf(pre_act * root_half))
        density = jnp.exp(-0.5 * pre_act * pre_act) * inv_root_tau
        act_ref[:, span] = (pre_act * normal_cdf).astype(jnp.bfloat16)
        slope_ref[:, span] = (normal_cdf + pre_act * density).astype(jnp.bfloat16)


def feed_out_kernel(
    me_ref, act_ref, rest_ref, cot_near_ref, cot_far_ref, vec_ref, b0, b1, b2, b3,
    near_ref, far_ref, second_ref, outer_ref, sums_ref, keep_ref, send_ref,
    wu_ref, grad_ref, sem_u,
):
    me = read_me(me_ref)
    tokens, width = rest_ref.shape
    inner = act_ref.shape[1]
    blocks = 32
    rows = inner // blocks
    quarter = tokens // 2
    start_load(me, (b0, b1, b2, b3), None, wu_ref, rows, blocks, sem_u)
    ffn_gain, ffn_shift = vec_ref[6:7, :], vec_ref[7:8, :]
    end_load(wu_ref, sem_u)
    sums = [jnp.zeros((1, width), jnp.float32) for _ in range(3)]
    for part in range(2):
        span = pl.ds(part * quarter, quarter)
        unit_two, inverse_two = normalize(rest_ref[span, :] + nn(act_ref[span, :], wu_ref[...]))
        out_ref, cot_ref = ((near_ref, cot_near_ref), (far_ref, cot_far_ref))[part]
        out_ref[...] = (unit_two * ffn_gain + ffn_shift).astype(jnp.bfloat16)
        tangent = cot_ref[...].astype(jnp.float32)
        second = normalize_back(tangent, unit_two, inverse_two, ffn_gain)
        second_ref[span, :] = second
        outer = second.astype(jnp.bfloat16)
        outer_ref[span, :] = outer
        sums[0] = sums[0] + row_sum(outer.astype(jnp.float32))
        sums[1] = sums[1] + row_sum(tangent * unit_two)
        sums[2] = sums[2] + row_sum(tangent)
    sums_ref[...] = jnp.concatenate(sums + [jnp.zeros((5, width), jnp.float32)], axis=0)
    half = width // 2

    @pl.loop(0, inner // half)
    def _(turn):
        cols = pl.ds(pl.multiple_of(turn * half, half), half)
        grad_ref[...] = tn(act_ref[:, cols], outer_ref[...])
        store_blocks(
            me, grad_ref, keep_ref, send_ref, turn * (half // rows), half // rows, rows, 0, width
        )


def slope_kernel(
    me_ref, slope_ref, outer_ref, b0, b1, b2, b3, pre_ref, bsum_ref, wu_ref, sem_u
):
    me = read_me(me_ref)
    inner = slope_ref.shape[1]
    blocks = 32
    start_load(me, (b0, b1, b2, b3), None, wu_ref, inner // blocks, blocks, sem_u)
    end_load(wu_ref, sem_u)
    step = 512

    @pl.loop(0, inner // step)
    def _(turn):
        span = pl.ds(pl.multiple_of(turn * step, step), step)
        grad_act = nt(outer_ref[...], wu_ref[span, :])
        grad_pre = (grad_act * slope_ref[:, span].astype(jnp.float32)).astype(jnp.bfloat16)
        bsum_ref[0:1, span] = row_sum(grad_pre.astype(jnp.float32))
        pre_ref[:, span] = grad_pre


def feed_back_kernel(
    me_ref, pre_ref, second_ref, low_ref, unit_ref, inverse_ref, mixed_a_ref, mixed_b_ref, vec_ref,
    a0, a1, a2, a3,
    mid_ref, gm_ref, sums_ref, keep_ref, send_ref,
    wo_ref, wi_ref, grad_ref, sem_o, sem_i,
):
    me = read_me(me_ref)
    tokens, width = second_ref.shape
    inner = wi_ref.shape[1]
    blocks = 32
    rows = width // blocks
    start_load(me, (a0, a1, a2, a3), (width, inner), wi_ref, rows, blocks, sem_i)
    start_load(me, (a0, a1, a2, a3), (0, width), wo_ref, rows, blocks, sem_o)
    step = 512

    @pl.loop(0, inner // step)
    def _(turn):
        first = pl.multiple_of(turn * step, step)
        grad_ref[:, 0:step] = tn(low_ref[...], pre_ref[:, pl.ds(first, step)])
        store_blocks(
            me, grad_ref.at[:, 0:step], keep_ref, send_ref, 0, blocks, rows,
            pl.multiple_of(width + first, 128), step,
        )

    end_load(wi_ref, sem_i)
    grad_normed = second_ref[...] + nt(pre_ref[...], wi_ref[...])
    end_load(wo_ref, sem_o)
    attn_gain = vec_ref[3:4, :]
    unit = unit_ref[...]
    mid = normalize_back(grad_normed, unit, inverse_ref[:, 0:1], attn_gain)
    mid_ref[...] = mid
    branch = mid.astype(jnp.bfloat16)
    sums_ref[...] = jnp.zeros(sums_ref.shape, jnp.float32)
    sums_ref[0:1, :] = row_sum(branch.astype(jnp.float32))
    sums_ref[1:2, :] = row_sum(grad_normed * unit)
    sums_ref[2:3, :] = row_sum(grad_normed)
    gm_ref[...] = nt(branch, wo_ref[...]).astype(jnp.bfloat16)
    part = mixed_a_ref.shape[1]
    grad_ref[0:part, :] = tn(mixed_a_ref[...].astype(jnp.bfloat16), branch)
    grad_ref[part:width, :] = tn(mixed_b_ref[...].astype(jnp.bfloat16), branch)
    store_blocks(me, grad_ref, keep_ref, send_ref, 0, blocks, rows, 0, width)


def weight_kernel(
    me_ref, x_ref, dqa_ref, dka_ref, dva_ref, dqb_ref, dkb_ref, dvb_ref,
    sums_two_ref, sums_one_ref, bsum_ref, keep_ref, send_ref, grad_ref, slab_ref,
):
    me = read_me(me_ref)
    tokens, half = dqa_ref.shape
    width = 2 * half
    blocks = 32
    rows = width // blocks
    refs = (dqa_ref, dqb_ref, dka_ref, dkb_ref, dva_ref, dvb_ref)
    for number, ref in enumerate(refs):
        grad_ref[...] = tn(x_ref[0 : ref.shape[0], :], ref[...])
        store_blocks(me, grad_ref, keep_ref, send_ref, 0, blocks, rows, number * half, half)

    def sums(first, second):
        return jnp.concatenate(
            [row_sum(first[...].astype(jnp.float32)), row_sum(second[...].astype(jnp.float32))],
            axis=1,
        )

    vectors = jnp.concatenate(
        [
            sums(dqa_ref, dqb_ref),
            sums(dva_ref, dvb_ref),
            sums_one_ref[0:3, :],
            sums_two_ref[0:3, :],
        ],
        axis=0,
    )
    share = bsum_ref.shape[1] // blocks
    lane = lanes_of((8, 128))
    slab_ref[...] = jnp.zeros(slab_ref.shape, jnp.float32)
    for index in range(blocks):
        tile, offset = rows * index // 128, rows * index % 128
        piece = vectors[:, tile * 128 : tile * 128 + 128]
        if offset + rows > 128:
            piece = jnp.where(
                lane >= offset, piece, vectors[:, tile * 128 + 128 : tile * 128 + 256]
            )
        moved = pltpu.roll(piece, (128 - offset) % 128, axis=1) if offset else piece
        slab_ref[rows * index : rows * index + 8, :] = jnp.where(lane < rows, moved, 0.0)
    groups = jnp.concatenate([bsum_ref[0:1, pl.ds(384 * g, 384)] for g in range(8)], axis=0)
    for turn in range(4):
        tile, offset = share * turn // 128, share * turn % 128
        piece = groups[:, tile * 128 : tile * 128 + 128]
        if offset + share > 128:
            piece = jnp.where(lane >= offset, piece, groups[:, tile * 128 + 128 : tile * 128 + 256])
        moved = pltpu.roll(piece, (128 - offset) % 128, axis=1) if offset else piece
        slab_ref[pl.ds(rows * turn + 8, 8, stride=4 * rows), :] = jnp.where(lane < share, moved, 0.0)
    store_blocks(me, slab_ref, keep_ref, send_ref, 0, blocks, rows, 3 * width, SLAB)


def input_kernel(
    me_ref, mid_ref, dqa_ref, dka_ref, dva_ref, dqb_ref, dkb_ref, dvb_ref, other_ref,
    p0, p1, p2, p3, near_ref, far_ref, w_ref, sem,
):
    me = read_me(me_ref)
    tokens, width = mid_ref.shape
    half = width // 2
    blocks = 32
    start_load(me, (p0, p1, p2, p3), (0, 3 * width), w_ref, width // blocks, blocks, sem)
    own = []
    for number, ref in enumerate((dka_ref, dva_ref, dkb_ref, dvb_ref)):
        theirs = other_ref[:, number * half : (number + 1) * half].astype(jnp.float32)
        own.append((ref[0:tokens, :].astype(jnp.float32) + theirs).astype(jnp.bfloat16))
    end_load(w_ref, sem)
    total = mid_ref[...]
    for number, value in enumerate((dqa_ref[...], dqb_ref[...], own[0], own[2], own[1], own[3])):
        total = total + nt(value, w_ref[:, number * half : (number + 1) * half])
    low = total.astype(jnp.bfloat16)
    near_ref[...] = low[: tokens // 2]
    far_ref[...] = low[tokens // 2 :]


def shape_of(shape, dtype):
    return jax.ShapeDtypeStruct(shape, dtype)


def call(kernel, name, out_shape, kinds, scratch, flops, moved):
    spaces = {"s": pltpu.SMEM, "v": pltpu.VMEM, "a": pl.ANY}
    return pl.pallas_call(
        kernel,
        name=name,
        out_shape=out_shape,
        in_specs=[pl.BlockSpec(memory_space=spaces[kind]) for kind in kinds],
        scratch_shapes=scratch,
        compiler_params=pltpu.CompilerParams(vmem_limit_bytes=VMEM_BYTES),
        cost_estimate=pl.CostEstimate(flops=flops, bytes_accessed=moved, transcendentals=0),
    )


def tie(*values):
    return lax.optimization_barrier(values)


def fast_device(depth, hidden, segment, cotangent, *weights):
    (
        w_query, b_query, w_key, w_value, b_value, w_output, b_output, attn_gain, attn_shift,
        w_inner, b_inner, w_outer, b_outer, ffn_gain, ffn_shift,
    ) = weights
    bf16, f32 = jnp.bfloat16, jnp.float32
    quarter, width = hidden.shape[1], hidden.shape[2]
    tokens = 2 * quarter
    keys = 2 * tokens
    rows = w_query.shape[0]
    inner = w_inner.shape[1]
    inner_rows = w_outer.shape[0]
    seq_index, ctx_index = lax.axis_index("seq"), lax.axis_index("ctx")
    me = jnp.stack([seq_index >> 1, seq_index & 1, ctx_index >> 1, ctx_index & 1]).astype(jnp.int32)

    def table(move):
        pairs = []
        for bz in range(depth):
            for bc in range(2):
                for by in range(2):
                    for bx in range(2):
                        tz, tc, ty, tx = move(bz, bc, by, bx)
                        pairs.append(
                            (((bz * 2 + bc) * 2 + by) * 2 + bx, ((tz * 2 + tc) * 2 + ty) * 2 + tx)
                        )
        return pairs

    along_z = [table(lambda a, b, d, e, k=k: (a ^ k, b, d, e)) for k in range(1, depth)]
    plane_one = table(lambda a, b, d, e: (a, b, d, 1 - e) if b == 0 else (a, b, 1 - d, e))
    plane_two = table(lambda a, b, d, e: (a, b, 1 - d, e) if b == 0 else (a, b, d, 1 - e))
    partner = table(lambda a, b, d, e: (a, 1 - b, d, e))
    home_near = table(lambda a, b, d, e: (a, d, b, e))
    home_far = table(lambda a, b, d, e: (a, d, b, 1 - e))

    def hop(value, pairs):
        return lax.ppermute(value, AXES, pairs)

    def levels_of(value):
        return jnp.stack([value] + [hop(value, pairs) for pairs in along_z])

    sem = pltpu.SemaphoreType.DMA
    flat = 2 * tokens * width
    slabbed = 3 * width + SLAB

    vectors_in = (
        b_query, b_value, b_output, attn_gain, attn_shift, b_outer, ffn_gain, ffn_shift, b_inner,
    )
    packed = call(
        pack_weights_kernel, "pack_weights", shape_of((rows, slabbed), bf16), "v" * 12, [], 1, 1 << 20
    )(w_query, w_key, w_value, *[vector[None, :] for vector in vectors_in])
    levels_one = levels_of(packed)

    packed_row = shape_of((quarter + 8, width), bf16)
    near, far = call(
        pack_rows_kernel, "pack_rows", (packed_row, packed_row), "svv", [], 1, 1 << 20
    )(me, hidden, segment)
    near, far = hop(near, home_near), hop(far, home_far)
    plain_row = shape_of((quarter, width), bf16)
    cot_near, cot_far = call(
        pick_rows_kernel, "pick_rows", (plain_row, plain_row), "sv", [], 1, 1 << 20
    )(me, cotangent)
    cot_near, cot_far = hop(cot_near, home_near), hop(cot_far, home_far)

    near, far, levels_one = tie(near, far, levels_one)
    half_one = jnp.stack([levels_one, hop(levels_one, plane_one)])
    near_other, far_other = hop(near, partner), hop(far, partner)

    second_in = jnp.concatenate([w_output, w_inner], axis=1)
    half_one, second_in, cot_near, cot_far = tie(half_one, second_in, cot_near, cot_far)
    other_one = hop(half_one, plane_two)
    half_one_p = hop(half_one, partner)
    levels_two = levels_of(second_in)
    other_one, levels_two, third_in = tie(other_one, levels_two, w_outer)
    other_one_p = hop(other_one, partner)
    got_two = hop(levels_two, plane_one)
    levels_three = levels_of(third_in)
    group_one = (half_one, other_one, half_one_p, other_one_p)

    q, k, v, vectors, bias, x_all, segrow, segcol = call(
        project_kernel,
        "project",
        (
            shape_of((tokens, width), bf16),
            shape_of((keys, width), bf16),
            shape_of((keys, width), bf16),
            shape_of((8, width), f32),
            shape_of((1, inner), f32),
            shape_of((keys, width), bf16),
            shape_of((8, keys), f32),
            shape_of((keys, 128), f32),
        ),
        "svvvvaaaa",
        [pltpu.VMEM((width, slabbed), bf16), pltpu.VMEM((width, SLAB), f32), sem],
        5 * flat * width,
        10 << 20,
    )(me, near, far, near_other, far_other, *group_one)

    half_two = jnp.stack([levels_two, got_two])
    q, half_two, levels_three = tie(q, half_two, levels_three)
    other_two = hop(half_two, plane_two)
    half_two_p = hop(half_two, partner)
    got_three = hop(levels_three, plane_one)

    parts = 2
    pairs_now = width // 128 // parts
    params = pltpu.CompilerParams(vmem_limit_bytes=VMEM_BYTES)

    def attend(part):
        def column(count):
            return pl.BlockSpec((count, 128), lambda i: (0, i + part * pairs_now))

        def column_out(count):
            return pl.BlockSpec((count, 128), lambda i: (0, i))

        def whole(shape):
            return pl.BlockSpec(shape, lambda i: (0, 0))

        return pl.pallas_call(
            attend_kernel,
            name="attend",
            grid=(pairs_now,),
            out_shape=(
                shape_of((tokens, pairs_now * 128), f32),
                shape_of((pairs_now, 8, tokens), f32),
            ),
            in_specs=[
                column(tokens), column(keys), column(keys), whole((keys, 128)), whole((8, keys)),
            ],
            out_specs=(column_out(tokens), pl.BlockSpec((1, 8, tokens), lambda i: (i, 0, 0))),
            scratch_shapes=[pltpu.VMEM((tokens, keys), f32)],
            compiler_params=params,
            cost_estimate=pl.CostEstimate(
                flops=8 * tokens * keys * width // parts, bytes_accessed=4 << 20, transcendentals=0
            ),
        )

    mixed_a, lse_a = attend(0)(q, k, v, segcol, segrow)
    half_three = jnp.stack([levels_three, got_three])
    mixed_a, half_three, q_b = tie(mixed_a, half_three, q)
    mixed_b, lse_b = attend(1)(q_b, k, v, segcol, segrow)
    mixed_b, other_two, half_three = tie(mixed_b, other_two, half_three)
    other_two_p = hop(other_two, partner)
    group_two = (half_two, other_two, half_two_p, other_two_p)
    other_three = hop(half_three, plane_two)
    half_three_p = hop(half_three, partner)

    low, act, slope, unit, inverse, rest = call(
        feed_in_kernel,
        "feed_in",
        (
            shape_of((tokens, width), bf16),
            shape_of((tokens, inner), bf16),
            shape_of((tokens, inner), bf16),
            shape_of((tokens, width), f32),
            shape_of((tokens, 128), f32),
            shape_of((tokens, width), f32),
        ),
        "svvvvvaaaa",
        [pltpu.VMEM((width, width), bf16), pltpu.VMEM((width, inner), bf16), sem, sem],
        flat * (width + inner),
        20 << 20,
    )(me, mixed_a, mixed_b, x_all, vectors, bias, *group_two)

    other_three_p = hop(other_three, partner)
    group_three = (half_three, other_three, half_three_p, other_three_p)
    near_out, far_out, second, outer, sums_two, keep_three, send_three = call(
        feed_out_kernel,
        "feed_out",
        (
            plain_row,
            plain_row,
            shape_of((tokens, width), f32),
            shape_of((tokens, width), bf16),
            shape_of((8, width), f32),
            shape_of((2, 2, depth, inner_rows, width), bf16),
            shape_of((2, 2, depth, inner_rows, width), bf16),
        ),
        "svvvvvaaaa",
        [pltpu.VMEM((inner, width), bf16), pltpu.VMEM((width // 2, width), f32), sem],
        2 * flat * inner,
        20 << 20,
    )(me, act, rest, cot_near, cot_far, vectors, *group_three)

    got = hop(send_three, partner)
    near_out, far_out = hop(near_out, home_near), hop(far_out, home_far)

    grad_pre, bias_sums = call(
        slope_kernel,
        "slope",
        (shape_of((tokens, inner), bf16), shape_of((1, inner), f32)),
        "svvaaaa",
        [pltpu.VMEM((inner, width), bf16), sem],
        flat * inner,
        16 << 20,
    )(me, slope, outer, *group_three)

    def first_sum(keep, got):
        return keep[1] + got[1], keep[0] + got[0]

    def second_sum(kept, got):
        return kept[1] + got[1], kept[0] + got[0]

    def last_sum(levels, arrived):
        total = levels[0].astype(f32)
        for value in arrived:
            total = total + value.astype(f32)
        return total

    def climb(levels):
        return [hop(levels[k + 1], pairs) for k, pairs in enumerate(along_z)]

    three_send, three_kept = first_sum(keep_three, got)
    grad_pre, three_send, three_kept = tie(grad_pre, three_send, three_kept)
    three_got = hop(three_send, plane_one)

    mid, grad_mixed, sums_one, keep_two, send_two = call(
        feed_back_kernel,
        "feed_back",
        (
            shape_of((tokens, width), f32),
            shape_of((tokens, width), bf16),
            shape_of((8, width), f32),
            shape_of((2, 2, depth, rows, width + inner), bf16),
            shape_of((2, 2, depth, rows, width + inner), bf16),
        ),
        "svvvvvvvvaaaa",
        [
            pltpu.VMEM((width, width), bf16),
            pltpu.VMEM((width, inner), bf16),
            pltpu.VMEM((width, width), f32),
            sem, sem,
        ],
        flat * (2 * inner + 2 * width),
        30 << 20,
    )(me, grad_pre, second, low, unit, inverse, mixed_a, mixed_b, vectors, *group_two)

    two_got = hop(send_two, partner)
    three_send, three_kept = three_kept[1] + three_got[1], three_kept[0] + three_got[0]
    grad_mixed, three_send, three_kept = tie(grad_mixed, three_send, three_kept)
    three_got = hop(three_send, plane_two)

    def attend_back(part):
        def column(count):
            return pl.BlockSpec((count, 128), lambda i: (0, i + part * pairs_now))

        def column_out(count):
            return pl.BlockSpec((count, 128), lambda i: (0, i))

        def whole(shape):
            return pl.BlockSpec(shape, lambda i: (0, 0))

        return pl.pallas_call(
            attend_back_kernel,
            name="attend_back",
            grid=(pairs_now,),
            out_shape=(
                shape_of((tokens, pairs_now * 128), bf16),
                shape_of((keys, pairs_now * 128), bf16),
                shape_of((keys, pairs_now * 128), bf16),
            ),
            in_specs=[
                column(tokens), column(keys), column(keys), column(tokens), column_out(tokens),
                pl.BlockSpec((1, 8, tokens), lambda i: (i, 0, 0)),
                whole((keys, 128)), whole((8, keys)),
            ],
            out_specs=(column_out(tokens), column_out(keys), column_out(keys)),
            scratch_shapes=[pltpu.VMEM((keys, tokens), f32)],
            compiler_params=params,
            cost_estimate=pl.CostEstimate(
                flops=20 * tokens * keys * width // parts, bytes_accessed=6 << 20, transcendentals=0
            ),
        )

    back_a = attend_back(0)(q, k, v, grad_mixed, mixed_a, lse_a, segcol, segrow)

    three_levels = three_kept + three_got
    two_send, two_kept = first_sum(keep_two, two_got)
    back_a, three_levels, two_send, two_kept, grad_mixed_b = tie(
        back_a, three_levels, two_send, two_kept, grad_mixed
    )
    three_climb = climb(three_levels)
    two_got = hop(two_send, plane_one)

    back_b = attend_back(1)(q, k, v, grad_mixed_b, mixed_b, lse_b, segcol, segrow)

    total_three = last_sum(three_levels, three_climb)
    two_send, two_kept = second_sum(two_kept, two_got)
    back_b, total_three, two_send, two_kept = tie(back_b, total_three, two_send, two_kept)
    two_got = hop(two_send, plane_two)
    from_partner = hop(
        jnp.concatenate([value[tokens:] for value in back_a[1:] + back_b[1:]], axis=1), partner
    )

    keep_one, send_one = call(
        weight_kernel,
        "weight",
        (
            shape_of((2, 2, depth, rows, slabbed), bf16),
            shape_of((2, 2, depth, rows, slabbed), bf16),
        ),
        "svvvvvvvvvv",
        [pltpu.VMEM((width, width // 2), f32), pltpu.VMEM((width, SLAB), f32)],
        5 * flat * width,
        12 << 20,
    )(me, x_all, *back_a, *back_b, sums_two, sums_one, bias_sums)

    two_levels = two_kept + two_got
    one_got = hop(send_one, partner)
    two_levels, mid, keep_one = tie(two_levels, mid, keep_one)
    two_climb = climb(two_levels)

    near_in, far_in = call(
        input_kernel,
        "input",
        (plain_row, plain_row),
        "svvvvvvvvaaaa",
        [pltpu.VMEM((width, 3 * width), bf16), sem],
        3 * flat * width,
        12 << 20,
    )(me, mid, *back_a, *back_b, from_partner, *group_one)

    one_send, one_kept = first_sum(keep_one, one_got)
    near_in, far_in, one_send, one_kept = tie(near_in, far_in, one_send, one_kept)
    one_got = hop(one_send, plane_one)
    total_two = last_sum(two_levels, two_climb)
    one_send, one_kept = second_sum(one_kept, one_got)
    one_send, one_kept, near_in, far_in, total_two = tie(one_send, one_kept, near_in, far_in, total_two)
    one_got = hop(one_send, plane_two)
    near_in, far_in = hop(near_in, home_near), hop(far_in, home_far)
    one_levels = one_kept + one_got
    one_levels, near_in, far_in = tie(one_levels, near_in, far_in)
    one_climb = climb(one_levels)

    def settle(first, second, dtype):
        return call(
            settle_kernel, "settle", shape_of((2, quarter, width), dtype), "svv", [], 1, 2 << 20
        )(me, first, second)

    result = settle(near_out, far_out, bf16)
    grad_input = settle(near_in, far_in, f32)
    total_one = last_sum(one_levels, one_climb)
    vector = [total_one[j, 3 * width : 3 * width + rows] for j in range(8)]
    grad_b_inner = total_one[8, 3 * width : 3 * width + inner_rows]
    return (
        result,
        grad_input,
        total_one[:, :width],
        vector[0],
        total_one[:, width : 2 * width],
        total_one[:, 2 * width : 3 * width],
        vector[1],
        total_two[:, :width],
        vector[2],
        vector[3],
        vector[4],
        total_two[:, width:],
        grad_b_inner,
        total_three,
        vector[5],
        vector[6],
        vector[7],
    )


def takes_fast(mesh):
    seq, ctx = mesh.shape["seq"], mesh.shape["ctx"]
    return ctx == 4 and seq == 8


def solution(mesh):
    return jax.shard_map(
        functools.partial(fast_device, mesh.shape["seq"] // 2) if takes_fast(mesh) else on_device,
        mesh=mesh,
        in_specs=(
            P("seq", "ctx", None),
            P("seq", "ctx"),
            P("seq", "ctx", None),
            P(("seq", "ctx"), None),
            P(("seq", "ctx")),
            P(("seq", "ctx"), None),
            P(("seq", "ctx"), None),
            P(("seq", "ctx")),
            P(("seq", "ctx"), None),
            P(("seq", "ctx")),
            P(("seq", "ctx")),
            P(("seq", "ctx")),
            P(("seq", "ctx"), None),
            P(("seq", "ctx")),
            P(("seq", "ctx"), None),
            P(("seq", "ctx")),
            P(("seq", "ctx")),
            P(("seq", "ctx")),
        ),
        out_specs=(
            P("seq", "ctx", None),
            P("seq", "ctx", None),
            P(("seq", "ctx"), None),
            P(("seq", "ctx")),
            P(("seq", "ctx"), None),
            P(("seq", "ctx"), None),
            P(("seq", "ctx")),
            P(("seq", "ctx"), None),
            P(("seq", "ctx")),
            P(("seq", "ctx")),
            P(("seq", "ctx")),
            P(("seq", "ctx"), None),
            P(("seq", "ctx")),
            P(("seq", "ctx"), None),
            P(("seq", "ctx")),
            P(("seq", "ctx")),
            P(("seq", "ctx")),
        ),
        check_vma=False,
    )
```

```python
import functools

import jax
import jax.numpy as jnp
from jax import lax
from jax.experimental import pallas as pl
from jax.experimental.pallas import tpu as pltpu
from jax.sharding import PartitionSpec as P

H = 12
DH = 64


epsilon = 1e-06
root_half = 0.7071067811865476
inv_root_tau = 0.3989422804014327


def matmul(left_side, right_side):
    return jnp.dot(left_side, right_side, preferred_element_type=jnp.float32)


def outer_dot(left_side, right_side):
    return lax.dot_general(
        left_side, right_side, (((0,), (0,)), ((), ())), preferred_element_type=jnp.float32
    )


def back_dot(left_side, right_side):
    return lax.dot_general(
        left_side, right_side, (((1,), (1,)), ((), ())), preferred_element_type=jnp.float32
    )


def forward_norm(values, gain_row, shift_row):
    average = jnp.mean(values, axis=-1, keepdims=True)
    centered = values - average
    spread = jnp.mean(centered * centered, axis=-1, keepdims=True)
    inv_scale = lax.rsqrt(spread + epsilon)
    unit_rows = centered * inv_scale
    return (unit_rows * gain_row + shift_row, unit_rows, inv_scale)


def backward_norm(grad_rows, unit_rows, inv_scale, gain_row):
    scaled = grad_rows * gain_row
    plain_mean = jnp.mean(scaled, axis=-1, keepdims=True)
    cross_mean = jnp.mean(scaled * unit_rows, axis=-1, keepdims=True)
    grad_values = inv_scale * (scaled - plain_mean - unit_rows * cross_mean)
    return (grad_values, jnp.sum(grad_rows * unit_rows, axis=0), jnp.sum(grad_rows, axis=0))


def as_float(weights):
    return tuple((item.astype(jnp.float32) if item.ndim == 1 else item for item in weights))


def forward_pass(token_rows, seg_ids, weights):
    (
        w_query,
        b_query,
        w_key,
        w_value,
        b_value,
        w_output,
        b_output,
        attn_gain,
        attn_shift,
        w_inner,
        b_inner,
        w_outer,
        b_outer,
        ffn_gain,
        ffn_shift,
    ) = as_float(weights)
    tokens = token_rows.shape[0]
    model_width = token_rows.shape[1]
    queries = (matmul(token_rows, w_query) + b_query).astype(jnp.bfloat16)
    key_rows = matmul(token_rows, w_key).astype(jnp.bfloat16)
    value_rows = (matmul(token_rows, w_value) + b_value).astype(jnp.bfloat16)
    seg_low = seg_ids.astype(jnp.bfloat16)
    query_heads = queries.reshape(tokens, H, DH)
    piece_keys = lax.all_gather(key_rows, "ctx", axis=0, tiled=True)
    piece_values = lax.all_gather(value_rows, "ctx", axis=0, tiled=True)
    piece_seg = lax.all_gather(seg_low, "ctx", axis=0, tiled=True)
    piece_len = piece_keys.shape[0]
    row_max = jnp.full((H, tokens), -1e30, jnp.float32)
    weighted = jnp.zeros((tokens, H, DH), jnp.float32)
    scores = (
        jnp.einsum(
            "qhd,khd->hqk",
            query_heads,
            piece_keys.reshape(piece_len, H, DH),
            preferred_element_type=jnp.float32,
        )
        * 0.125
    )
    visible = (seg_low[:, None] == piece_seg[None, :])[None]
    masked = jnp.where(visible, scores, -1e30)
    new_max = jnp.maximum(row_max, jnp.max(masked, axis=-1))
    weights_now = jnp.where(visible, jnp.exp(masked - new_max[:, :, None]), 0.0)
    rescale = jnp.exp(row_max - new_max)
    row_sum = jnp.sum(weights_now, axis=-1)
    added = jnp.einsum(
        "hqk,khd->qhd",
        weights_now.astype(jnp.bfloat16),
        piece_values.reshape(piece_len, H, DH),
        preferred_element_type=jnp.float32,
    )
    weighted = rescale.T[:, :, None] * weighted + added
    row_max, row_sum, weighted = (new_max, row_sum, weighted)
    mixed_full = (weighted / row_sum.T[:, :, None]).reshape(tokens, model_width)
    log_sum = row_max + jnp.log(row_sum)
    mixed = mixed_full.astype(jnp.bfloat16)
    branch = matmul(mixed, w_output) + b_output
    normed, unit_one, inv_one = forward_norm(
        token_rows.astype(jnp.float32) + branch, attn_gain, attn_shift
    )
    normed_low = normed.astype(jnp.bfloat16)
    pre_act = matmul(normed_low, w_inner) + b_inner
    activated = jax.nn.gelu(pre_act, approximate=False).astype(jnp.bfloat16)
    outer_sum = matmul(activated, w_outer) + b_outer
    result, unit_two, inv_two = forward_norm(normed + outer_sum, ffn_gain, ffn_shift)
    kept = (
        token_rows,
        seg_low,
        queries,
        key_rows,
        value_rows,
        mixed_full,
        mixed,
        log_sum,
        unit_one,
        inv_one,
        normed_low,
        pre_act,
        activated,
        unit_two,
        inv_two,
    )
    return (kept, result.astype(jnp.bfloat16))


def backward_pass(tangent, kept, weights):
    (
        w_query,
        b_query,
        w_key,
        w_value,
        b_value,
        w_output,
        b_output,
        attn_gain,
        attn_shift,
        w_inner,
        b_inner,
        w_outer,
        b_outer,
        ffn_gain,
        ffn_shift,
    ) = as_float(weights)
    (
        token_rows,
        seg_low,
        queries,
        key_rows,
        value_rows,
        mixed_full,
        mixed,
        log_sum,
        unit_one,
        inv_one,
        normed_low,
        pre_act,
        activated,
        unit_two,
        inv_two,
    ) = kept
    tokens = token_rows.shape[0]
    model_width = token_rows.shape[1]
    grad_second, grad_ffn_gain, grad_ffn_shift = backward_norm(
        tangent.astype(jnp.float32), unit_two, inv_two, ffn_gain
    )
    grad_outer = grad_second.astype(jnp.bfloat16)
    grad_b_outer = jnp.sum(grad_outer.astype(jnp.float32), axis=0)
    grad_w_outer = outer_dot(activated, grad_outer)
    grad_act = back_dot(grad_outer, w_outer)
    normal_cdf = 0.5 * (1.0 + lax.erf(pre_act * root_half))
    density = jnp.exp(-0.5 * pre_act * pre_act) * inv_root_tau
    grad_pre = (grad_act * (normal_cdf + pre_act * density)).astype(jnp.bfloat16)
    grad_b_inner = jnp.sum(grad_pre.astype(jnp.float32), axis=0)
    grad_w_inner = outer_dot(normed_low, grad_pre)
    grad_normed = grad_second + back_dot(grad_pre, w_inner)
    grad_mid, grad_attn_gain, grad_attn_shift = backward_norm(
        grad_normed, unit_one, inv_one, attn_gain
    )
    grad_branch = grad_mid.astype(jnp.bfloat16)
    grad_b_output = jnp.sum(grad_branch.astype(jnp.float32), axis=0)
    grad_w_output = outer_dot(mixed, grad_branch)
    grad_mixed = back_dot(grad_branch, w_output).astype(jnp.bfloat16)
    mixed_heads = grad_mixed.reshape(tokens, H, DH)
    query_heads = queries.reshape(tokens, H, DH)
    row_dot = jnp.sum(
        grad_mixed.astype(jnp.float32).reshape(tokens, H, DH) * mixed_full.reshape(tokens, H, DH),
        axis=-1,
    ).T
    whole_keys, whole_values, whole_seg = (
        lax.all_gather(key_rows, "ctx", axis=0, tiled=True),
        lax.all_gather(value_rows, "ctx", axis=0, tiled=True),
        lax.all_gather(seg_low, "ctx", axis=0, tiled=True),
    )
    length = whole_keys.shape[0]
    key_block = min(512, length)
    block_count = length // key_block

    def visit(block_index, carry_now):
        offset = block_index * key_block
        block_keys = lax.dynamic_slice_in_dim(whole_keys, offset, key_block, 0).reshape(
            key_block, H, DH
        )
        block_values = lax.dynamic_slice_in_dim(whole_values, offset, key_block, 0).reshape(
            key_block, H, DH
        )
        block_seg = lax.dynamic_slice_in_dim(whole_seg, offset, key_block, 0)
        grad_query_sum, key_terms, value_terms = carry_now
        scores = (
            jnp.einsum("qhd,khd->hqk", query_heads, block_keys, preferred_element_type=jnp.float32)
            * 0.125
        )
        visible = (seg_low[:, None] == block_seg[None, :])[None]
        probs = jnp.where(visible, jnp.exp(scores - log_sum[:, :, None]), 0.0)
        grad_probs = jnp.einsum(
            "qhd,khd->hqk", mixed_heads, block_values, preferred_element_type=jnp.float32
        )
        grad_scores = (probs * (grad_probs - row_dot[:, :, None])).astype(jnp.bfloat16)
        grad_query_sum = grad_query_sum + jnp.einsum(
            "hqk,khd->qhd", grad_scores, block_keys, preferred_element_type=jnp.float32
        )
        key_part = (
            jnp.einsum(
                "hqk,qhd->khd", grad_scores, query_heads, preferred_element_type=jnp.float32
            ).reshape(key_block, model_width)
            * 0.125
        )
        value_part = jnp.einsum(
            "hqk,qhd->khd",
            probs.astype(jnp.bfloat16),
            mixed_heads,
            preferred_element_type=jnp.float32,
        ).reshape(key_block, model_width)
        key_terms = lax.dynamic_update_slice_in_dim(key_terms, key_part, offset, 0)
        value_terms = lax.dynamic_update_slice_in_dim(value_terms, value_part, offset, 0)
        return (grad_query_sum, key_terms, value_terms)

    initial = (
        jnp.zeros((tokens, H, DH), jnp.float32),
        jnp.zeros((length, model_width), jnp.float32),
        jnp.zeros((length, model_width), jnp.float32),
    )
    grad_query_sum, key_terms, value_terms = lax.fori_loop(0, block_count, visit, initial)
    grad_key_sum, grad_value_sum = (
        lax.psum_scatter(
            key_terms.astype(jnp.bfloat16), "ctx", scatter_dimension=0, tiled=True
        ).astype(jnp.float32),
        lax.psum_scatter(
            value_terms.astype(jnp.bfloat16), "ctx", scatter_dimension=0, tiled=True
        ).astype(jnp.float32),
    )
    grad_queries = (grad_query_sum.reshape(tokens, model_width) * 0.125).astype(jnp.bfloat16)
    grad_keys = grad_key_sum.astype(jnp.bfloat16)
    grad_values = grad_value_sum.astype(jnp.bfloat16)
    grad_w_query = outer_dot(token_rows, grad_queries)
    grad_b_query = jnp.sum(grad_queries.astype(jnp.float32), axis=0)
    grad_w_key = outer_dot(token_rows, grad_keys)
    grad_w_value = outer_dot(token_rows, grad_values)
    grad_b_value = jnp.sum(grad_values.astype(jnp.float32), axis=0)
    grad_rows = (
        grad_mid
        + back_dot(grad_queries, w_query)
        + back_dot(grad_keys, w_key)
        + back_dot(grad_values, w_value)
    )
    grads = (
        grad_w_query,
        grad_b_query,
        grad_w_key,
        grad_w_value,
        grad_b_value,
        grad_w_output,
        grad_b_output,
        grad_attn_gain,
        grad_attn_shift,
        grad_w_inner,
        grad_b_inner,
        grad_w_outer,
        grad_b_outer,
        grad_ffn_gain,
        grad_ffn_shift,
    )
    return (grad_rows, grads)


def on_device(
    hidden,
    segment,
    cotangent,
    w_query,
    b_query,
    w_key,
    w_value,
    b_value,
    w_output,
    b_output,
    attn_gain,
    attn_shift,
    w_inner,
    b_inner,
    w_outer,
    b_outer,
    ffn_gain,
    ffn_shift,
):
    micro_count = hidden.shape[0]
    totals = None
    results = []
    input_grads = []
    for micro_index in range(micro_count):
        forward_weights = (
            lax.all_gather(w_query, ("seq", "ctx"), axis=0, tiled=True),
            lax.all_gather(b_query, ("seq", "ctx"), axis=0, tiled=True),
            lax.all_gather(w_key, ("seq", "ctx"), axis=0, tiled=True),
            lax.all_gather(w_value, ("seq", "ctx"), axis=0, tiled=True),
            lax.all_gather(b_value, ("seq", "ctx"), axis=0, tiled=True),
            lax.all_gather(w_output, ("seq", "ctx"), axis=0, tiled=True),
            lax.all_gather(b_output, ("seq", "ctx"), axis=0, tiled=True),
            lax.all_gather(attn_gain, ("seq", "ctx"), axis=0, tiled=True),
            lax.all_gather(attn_shift, ("seq", "ctx"), axis=0, tiled=True),
            lax.all_gather(w_inner, ("seq", "ctx"), axis=0, tiled=True),
            lax.all_gather(b_inner, ("seq", "ctx"), axis=0, tiled=True),
            lax.all_gather(w_outer, ("seq", "ctx"), axis=0, tiled=True),
            lax.all_gather(b_outer, ("seq", "ctx"), axis=0, tiled=True),
            lax.all_gather(ffn_gain, ("seq", "ctx"), axis=0, tiled=True),
            lax.all_gather(ffn_shift, ("seq", "ctx"), axis=0, tiled=True),
        )
        kept, result = forward_pass(hidden[micro_index], segment[micro_index], forward_weights)
        results.append(result)
        backward_weights = (
            lax.all_gather(w_query, ("seq", "ctx"), axis=0, tiled=True),
            lax.all_gather(b_query, ("seq", "ctx"), axis=0, tiled=True),
            lax.all_gather(w_key, ("seq", "ctx"), axis=0, tiled=True),
            lax.all_gather(w_value, ("seq", "ctx"), axis=0, tiled=True),
            lax.all_gather(b_value, ("seq", "ctx"), axis=0, tiled=True),
            lax.all_gather(w_output, ("seq", "ctx"), axis=0, tiled=True),
            lax.all_gather(b_output, ("seq", "ctx"), axis=0, tiled=True),
            lax.all_gather(attn_gain, ("seq", "ctx"), axis=0, tiled=True),
            lax.all_gather(attn_shift, ("seq", "ctx"), axis=0, tiled=True),
            lax.all_gather(w_inner, ("seq", "ctx"), axis=0, tiled=True),
            lax.all_gather(b_inner, ("seq", "ctx"), axis=0, tiled=True),
            lax.all_gather(w_outer, ("seq", "ctx"), axis=0, tiled=True),
            lax.all_gather(b_outer, ("seq", "ctx"), axis=0, tiled=True),
            lax.all_gather(ffn_gain, ("seq", "ctx"), axis=0, tiled=True),
            lax.all_gather(ffn_shift, ("seq", "ctx"), axis=0, tiled=True),
        )
        grad_rows, grads = backward_pass(cotangent[micro_index], kept, backward_weights)
        input_grads.append(grad_rows)
        if totals is None:
            totals = grads
        else:
            totals = jax.tree.map(jnp.add, totals, grads)
    owned = (
        lax.psum_scatter(totals[0], ("seq", "ctx"), scatter_dimension=0, tiled=True),
        lax.psum_scatter(totals[1], ("seq", "ctx"), scatter_dimension=0, tiled=True),
        lax.psum_scatter(totals[2], ("seq", "ctx"), scatter_dimension=0, tiled=True),
        lax.psum_scatter(totals[3], ("seq", "ctx"), scatter_dimension=0, tiled=True),
        lax.psum_scatter(totals[4], ("seq", "ctx"), scatter_dimension=0, tiled=True),
        lax.psum_scatter(totals[5], ("seq", "ctx"), scatter_dimension=0, tiled=True),
        lax.psum_scatter(totals[6], ("seq", "ctx"), scatter_dimension=0, tiled=True),
        lax.psum_scatter(totals[7], ("seq", "ctx"), scatter_dimension=0, tiled=True),
        lax.psum_scatter(totals[8], ("seq", "ctx"), scatter_dimension=0, tiled=True),
        lax.psum_scatter(totals[9], ("seq", "ctx"), scatter_dimension=0, tiled=True),
        lax.psum_scatter(totals[10], ("seq", "ctx"), scatter_dimension=0, tiled=True),
        lax.psum_scatter(totals[11], ("seq", "ctx"), scatter_dimension=0, tiled=True),
        lax.psum_scatter(totals[12], ("seq", "ctx"), scatter_dimension=0, tiled=True),
        lax.psum_scatter(totals[13], ("seq", "ctx"), scatter_dimension=0, tiled=True),
        lax.psum_scatter(totals[14], ("seq", "ctx"), scatter_dimension=0, tiled=True),
    )
    return (jnp.stack(results), jnp.stack(input_grads)) + tuple(owned)


AXES = ("seq", "ctx")
LOG2E = 1.4426950408889634
SCORE_UNIT = 0.125 * LOG2E
HIDDEN_SCORE = -1e30
VMEM_BYTES = 62 << 20
SLAB = 128
WEIGHT = 30


def place_of(index, me):
    mz, mc, my, mx = me
    bx, by, bc, bz = index & 1, (index >> 1) & 1, (index >> 2) & 1, index >> 3
    kx, ky, kz = bx ^ mx, by ^ my, bz ^ mz
    even = bc == 0
    first = jnp.where(even, kx, ky)
    second = jnp.where(even, ky, kx)
    return bc == mc, first, second, kz


def read_me(me_ref):
    return me_ref[0], me_ref[1], me_ref[2], me_ref[3]


def start_load(me, pieces, columns, target, rows, count, sem):
    def body(index, carry):
        own, first, second, kz = place_of(index, me)
        spot = target.at[pl.ds(pl.multiple_of(index * rows, 8), rows), :]
        for number, piece in enumerate(pieces):
            mine = own if number < 2 else jnp.logical_not(own)

            @pl.when(jnp.logical_and(mine, second == number % 2))
            def _(piece=piece):
                source = piece.at[first, kz]
                if columns is not None:
                    source = source.at[:, pl.ds(columns[0], columns[1])]
                pltpu.make_async_copy(source, spot, sem).start()

        return carry

    lax.fori_loop(0, count, body, 0)


def end_load(target, sem):
    pltpu.make_async_copy(target, target, sem).wait()


def store_blocks(me, value_ref, keep_ref, send_ref, first_block, count, rows, column, width):
    def body(step, carry):
        own, first, second, kz = place_of(first_block + step, me)
        value = value_ref[pl.ds(pl.multiple_of(step * rows, 8), rows), :].astype(jnp.bfloat16)

        @pl.when(own)
        def _():
            keep_ref[first, second, kz, :, pl.ds(column, width)] = value

        @pl.when(jnp.logical_not(own))
        def _():
            send_ref[first, second, kz, :, pl.ds(column, width)] = value

        return carry

    lax.fori_loop(0, count, body, 0)


def lanes_of(shape):
    return lax.broadcasted_iota(jnp.int32, shape, len(shape) - 1)


def nn(a, b):
    return jnp.dot(a, b, preferred_element_type=jnp.float32)


def nt(a, b):
    return lax.dot_general(a, b, (((1,), (1,)), ((), ())), preferred_element_type=jnp.float32)


def tn(a, b):
    return lax.dot_general(a, b, (((0,), (0,)), ((), ())), preferred_element_type=jnp.float32)


def row_sum(values):
    return jnp.sum(values, axis=0, keepdims=True)


def pack_weights_kernel(wq_ref, wk_ref, wv_ref, *rest):
    vectors, inner_ref, out_ref = rest[:8], rest[8], rest[9]
    rows, width = wq_ref.shape
    out_ref[:, 0:width] = wq_ref[...]
    out_ref[:, width : 2 * width] = wk_ref[...]
    out_ref[:, 2 * width : 3 * width] = wv_ref[...]
    share = inner_ref.shape[1]
    lines = [ref[...].astype(jnp.float32) for ref in vectors]
    lines = [jnp.concatenate([line, jnp.zeros((1, SLAB - rows), jnp.float32)], axis=1) for line in lines]
    last = jnp.concatenate(
        [inner_ref[...].astype(jnp.float32), jnp.zeros((1, SLAB - share), jnp.float32)], axis=1
    )
    slab = jnp.concatenate(lines + [last, jnp.zeros((rows - 9, SLAB), jnp.float32)], axis=0)
    out_ref[:, 3 * width : 3 * width + SLAB] = slab.astype(jnp.bfloat16)


def pack_rows_kernel(me_ref, hidden_ref, segment_ref, cot_ref, near_ref, far_ref):
    x = me_ref[3]
    quarter, width = hidden_ref.shape[1], hidden_ref.shape[2]
    for ref, pick in ((near_ref, x), (far_ref, 1 - x)):
        ref[0:quarter, :] = hidden_ref[pick]
        both = segment_ref[...].astype(jnp.float32)
        line = jnp.where(pick == 0, both[0:1, :], both[1:2, :]).astype(jnp.bfloat16)
        ref[quarter : quarter + 8, 0:quarter] = jnp.broadcast_to(line, (8, quarter))
        ref[quarter : quarter + 8, quarter:width] = jnp.zeros((8, width - quarter), jnp.bfloat16)
        ref[quarter + 8 : 2 * quarter + 8, :] = cot_ref[pick]


def settle_kernel(me_ref, near_ref, far_ref, out_ref):
    x = me_ref[3]
    out_ref[x] = near_ref[...].astype(out_ref.dtype)
    out_ref[1 - x] = far_ref[...].astype(out_ref.dtype)


def spread_lanes(block, share, offset, tiles, tile):
    lane = lanes_of(block.shape)
    moved = pltpu.roll(block, offset, axis=1) if offset else block
    tiles[tile] = jnp.where(
        jnp.logical_and(lane >= offset, lane < offset + share), moved, tiles[tile]
    )
    if offset + share > 128:
        tiles[tile + 1] = jnp.where(lane < offset + share - 128, moved, tiles[tile + 1])


def project_kernel(
    me_ref, r0, r1, r2, r3, p0, p1, p2, p3,
    q_ref, k_ref, v_ref, vec_ref, bias_ref, x_ref, segrow_ref, segcol_ref, w_ref, slab_ref, sem,
):
    me = read_me(me_ref)
    tokens, width = q_ref.shape
    blocks = 32
    rows = width // blocks
    start_load(me, (p0, p1, p2, p3), None, w_ref, rows, blocks, sem)
    quarter = tokens // 2
    for number, ref in enumerate((r0, r1, r2, r3)):
        span = pl.ds(number * quarter, quarter)
        x_ref[span, :] = ref[0:quarter, :]
        line = ref[quarter : quarter + 8, 0:quarter].astype(jnp.float32)
        segrow_ref[:, span] = line
        segcol_ref[span, :] = jnp.broadcast_to(line[0:1, :], (128, quarter)).T
    end_load(w_ref, sem)
    slab_ref[...] = w_ref[:, 3 * width : 3 * width + SLAB].astype(jnp.float32)
    tiles = [jnp.zeros((8, 128), jnp.float32) for _ in range(width // 128 + 1)]
    for index in range(blocks):
        start = rows * index
        spread_lanes(slab_ref[start : start + 8, :], rows, start % 128, tiles, start // 128)
    vectors = jnp.concatenate(tiles[: width // 128], axis=1)
    vec_ref[...] = vectors
    share = bias_ref.shape[1] // blocks
    tiles = [jnp.zeros((8, 128), jnp.float32) for _ in range(4)]
    for turn in range(4):
        lines = slab_ref[pl.ds(rows * turn + 8, 8, stride=4 * rows), :]
        spread_lanes(lines, share, share * turn % 128, tiles, share * turn // 128)
    for group in range(8):
        for tile in range(3):
            bias_ref[0:1, pl.ds(group * 384 + tile * 128, 128)] = tiles[tile][group : group + 1, :]
    b_query, b_value = vectors[0:1, :], vectors[1:2, :]
    q_ref[...] = (nn(x_ref[0:tokens, :], w_ref[:, 0:width]) + b_query).astype(jnp.bfloat16)
    for part in range(2):
        span = pl.ds(part * tokens, tokens)
        k_ref[span, :] = nn(x_ref[span, :], w_ref[:, width : 2 * width]).astype(jnp.bfloat16)
        v_ref[span, :] = (nn(x_ref[span, :], w_ref[:, 2 * width : 3 * width]) + b_value).astype(
            jnp.bfloat16
        )


def attend_kernel(q_ref, k_ref, v_ref, segcol_ref, segrow_ref, mixed_ref, lse_ref, bias_ref):
    tokens = q_ref.shape[0]
    keys = k_ref.shape[0]
    tile = 256

    @pl.when(pl.program_id(0) == 0)
    def _():
        visible = segcol_ref[0:tokens, 0:1] == segrow_ref[0:1, :]
        bias_ref[...] = jnp.where(visible, 0.0, HIDDEN_SCORE)

    low_half = lanes_of((1, 128)) < 64
    key_rows = k_ref[...]
    value_rows = v_ref[...]
    one = jnp.ones((), jnp.bfloat16)
    zero = jnp.zeros((), jnp.bfloat16)
    for part in range(tokens // tile):
        span = pl.ds(part * tile, tile)
        query = q_ref[span, :]
        bias = bias_ref[span, :]
        outs, sums = [], []
        for head in range(2):
            mine = low_half if head == 0 else jnp.logical_not(low_half)
            scores = nt(jnp.where(mine, query, zero), key_rows) + bias
            top = jnp.max(scores, axis=-1, keepdims=True)
            weights = jnp.exp2((scores - top) * SCORE_UNIT).astype(jnp.bfloat16)
            product = nn(weights, jnp.where(mine, value_rows, one))
            total = product[:, 64:65] if head == 0 else product[:, 0:1]
            outs.append(product / total)
            sums.append(top * SCORE_UNIT + jnp.log2(total))
        mixed_ref[span, :] = jnp.where(low_half, outs[0], outs[1])
        lane = lanes_of((tile, 128))
        both = jnp.where(lane == 0, sums[0], jnp.where(lane == 1, sums[1], 0.0))
        lse_ref[0, :, span] = both.T[0:8, :]


def attend_back_kernel(
    q_ref, k_ref, v_ref, gm_ref, mixed_ref, lse_ref, segcol_ref, segrow_ref,
    dq_ref, dk_ref, dv_ref, bias_ref,
):
    tokens = q_ref.shape[0]
    keys = k_ref.shape[0]
    tile = 256

    @pl.when(pl.program_id(0) == 0)
    def _():
        visible = segcol_ref[:, 0:1] == segrow_ref[0:1, 0:tokens]
        bias_ref[...] = jnp.where(visible, 0.0, HIDDEN_SCORE)

    low_half = lanes_of((1, 128)) < 64
    zero = jnp.zeros((), jnp.bfloat16)
    query = q_ref[...]
    grad = gm_ref[...]
    product = (grad.astype(jnp.float32) * mixed_ref[...]).T
    row_dots = [row_sum(product[0:64, :]), row_sum(product[64:128, :])]
    masks = (low_half, jnp.logical_not(low_half))
    queries = [jnp.where(mine, query, zero) for mine in masks]
    grads = [jnp.where(mine, grad, zero) for mine in masks]
    grad_query = jnp.zeros((tokens, 128), jnp.float32)
    for part in range(keys // tile):
        span = pl.ds(part * tile, tile)
        key_rows = k_ref[span, :]
        value_rows = v_ref[span, :]
        bias = bias_ref[span, :]
        grad_key = jnp.zeros((tile, 128), jnp.float32)
        grad_value = jnp.zeros((tile, 128), jnp.float32)
        for head in range(2):
            scores = nt(key_rows, queries[head])
            probs = jnp.exp2(scores * SCORE_UNIT + (bias - lse_ref[0, head : head + 1, :]))
            grad_probs = nt(value_rows, grads[head])
            grad_scores = (probs * (grad_probs - row_dots[head])).astype(jnp.bfloat16)
            grad_key = grad_key + nn(grad_scores, queries[head])
            grad_value = grad_value + nn(probs.astype(jnp.bfloat16), grads[head])
            grad_query = grad_query + tn(grad_scores, jnp.where(masks[head], key_rows, zero))
        dk_ref[span, :] = (grad_key * 0.125).astype(jnp.bfloat16)
        dv_ref[span, :] = grad_value.astype(jnp.bfloat16)
    dq_ref[...] = (grad_query * 0.125).astype(jnp.bfloat16)


def normalize(values):
    average = jnp.mean(values, axis=-1, keepdims=True)
    centered = values - average
    spread = jnp.mean(centered * centered, axis=-1, keepdims=True)
    inverse = lax.rsqrt(spread + epsilon)
    return centered * inverse, inverse


def normalize_back(grad, unit, inverse, gain):
    scaled = grad * gain
    plain = jnp.mean(scaled, axis=-1, keepdims=True)
    cross = jnp.mean(scaled * unit, axis=-1, keepdims=True)
    return inverse * (scaled - plain - unit * cross)


def feed_in_kernel(
    me_ref, mixed_a_ref, mixed_b_ref, x_ref, vec_ref, bias_ref, a0, a1, a2, a3,
    low_ref, act_ref, slope_ref, unit_ref, inverse_ref, rest_ref, wo_ref, wi_ref, sem_o, sem_i,
):
    me = read_me(me_ref)
    tokens, width = low_ref.shape
    inner = wi_ref.shape[1]
    blocks = 32
    start_load(me, (a0, a1, a2, a3), (0, width), wo_ref, width // blocks, blocks, sem_o)
    start_load(me, (a0, a1, a2, a3), (width, inner), wi_ref, width // blocks, blocks, sem_i)
    b_output, attn_gain, attn_shift = vec_ref[2:3, :], vec_ref[3:4, :], vec_ref[4:5, :]
    b_outer = vec_ref[5:6, :]
    end_load(wo_ref, sem_o)
    part = mixed_a_ref.shape[1]
    branch = b_output + nn(mixed_a_ref[...].astype(jnp.bfloat16), wo_ref[0:part, :])
    branch = branch + nn(mixed_b_ref[...].astype(jnp.bfloat16), wo_ref[part:width, :])
    unit_one, inverse_one = normalize(x_ref[0:tokens, :].astype(jnp.float32) + branch)
    normed = unit_one * attn_gain + attn_shift
    unit_ref[...] = unit_one
    inverse_ref[...] = jnp.broadcast_to(inverse_one, inverse_ref.shape)
    low_ref[...] = normed.astype(jnp.bfloat16)
    rest_ref[...] = normed + b_outer
    end_load(wi_ref, sem_i)
    step = 512

    @pl.loop(0, inner // step)
    def _(turn):
        span = pl.ds(pl.multiple_of(turn * step, step), step)
        pre_act = nn(low_ref[...], wi_ref[:, span]) + bias_ref[0:1, span]
        normal_cdf = 0.5 * (1.0 + lax.erf(pre_act * root_half))
        density = jnp.exp(-0.5 * pre_act * pre_act) * inv_root_tau
        act_ref[:, span] = (pre_act * normal_cdf).astype(jnp.bfloat16)
        slope_ref[:, span] = (normal_cdf + pre_act * density).astype(jnp.bfloat16)


def feed_out_kernel(
    me_ref, act_ref, rest_ref, cot_near_ref, cot_far_ref, vec_ref, b0, b1, b2, b3,
    near_ref, far_ref, second_ref, outer_ref, sums_ref, keep_ref, send_ref,
    wu_ref, grad_ref, sem_u,
):
    me = read_me(me_ref)
    tokens, width = rest_ref.shape
    inner = act_ref.shape[1]
    blocks = 32
    rows = inner // blocks
    quarter = tokens // 2
    start_load(me, (b0, b1, b2, b3), None, wu_ref, rows, blocks, sem_u)
    ffn_gain, ffn_shift = vec_ref[6:7, :], vec_ref[7:8, :]
    end_load(wu_ref, sem_u)
    sums = [jnp.zeros((1, width), jnp.float32) for _ in range(3)]
    for part in range(2):
        span = pl.ds(part * quarter, quarter)
        unit_two, inverse_two = normalize(rest_ref[span, :] + nn(act_ref[span, :], wu_ref[...]))
        out_ref, packed_ref = ((near_ref, cot_near_ref), (far_ref, cot_far_ref))[part]
        out_ref[...] = (unit_two * ffn_gain + ffn_shift).astype(jnp.bfloat16)
        tangent = packed_ref[quarter + 8 : tokens + 8, :].astype(jnp.float32)
        second = normalize_back(tangent, unit_two, inverse_two, ffn_gain)
        second_ref[span, :] = second
        outer = second.astype(jnp.bfloat16)
        outer_ref[span, :] = outer
        sums[0] = sums[0] + row_sum(outer.astype(jnp.float32))
        sums[1] = sums[1] + row_sum(tangent * unit_two)
        sums[2] = sums[2] + row_sum(tangent)
    sums_ref[...] = jnp.concatenate(sums + [jnp.zeros((5, width), jnp.float32)], axis=0)
    half = width // 2

    @pl.loop(0, inner // half)
    def _(turn):
        cols = pl.ds(pl.multiple_of(turn * half, half), half)
        grad_ref[...] = tn(act_ref[:, cols], outer_ref[...])
        store_blocks(
            me, grad_ref, keep_ref, send_ref, turn * (half // rows), half // rows, rows, 0, width
        )


def slope_kernel(
    me_ref, slope_ref, outer_ref, b0, b1, b2, b3, pre_ref, bsum_ref, wu_ref, sem_u
):
    me = read_me(me_ref)
    inner = slope_ref.shape[1]
    blocks = 32
    start_load(me, (b0, b1, b2, b3), None, wu_ref, inner // blocks, blocks, sem_u)
    end_load(wu_ref, sem_u)
    step = 512

    @pl.loop(0, inner // step)
    def _(turn):
        span = pl.ds(pl.multiple_of(turn * step, step), step)
        grad_act = nt(outer_ref[...], wu_ref[span, :])
        grad_pre = (grad_act * slope_ref[:, span].astype(jnp.float32)).astype(jnp.bfloat16)
        bsum_ref[0:1, span] = row_sum(grad_pre.astype(jnp.float32))
        pre_ref[:, span] = grad_pre


def feed_back_kernel(
    me_ref, pre_ref, second_ref, low_ref, unit_ref, inverse_ref, mixed_a_ref, mixed_b_ref, vec_ref,
    a0, a1, a2, a3,
    mid_ref, gm_ref, sums_ref, keep_ref, send_ref,
    wo_ref, wi_ref, grad_ref, sem_o, sem_i,
):
    me = read_me(me_ref)
    tokens, width = second_ref.shape
    inner = wi_ref.shape[1]
    blocks = 32
    rows = width // blocks
    start_load(me, (a0, a1, a2, a3), (width, inner), wi_ref, rows, blocks, sem_i)
    start_load(me, (a0, a1, a2, a3), (0, width), wo_ref, rows, blocks, sem_o)
    step = 512

    @pl.loop(0, inner // step)
    def _(turn):
        first = pl.multiple_of(turn * step, step)
        grad_ref[:, 0:step] = tn(low_ref[...], pre_ref[:, pl.ds(first, step)])
        store_blocks(
            me, grad_ref.at[:, 0:step], keep_ref, send_ref, 0, blocks, rows,
            pl.multiple_of(width + first, 128), step,
        )

    end_load(wi_ref, sem_i)
    grad_normed = second_ref[...] + nt(pre_ref[...], wi_ref[...])
    end_load(wo_ref, sem_o)
    attn_gain = vec_ref[3:4, :]
    unit = unit_ref[...]
    mid = normalize_back(grad_normed, unit, inverse_ref[:, 0:1], attn_gain)
    mid_ref[...] = mid
    branch = mid.astype(jnp.bfloat16)
    sums_ref[...] = jnp.zeros(sums_ref.shape, jnp.float32)
    sums_ref[0:1, :] = row_sum(branch.astype(jnp.float32))
    sums_ref[1:2, :] = row_sum(grad_normed * unit)
    sums_ref[2:3, :] = row_sum(grad_normed)
    gm_ref[...] = nt(branch, wo_ref[...]).astype(jnp.bfloat16)
    part = mixed_a_ref.shape[1]
    grad_ref[0:part, :] = tn(mixed_a_ref[...].astype(jnp.bfloat16), branch)
    grad_ref[part:width, :] = tn(mixed_b_ref[...].astype(jnp.bfloat16), branch)
    store_blocks(me, grad_ref, keep_ref, send_ref, 0, blocks, rows, 0, width)


def weight_kernel(
    me_ref, x_ref, dqa_ref, dka_ref, dva_ref, dqb_ref, dkb_ref, dvb_ref,
    sums_two_ref, sums_one_ref, bsum_ref, keep_ref, send_ref, grad_ref, slab_ref,
):
    me = read_me(me_ref)
    tokens, half = dqa_ref.shape
    width = 2 * half
    blocks = 32
    rows = width // blocks
    refs = (dqa_ref, dqb_ref, dka_ref, dkb_ref, dva_ref, dvb_ref)
    for number, ref in enumerate(refs):
        grad_ref[...] = tn(x_ref[0 : ref.shape[0], :], ref[...])
        store_blocks(me, grad_ref, keep_ref, send_ref, 0, blocks, rows, number * half, half)

    def sums(first, second):
        return jnp.concatenate(
            [row_sum(first[...].astype(jnp.float32)), row_sum(second[...].astype(jnp.float32))],
            axis=1,
        )

    vectors = jnp.concatenate(
        [
            sums(dqa_ref, dqb_ref),
            sums(dva_ref, dvb_ref),
            sums_one_ref[0:3, :],
            sums_two_ref[0:3, :],
        ],
        axis=0,
    )
    share = bsum_ref.shape[1] // blocks
    lane = lanes_of((8, 128))
    slab_ref[...] = jnp.zeros(slab_ref.shape, jnp.float32)
    for index in range(blocks):
        tile, offset = rows * index // 128, rows * index % 128
        piece = vectors[:, tile * 128 : tile * 128 + 128]
        if offset + rows > 128:
            piece = jnp.where(
                lane >= offset, piece, vectors[:, tile * 128 + 128 : tile * 128 + 256]
            )
        moved = pltpu.roll(piece, (128 - offset) % 128, axis=1) if offset else piece
        slab_ref[rows * index : rows * index + 8, :] = jnp.where(lane < rows, moved, 0.0)
    groups = jnp.concatenate([bsum_ref[0:1, pl.ds(384 * g, 384)] for g in range(8)], axis=0)
    for turn in range(4):
        tile, offset = share * turn // 128, share * turn % 128
        piece = groups[:, tile * 128 : tile * 128 + 128]
        if offset + share > 128:
            piece = jnp.where(lane >= offset, piece, groups[:, tile * 128 + 128 : tile * 128 + 256])
        moved = pltpu.roll(piece, (128 - offset) % 128, axis=1) if offset else piece
        slab_ref[pl.ds(rows * turn + 8, 8, stride=4 * rows), :] = jnp.where(lane < share, moved, 0.0)
    store_blocks(me, slab_ref, keep_ref, send_ref, 0, blocks, rows, 3 * width, SLAB)


def input_kernel(
    me_ref, mid_ref, dqa_ref, dka_ref, dva_ref, dqb_ref, dkb_ref, dvb_ref, other_ref,
    p0, p1, p2, p3, near_ref, far_ref, w_ref, sem,
):
    me = read_me(me_ref)
    tokens, width = mid_ref.shape
    half = width // 2
    blocks = 32
    start_load(me, (p0, p1, p2, p3), (0, 3 * width), w_ref, width // blocks, blocks, sem)
    own = []
    for number, ref in enumerate((dka_ref, dva_ref, dkb_ref, dvb_ref)):
        theirs = other_ref[:, number * half : (number + 1) * half].astype(jnp.float32)
        own.append((ref[0:tokens, :].astype(jnp.float32) + theirs).astype(jnp.bfloat16))
    end_load(w_ref, sem)
    total = mid_ref[...]
    for number, value in enumerate((dqa_ref[...], dqb_ref[...], own[0], own[2], own[1], own[3])):
        total = total + nt(value, w_ref[:, number * half : (number + 1) * half])
    low = total.astype(jnp.bfloat16)
    near_ref[...] = low[: tokens // 2]
    far_ref[...] = low[tokens // 2 :]


def shape_of(shape, dtype):
    return jax.ShapeDtypeStruct(shape, dtype)


def call(kernel, name, out_shape, kinds, scratch, flops, moved):
    spaces = {"s": pltpu.SMEM, "v": pltpu.VMEM, "a": pl.ANY}
    return pl.pallas_call(
        kernel,
        name=name,
        out_shape=out_shape,
        in_specs=[pl.BlockSpec(memory_space=spaces[kind]) for kind in kinds],
        scratch_shapes=scratch,
        compiler_params=pltpu.CompilerParams(vmem_limit_bytes=VMEM_BYTES),
        cost_estimate=pl.CostEstimate(
            flops=WEIGHT * flops, bytes_accessed=WEIGHT * moved, transcendentals=0
        ),
    )


def tie(*values):
    return lax.optimization_barrier(values)


def fast_device(depth, hidden, segment, cotangent, *weights):
    (
        w_query, b_query, w_key, w_value, b_value, w_output, b_output, attn_gain, attn_shift,
        w_inner, b_inner, w_outer, b_outer, ffn_gain, ffn_shift,
    ) = weights
    bf16, f32 = jnp.bfloat16, jnp.float32
    quarter, width = hidden.shape[1], hidden.shape[2]
    tokens = 2 * quarter
    keys = 2 * tokens
    rows = w_query.shape[0]
    inner = w_inner.shape[1]
    inner_rows = w_outer.shape[0]
    seq_index, ctx_index = lax.axis_index("seq"), lax.axis_index("ctx")
    me = jnp.stack([seq_index >> 1, seq_index & 1, ctx_index >> 1, ctx_index & 1]).astype(jnp.int32)

    def table(move):
        pairs = []
        for bz in range(depth):
            for bc in range(2):
                for by in range(2):
                    for bx in range(2):
                        tz, tc, ty, tx = move(bz, bc, by, bx)
                        pairs.append(
                            (((bz * 2 + bc) * 2 + by) * 2 + bx, ((tz * 2 + tc) * 2 + ty) * 2 + tx)
                        )
        return pairs

    along_z = [table(lambda a, b, d, e, k=k: (a ^ k, b, d, e)) for k in range(1, depth)]
    plane_one = table(lambda a, b, d, e: (a, b, d, 1 - e) if b == 0 else (a, b, 1 - d, e))
    plane_two = table(lambda a, b, d, e: (a, b, 1 - d, e) if b == 0 else (a, b, d, 1 - e))
    partner = table(lambda a, b, d, e: (a, 1 - b, d, e))
    home_near = table(lambda a, b, d, e: (a, d, b, e))
    home_far = table(lambda a, b, d, e: (a, d, b, 1 - e))

    def hop(value, pairs):
        return lax.ppermute(value, AXES, pairs)

    def levels_of(value):
        return jnp.stack([value] + [hop(value, pairs) for pairs in along_z])

    sem = pltpu.SemaphoreType.DMA
    flat = 2 * tokens * width
    slabbed = 3 * width + SLAB

    vectors_in = (
        b_query, b_value, b_output, attn_gain, attn_shift, b_outer, ffn_gain, ffn_shift, b_inner,
    )
    packed = call(
        pack_weights_kernel, "pack_weights", shape_of((rows, slabbed), bf16), "v" * 12, [], 1, 1 << 20
    )(w_query, w_key, w_value, *[vector[None, :] for vector in vectors_in])
    levels_one = levels_of(packed)

    packed_row = shape_of((tokens + 8, width), bf16)
    near, far = call(
        pack_rows_kernel, "pack_rows", (packed_row, packed_row), "svvv", [], 1, 1 << 20
    )(me, hidden, segment, cotangent)
    near, far = hop(near, home_near), hop(far, home_far)
    plain_row = shape_of((quarter, width), bf16)

    second_in = jnp.concatenate([w_output, w_inner], axis=1)
    levels_one, second_in = tie(levels_one, second_in)
    half_one = jnp.stack([levels_one, hop(levels_one, plane_one)])
    levels_two = levels_of(second_in)

    half_one, near, far = tie(half_one, near, far)
    other_one = hop(half_one, plane_two)
    half_one_p = hop(half_one, partner)
    near_other, far_other = hop(near, partner), hop(far, partner)
    other_one, levels_two, third_in = tie(other_one, levels_two, w_outer)
    other_one_p = hop(other_one, partner)
    got_two = hop(levels_two, plane_one)
    levels_three = levels_of(third_in)
    group_one = (half_one, other_one, half_one_p, other_one_p)

    q, k, v, vectors, bias, x_all, segrow, segcol = call(
        project_kernel,
        "project",
        (
            shape_of((tokens, width), bf16),
            shape_of((keys, width), bf16),
            shape_of((keys, width), bf16),
            shape_of((8, width), f32),
            shape_of((1, inner), f32),
            shape_of((keys, width), bf16),
            shape_of((8, keys), f32),
            shape_of((keys, 128), f32),
        ),
        "svvvvaaaa",
        [pltpu.VMEM((width, slabbed), bf16), pltpu.VMEM((width, SLAB), f32), sem],
        5 * flat * width,
        10 << 20,
    )(me, near, far, near_other, far_other, *group_one)

    half_two = jnp.stack([levels_two, got_two])
    q, half_two, levels_three = tie(q, half_two, levels_three)
    other_two = hop(half_two, plane_two)
    half_two_p = hop(half_two, partner)
    got_three = hop(levels_three, plane_one)

    parts = 2
    pairs_now = width // 128 // parts
    params = pltpu.CompilerParams(vmem_limit_bytes=VMEM_BYTES)

    def attend(part):
        def column(count):
            return pl.BlockSpec((count, 128), lambda i: (0, i + part * pairs_now))

        def column_out(count):
            return pl.BlockSpec((count, 128), lambda i: (0, i))

        def whole(shape):
            return pl.BlockSpec(shape, lambda i: (0, 0))

        return pl.pallas_call(
            attend_kernel,
            name="attend",
            grid=(pairs_now,),
            out_shape=(
                shape_of((tokens, pairs_now * 128), f32),
                shape_of((pairs_now, 8, tokens), f32),
            ),
            in_specs=[
                column(tokens), column(keys), column(keys), whole((keys, 128)), whole((8, keys)),
            ],
            out_specs=(column_out(tokens), pl.BlockSpec((1, 8, tokens), lambda i: (i, 0, 0))),
            scratch_shapes=[pltpu.VMEM((tokens, keys), f32)],
            compiler_params=params,
            cost_estimate=pl.CostEstimate(
                flops=WEIGHT * 8 * tokens * keys * width // parts, bytes_accessed=WEIGHT << 22, transcendentals=0
            ),
        )

    mixed_a, lse_a = attend(0)(q, k, v, segcol, segrow)
    half_three = jnp.stack([levels_three, got_three])
    q_b, mixed_a = tie(q, mixed_a)
    mixed_b, lse_b = attend(1)(q_b, k, v, segcol, segrow)
    mixed_b, other_two, half_three = tie(mixed_b, other_two, half_three)
    other_two_p = hop(other_two, partner)
    group_two = (half_two, other_two, half_two_p, other_two_p)
    other_three = hop(half_three, plane_two)
    half_three_p = hop(half_three, partner)

    low, act, slope, unit, inverse, rest = call(
        feed_in_kernel,
        "feed_in",
        (
            shape_of((tokens, width), bf16),
            shape_of((tokens, inner), bf16),
            shape_of((tokens, inner), bf16),
            shape_of((tokens, width), f32),
            shape_of((tokens, 128), f32),
            shape_of((tokens, width), f32),
        ),
        "svvvvvaaaa",
        [pltpu.VMEM((width, width), bf16), pltpu.VMEM((width, inner), bf16), sem, sem],
        flat * (width + inner),
        20 << 20,
    )(me, mixed_a, mixed_b, x_all, vectors, bias, *group_two)

    act, other_three = tie(act, other_three)
    other_three_p = hop(other_three, partner)
    group_three = (half_three, other_three, half_three_p, other_three_p)
    near_out, far_out, second, outer, sums_two, keep_three, send_three = call(
        feed_out_kernel,
        "feed_out",
        (
            plain_row,
            plain_row,
            shape_of((tokens, width), f32),
            shape_of((tokens, width), bf16),
            shape_of((8, width), f32),
            shape_of((2, 2, depth, inner_rows, width), bf16),
            shape_of((2, 2, depth, inner_rows, width), bf16),
        ),
        "svvvvvaaaa",
        [pltpu.VMEM((inner, width), bf16), pltpu.VMEM((width // 2, width), f32), sem],
        2 * flat * inner,
        20 << 20,
    )(me, act, rest, near, far, vectors, *group_three)

    got = hop(send_three, partner)
    near_out, far_out = hop(near_out, home_near), hop(far_out, home_far)

    grad_pre, bias_sums = call(
        slope_kernel,
        "slope",
        (shape_of((tokens, inner), bf16), shape_of((1, inner), f32)),
        "svvaaaa",
        [pltpu.VMEM((inner, width), bf16), sem],
        flat * inner,
        16 << 20,
    )(me, slope, outer, *group_three)

    def first_sum(keep, got):
        return keep[1] + got[1], keep[0] + got[0]

    def second_sum(kept, got):
        return kept[1] + got[1], kept[0] + got[0]

    def last_sum(levels, arrived):
        total = levels[0].astype(f32)
        for value in arrived:
            total = total + value.astype(f32)
        return total

    def climb(levels):
        return [hop(levels[k + 1], pairs) for k, pairs in enumerate(along_z)]

    three_send, three_kept = first_sum(keep_three, got)
    grad_pre, three_send, three_kept, near_out, far_out = tie(
        grad_pre, three_send, three_kept, near_out, far_out
    )
    three_got = hop(three_send, plane_one)

    mid, grad_mixed, sums_one, keep_two, send_two = call(
        feed_back_kernel,
        "feed_back",
        (
            shape_of((tokens, width), f32),
            shape_of((tokens, width), bf16),
            shape_of((8, width), f32),
            shape_of((2, 2, depth, rows, width + inner), bf16),
            shape_of((2, 2, depth, rows, width + inner), bf16),
        ),
        "svvvvvvvvaaaa",
        [
            pltpu.VMEM((width, width), bf16),
            pltpu.VMEM((width, inner), bf16),
            pltpu.VMEM((width, width), f32),
            sem, sem,
        ],
        flat * (2 * inner + 2 * width),
        30 << 20,
    )(me, grad_pre, second, low, unit, inverse, mixed_a, mixed_b, vectors, *group_two)

    two_got = hop(send_two, partner)
    three_send, three_kept = three_kept[1] + three_got[1], three_kept[0] + three_got[0]
    grad_mixed, three_send, three_kept = tie(grad_mixed, three_send, three_kept)
    three_got = hop(three_send, plane_two)

    def attend_back(part):
        def column(count):
            return pl.BlockSpec((count, 128), lambda i: (0, i + part * pairs_now))

        def column_out(count):
            return pl.BlockSpec((count, 128), lambda i: (0, i))

        def whole(shape):
            return pl.BlockSpec(shape, lambda i: (0, 0))

        return pl.pallas_call(
            attend_back_kernel,
            name="attend_back",
            grid=(pairs_now,),
            out_shape=(
                shape_of((tokens, pairs_now * 128), bf16),
                shape_of((keys, pairs_now * 128), bf16),
                shape_of((keys, pairs_now * 128), bf16),
            ),
            in_specs=[
                column(tokens), column(keys), column(keys), column(tokens), column_out(tokens),
                pl.BlockSpec((1, 8, tokens), lambda i: (i, 0, 0)),
                whole((keys, 128)), whole((8, keys)),
            ],
            out_specs=(column_out(tokens), column_out(keys), column_out(keys)),
            scratch_shapes=[pltpu.VMEM((keys, tokens), f32)],
            compiler_params=params,
            cost_estimate=pl.CostEstimate(
                flops=WEIGHT * 20 * tokens * keys * width // parts, bytes_accessed=WEIGHT << 22, transcendentals=0
            ),
        )

    back_a = attend_back(0)(q, k, v, grad_mixed, mixed_a, lse_a, segcol, segrow)

    three_levels = three_kept + three_got
    two_send, two_kept = first_sum(keep_two, two_got)
    back_a, three_levels, two_send, two_kept, grad_mixed_b = tie(
        back_a, three_levels, two_send, two_kept, grad_mixed
    )
    three_climb = climb(three_levels)
    two_got = hop(two_send, plane_one)

    back_b = attend_back(1)(q, k, v, grad_mixed_b, mixed_b, lse_b, segcol, segrow)

    total_three = last_sum(three_levels, three_climb)
    two_send, two_kept = second_sum(two_kept, two_got)
    back_b, total_three, two_send, two_kept = tie(back_b, total_three, two_send, two_kept)
    two_got = hop(two_send, plane_two)
    from_partner = hop(
        jnp.concatenate([value[tokens:] for value in back_a[1:] + back_b[1:]], axis=1), partner
    )

    keep_one, send_one = call(
        weight_kernel,
        "weight",
        (
            shape_of((2, 2, depth, rows, slabbed), bf16),
            shape_of((2, 2, depth, rows, slabbed), bf16),
        ),
        "svvvvvvvvvv",
        [pltpu.VMEM((width, width // 2), f32), pltpu.VMEM((width, SLAB), f32)],
        5 * flat * width,
        12 << 20,
    )(me, x_all, *back_a, *back_b, sums_two, sums_one, bias_sums)

    one_got = hop(send_one, partner)
    keep_one, two_levels = tie(keep_one, two_kept + two_got)
    two_climb = climb(two_levels)
    one_send, one_kept = first_sum(keep_one, one_got)
    mid, one_send, one_kept = tie(mid, one_send, one_kept)
    one_got = hop(one_send, plane_one)

    near_in, far_in = call(
        input_kernel,
        "input",
        (plain_row, plain_row),
        "svvvvvvvvaaaa",
        [pltpu.VMEM((width, 3 * width), bf16), sem],
        3 * flat * width,
        12 << 20,
    )(me, mid, *back_a, *back_b, from_partner, *group_one)

    one_got, near_in, far_in = tie(one_got, near_in, far_in)
    one_send, one_kept = second_sum(one_kept, one_got)
    one_got = hop(one_send, plane_two)
    total_two = last_sum(two_levels, two_climb)
    one_levels = one_kept + one_got
    one_levels, near_in, far_in, total_two = tie(one_levels, near_in, far_in, total_two)
    near_in, far_in = hop(near_in, home_near), hop(far_in, home_far)
    one_climb = climb(one_levels)

    def settle(first, second, dtype):
        return call(
            settle_kernel, "settle", shape_of((2, quarter, width), dtype), "svv", [], 1, 2 << 20
        )(me, first, second)

    result = settle(near_out, far_out, bf16)
    grad_input = settle(near_in, far_in, f32)
    total_one = last_sum(one_levels, one_climb)
    vector = [total_one[j, 3 * width : 3 * width + rows] for j in range(8)]
    grad_b_inner = total_one[8, 3 * width : 3 * width + inner_rows]
    return (
        result,
        grad_input,
        total_one[:, :width],
        vector[0],
        total_one[:, width : 2 * width],
        total_one[:, 2 * width : 3 * width],
        vector[1],
        total_two[:, :width],
        vector[2],
        vector[3],
        vector[4],
        total_two[:, width:],
        grad_b_inner,
        total_three,
        vector[5],
        vector[6],
        vector[7],
    )


def takes_fast(mesh):
    seq, ctx = mesh.shape["seq"], mesh.shape["ctx"]
    return ctx == 4 and seq == 8


def solution(mesh):
    return jax.shard_map(
        functools.partial(fast_device, mesh.shape["seq"] // 2) if takes_fast(mesh) else on_device,
        mesh=mesh,
        in_specs=(
            P("seq", "ctx", None),
            P("seq", "ctx"),
            P("seq", "ctx", None),
            P(("seq", "ctx"), None),
            P(("seq", "ctx")),
            P(("seq", "ctx"), None),
            P(("seq", "ctx"), None),
            P(("seq", "ctx")),
            P(("seq", "ctx"), None),
            P(("seq", "ctx")),
            P(("seq", "ctx")),
            P(("seq", "ctx")),
            P(("seq", "ctx"), None),
            P(("seq", "ctx")),
            P(("seq", "ctx"), None),
            P(("seq", "ctx")),
            P(("seq", "ctx")),
            P(("seq", "ctx")),
        ),
        out_specs=(
            P("seq", "ctx", None),
            P("seq", "ctx", None),
            P(("seq", "ctx"), None),
            P(("seq", "ctx")),
            P(("seq", "ctx"), None),
            P(("seq", "ctx"), None),
            P(("seq", "ctx")),
            P(("seq", "ctx"), None),
            P(("seq", "ctx")),
            P(("seq", "ctx")),
            P(("seq", "ctx")),
            P(("seq", "ctx"), None),
            P(("seq", "ctx")),
            P(("seq", "ctx"), None),
            P(("seq", "ctx")),
            P(("seq", "ctx")),
            P(("seq", "ctx")),
        ),
        check_vma=False,
    )
```

```python
import functools

import jax
import jax.numpy as jnp
from jax import lax
from jax.experimental import pallas as pl
from jax.experimental.pallas import tpu as pltpu
from jax.sharding import PartitionSpec as P

H = 12
DH = 64


epsilon = 1e-06
root_half = 0.7071067811865476
inv_root_tau = 0.3989422804014327


def matmul(left_side, right_side):
    return jnp.dot(left_side, right_side, preferred_element_type=jnp.float32)


def outer_dot(left_side, right_side):
    return lax.dot_general(
        left_side, right_side, (((0,), (0,)), ((), ())), preferred_element_type=jnp.float32
    )


def back_dot(left_side, right_side):
    return lax.dot_general(
        left_side, right_side, (((1,), (1,)), ((), ())), preferred_element_type=jnp.float32
    )


def forward_norm(values, gain_row, shift_row):
    average = jnp.mean(values, axis=-1, keepdims=True)
    centered = values - average
    spread = jnp.mean(centered * centered, axis=-1, keepdims=True)
    inv_scale = lax.rsqrt(spread + epsilon)
    unit_rows = centered * inv_scale
    return (unit_rows * gain_row + shift_row, unit_rows, inv_scale)


def backward_norm(grad_rows, unit_rows, inv_scale, gain_row):
    scaled = grad_rows * gain_row
    plain_mean = jnp.mean(scaled, axis=-1, keepdims=True)
    cross_mean = jnp.mean(scaled * unit_rows, axis=-1, keepdims=True)
    grad_values = inv_scale * (scaled - plain_mean - unit_rows * cross_mean)
    return (grad_values, jnp.sum(grad_rows * unit_rows, axis=0), jnp.sum(grad_rows, axis=0))


def as_float(weights):
    return tuple((item.astype(jnp.float32) if item.ndim == 1 else item for item in weights))


def forward_pass(token_rows, seg_ids, weights):
    (
        w_query,
        b_query,
        w_key,
        w_value,
        b_value,
        w_output,
        b_output,
        attn_gain,
        attn_shift,
        w_inner,
        b_inner,
        w_outer,
        b_outer,
        ffn_gain,
        ffn_shift,
    ) = as_float(weights)
    tokens = token_rows.shape[0]
    model_width = token_rows.shape[1]
    queries = (matmul(token_rows, w_query) + b_query).astype(jnp.bfloat16)
    key_rows = matmul(token_rows, w_key).astype(jnp.bfloat16)
    value_rows = (matmul(token_rows, w_value) + b_value).astype(jnp.bfloat16)
    seg_low = seg_ids.astype(jnp.bfloat16)
    query_heads = queries.reshape(tokens, H, DH)
    piece_keys = lax.all_gather(key_rows, "ctx", axis=0, tiled=True)
    piece_values = lax.all_gather(value_rows, "ctx", axis=0, tiled=True)
    piece_seg = lax.all_gather(seg_low, "ctx", axis=0, tiled=True)
    piece_len = piece_keys.shape[0]
    row_max = jnp.full((H, tokens), -1e30, jnp.float32)
    weighted = jnp.zeros((tokens, H, DH), jnp.float32)
    scores = (
        jnp.einsum(
            "qhd,khd->hqk",
            query_heads,
            piece_keys.reshape(piece_len, H, DH),
            preferred_element_type=jnp.float32,
        )
        * 0.125
    )
    visible = (seg_low[:, None] == piece_seg[None, :])[None]
    masked = jnp.where(visible, scores, -1e30)
    new_max = jnp.maximum(row_max, jnp.max(masked, axis=-1))
    weights_now = jnp.where(visible, jnp.exp(masked - new_max[:, :, None]), 0.0)
    rescale = jnp.exp(row_max - new_max)
    row_sum = jnp.sum(weights_now, axis=-1)
    added = jnp.einsum(
        "hqk,khd->qhd",
        weights_now.astype(jnp.bfloat16),
        piece_values.reshape(piece_len, H, DH),
        preferred_element_type=jnp.float32,
    )
    weighted = rescale.T[:, :, None] * weighted + added
    row_max, row_sum, weighted = (new_max, row_sum, weighted)
    mixed_full = (weighted / row_sum.T[:, :, None]).reshape(tokens, model_width)
    log_sum = row_max + jnp.log(row_sum)
    mixed = mixed_full.astype(jnp.bfloat16)
    branch = matmul(mixed, w_output) + b_output
    normed, unit_one, inv_one = forward_norm(
        token_rows.astype(jnp.float32) + branch, attn_gain, attn_shift
    )
    normed_low = normed.astype(jnp.bfloat16)
    pre_act = matmul(normed_low, w_inner) + b_inner
    activated = jax.nn.gelu(pre_act, approximate=False).astype(jnp.bfloat16)
    outer_sum = matmul(activated, w_outer) + b_outer
    result, unit_two, inv_two = forward_norm(normed + outer_sum, ffn_gain, ffn_shift)
    kept = (
        token_rows,
        seg_low,
        queries,
        key_rows,
        value_rows,
        mixed_full,
        mixed,
        log_sum,
        unit_one,
        inv_one,
        normed_low,
        pre_act,
        activated,
        unit_two,
        inv_two,
    )
    return (kept, result.astype(jnp.bfloat16))


def backward_pass(tangent, kept, weights):
    (
        w_query,
        b_query,
        w_key,
        w_value,
        b_value,
        w_output,
        b_output,
        attn_gain,
        attn_shift,
        w_inner,
        b_inner,
        w_outer,
        b_outer,
        ffn_gain,
        ffn_shift,
    ) = as_float(weights)
    (
        token_rows,
        seg_low,
        queries,
        key_rows,
        value_rows,
        mixed_full,
        mixed,
        log_sum,
        unit_one,
        inv_one,
        normed_low,
        pre_act,
        activated,
        unit_two,
        inv_two,
    ) = kept
    tokens = token_rows.shape[0]
    model_width = token_rows.shape[1]
    grad_second, grad_ffn_gain, grad_ffn_shift = backward_norm(
        tangent.astype(jnp.float32), unit_two, inv_two, ffn_gain
    )
    grad_outer = grad_second.astype(jnp.bfloat16)
    grad_b_outer = jnp.sum(grad_outer.astype(jnp.float32), axis=0)
    grad_w_outer = outer_dot(activated, grad_outer)
    grad_act = back_dot(grad_outer, w_outer)
    normal_cdf = 0.5 * (1.0 + lax.erf(pre_act * root_half))
    density = jnp.exp(-0.5 * pre_act * pre_act) * inv_root_tau
    grad_pre = (grad_act * (normal_cdf + pre_act * density)).astype(jnp.bfloat16)
    grad_b_inner = jnp.sum(grad_pre.astype(jnp.float32), axis=0)
    grad_w_inner = outer_dot(normed_low, grad_pre)
    grad_normed = grad_second + back_dot(grad_pre, w_inner)
    grad_mid, grad_attn_gain, grad_attn_shift = backward_norm(
        grad_normed, unit_one, inv_one, attn_gain
    )
    grad_branch = grad_mid.astype(jnp.bfloat16)
    grad_b_output = jnp.sum(grad_branch.astype(jnp.float32), axis=0)
    grad_w_output = outer_dot(mixed, grad_branch)
    grad_mixed = back_dot(grad_branch, w_output).astype(jnp.bfloat16)
    mixed_heads = grad_mixed.reshape(tokens, H, DH)
    query_heads = queries.reshape(tokens, H, DH)
    row_dot = jnp.sum(
        grad_mixed.astype(jnp.float32).reshape(tokens, H, DH) * mixed_full.reshape(tokens, H, DH),
        axis=-1,
    ).T
    whole_keys, whole_values, whole_seg = (
        lax.all_gather(key_rows, "ctx", axis=0, tiled=True),
        lax.all_gather(value_rows, "ctx", axis=0, tiled=True),
        lax.all_gather(seg_low, "ctx", axis=0, tiled=True),
    )
    length = whole_keys.shape[0]
    key_block = min(512, length)
    block_count = length // key_block

    def visit(block_index, carry_now):
        offset = block_index * key_block
        block_keys = lax.dynamic_slice_in_dim(whole_keys, offset, key_block, 0).reshape(
            key_block, H, DH
        )
        block_values = lax.dynamic_slice_in_dim(whole_values, offset, key_block, 0).reshape(
            key_block, H, DH
        )
        block_seg = lax.dynamic_slice_in_dim(whole_seg, offset, key_block, 0)
        grad_query_sum, key_terms, value_terms = carry_now
        scores = (
            jnp.einsum("qhd,khd->hqk", query_heads, block_keys, preferred_element_type=jnp.float32)
            * 0.125
        )
        visible = (seg_low[:, None] == block_seg[None, :])[None]
        probs = jnp.where(visible, jnp.exp(scores - log_sum[:, :, None]), 0.0)
        grad_probs = jnp.einsum(
            "qhd,khd->hqk", mixed_heads, block_values, preferred_element_type=jnp.float32
        )
        grad_scores = (probs * (grad_probs - row_dot[:, :, None])).astype(jnp.bfloat16)
        grad_query_sum = grad_query_sum + jnp.einsum(
            "hqk,khd->qhd", grad_scores, block_keys, preferred_element_type=jnp.float32
        )
        key_part = (
            jnp.einsum(
                "hqk,qhd->khd", grad_scores, query_heads, preferred_element_type=jnp.float32
            ).reshape(key_block, model_width)
            * 0.125
        )
        value_part = jnp.einsum(
            "hqk,qhd->khd",
            probs.astype(jnp.bfloat16),
            mixed_heads,
            preferred_element_type=jnp.float32,
        ).reshape(key_block, model_width)
        key_terms = lax.dynamic_update_slice_in_dim(key_terms, key_part, offset, 0)
        value_terms = lax.dynamic_update_slice_in_dim(value_terms, value_part, offset, 0)
        return (grad_query_sum, key_terms, value_terms)

    initial = (
        jnp.zeros((tokens, H, DH), jnp.float32),
        jnp.zeros((length, model_width), jnp.float32),
        jnp.zeros((length, model_width), jnp.float32),
    )
    grad_query_sum, key_terms, value_terms = lax.fori_loop(0, block_count, visit, initial)
    grad_key_sum, grad_value_sum = (
        lax.psum_scatter(
            key_terms.astype(jnp.bfloat16), "ctx", scatter_dimension=0, tiled=True
        ).astype(jnp.float32),
        lax.psum_scatter(
            value_terms.astype(jnp.bfloat16), "ctx", scatter_dimension=0, tiled=True
        ).astype(jnp.float32),
    )
    grad_queries = (grad_query_sum.reshape(tokens, model_width) * 0.125).astype(jnp.bfloat16)
    grad_keys = grad_key_sum.astype(jnp.bfloat16)
    grad_values = grad_value_sum.astype(jnp.bfloat16)
    grad_w_query = outer_dot(token_rows, grad_queries)
    grad_b_query = jnp.sum(grad_queries.astype(jnp.float32), axis=0)
    grad_w_key = outer_dot(token_rows, grad_keys)
    grad_w_value = outer_dot(token_rows, grad_values)
    grad_b_value = jnp.sum(grad_values.astype(jnp.float32), axis=0)
    grad_rows = (
        grad_mid
        + back_dot(grad_queries, w_query)
        + back_dot(grad_keys, w_key)
        + back_dot(grad_values, w_value)
    )
    grads = (
        grad_w_query,
        grad_b_query,
        grad_w_key,
        grad_w_value,
        grad_b_value,
        grad_w_output,
        grad_b_output,
        grad_attn_gain,
        grad_attn_shift,
        grad_w_inner,
        grad_b_inner,
        grad_w_outer,
        grad_b_outer,
        grad_ffn_gain,
        grad_ffn_shift,
    )
    return (grad_rows, grads)


def on_device(
    hidden,
    segment,
    cotangent,
    w_query,
    b_query,
    w_key,
    w_value,
    b_value,
    w_output,
    b_output,
    attn_gain,
    attn_shift,
    w_inner,
    b_inner,
    w_outer,
    b_outer,
    ffn_gain,
    ffn_shift,
):
    micro_count = hidden.shape[0]
    totals = None
    results = []
    input_grads = []
    for micro_index in range(micro_count):
        forward_weights = (
            lax.all_gather(w_query, ("seq", "ctx"), axis=0, tiled=True),
            lax.all_gather(b_query, ("seq", "ctx"), axis=0, tiled=True),
            lax.all_gather(w_key, ("seq", "ctx"), axis=0, tiled=True),
            lax.all_gather(w_value, ("seq", "ctx"), axis=0, tiled=True),
            lax.all_gather(b_value, ("seq", "ctx"), axis=0, tiled=True),
            lax.all_gather(w_output, ("seq", "ctx"), axis=0, tiled=True),
            lax.all_gather(b_output, ("seq", "ctx"), axis=0, tiled=True),
            lax.all_gather(attn_gain, ("seq", "ctx"), axis=0, tiled=True),
            lax.all_gather(attn_shift, ("seq", "ctx"), axis=0, tiled=True),
            lax.all_gather(w_inner, ("seq", "ctx"), axis=0, tiled=True),
            lax.all_gather(b_inner, ("seq", "ctx"), axis=0, tiled=True),
            lax.all_gather(w_outer, ("seq", "ctx"), axis=0, tiled=True),
            lax.all_gather(b_outer, ("seq", "ctx"), axis=0, tiled=True),
            lax.all_gather(ffn_gain, ("seq", "ctx"), axis=0, tiled=True),
            lax.all_gather(ffn_shift, ("seq", "ctx"), axis=0, tiled=True),
        )
        kept, result = forward_pass(hidden[micro_index], segment[micro_index], forward_weights)
        results.append(result)
        backward_weights = (
            lax.all_gather(w_query, ("seq", "ctx"), axis=0, tiled=True),
            lax.all_gather(b_query, ("seq", "ctx"), axis=0, tiled=True),
            lax.all_gather(w_key, ("seq", "ctx"), axis=0, tiled=True),
            lax.all_gather(w_value, ("seq", "ctx"), axis=0, tiled=True),
            lax.all_gather(b_value, ("seq", "ctx"), axis=0, tiled=True),
            lax.all_gather(w_output, ("seq", "ctx"), axis=0, tiled=True),
            lax.all_gather(b_output, ("seq", "ctx"), axis=0, tiled=True),
            lax.all_gather(attn_gain, ("seq", "ctx"), axis=0, tiled=True),
            lax.all_gather(attn_shift, ("seq", "ctx"), axis=0, tiled=True),
            lax.all_gather(w_inner, ("seq", "ctx"), axis=0, tiled=True),
            lax.all_gather(b_inner, ("seq", "ctx"), axis=0, tiled=True),
            lax.all_gather(w_outer, ("seq", "ctx"), axis=0, tiled=True),
            lax.all_gather(b_outer, ("seq", "ctx"), axis=0, tiled=True),
            lax.all_gather(ffn_gain, ("seq", "ctx"), axis=0, tiled=True),
            lax.all_gather(ffn_shift, ("seq", "ctx"), axis=0, tiled=True),
        )
        grad_rows, grads = backward_pass(cotangent[micro_index], kept, backward_weights)
        input_grads.append(grad_rows)
        if totals is None:
            totals = grads
        else:
            totals = jax.tree.map(jnp.add, totals, grads)
    owned = (
        lax.psum_scatter(totals[0], ("seq", "ctx"), scatter_dimension=0, tiled=True),
        lax.psum_scatter(totals[1], ("seq", "ctx"), scatter_dimension=0, tiled=True),
        lax.psum_scatter(totals[2], ("seq", "ctx"), scatter_dimension=0, tiled=True),
        lax.psum_scatter(totals[3], ("seq", "ctx"), scatter_dimension=0, tiled=True),
        lax.psum_scatter(totals[4], ("seq", "ctx"), scatter_dimension=0, tiled=True),
        lax.psum_scatter(totals[5], ("seq", "ctx"), scatter_dimension=0, tiled=True),
        lax.psum_scatter(totals[6], ("seq", "ctx"), scatter_dimension=0, tiled=True),
        lax.psum_scatter(totals[7], ("seq", "ctx"), scatter_dimension=0, tiled=True),
        lax.psum_scatter(totals[8], ("seq", "ctx"), scatter_dimension=0, tiled=True),
        lax.psum_scatter(totals[9], ("seq", "ctx"), scatter_dimension=0, tiled=True),
        lax.psum_scatter(totals[10], ("seq", "ctx"), scatter_dimension=0, tiled=True),
        lax.psum_scatter(totals[11], ("seq", "ctx"), scatter_dimension=0, tiled=True),
        lax.psum_scatter(totals[12], ("seq", "ctx"), scatter_dimension=0, tiled=True),
        lax.psum_scatter(totals[13], ("seq", "ctx"), scatter_dimension=0, tiled=True),
        lax.psum_scatter(totals[14], ("seq", "ctx"), scatter_dimension=0, tiled=True),
    )
    return (jnp.stack(results), jnp.stack(input_grads)) + tuple(owned)


AXES = ("seq", "ctx")
LOG2E = 1.4426950408889634
SCORE_UNIT = 0.125 * LOG2E
HIDDEN_SCORE = -1e30
VMEM_BYTES = 62 << 20
SLAB = 128
WEIGHT = 30


def place_of(index, me):
    mz, mc, my, mx = me
    bx, by, bc, bz = index & 1, (index >> 1) & 1, (index >> 2) & 1, index >> 3
    kx, ky, kz = bx ^ mx, by ^ my, bz ^ mz
    even = bc == 0
    first = jnp.where(even, kx, ky)
    second = jnp.where(even, ky, kx)
    return bc == mc, first, second, kz


def read_me(me_ref):
    return me_ref[0], me_ref[1], me_ref[2], me_ref[3]


def start_load(me, pieces, columns, target, rows, count, sem):
    def body(index, carry):
        own, first, second, kz = place_of(index, me)
        spot = target.at[pl.ds(pl.multiple_of(index * rows, 8), rows), :]
        for number, piece in enumerate(pieces):
            mine = own if number < 2 else jnp.logical_not(own)

            @pl.when(jnp.logical_and(mine, second == number % 2))
            def _(piece=piece):
                source = piece.at[first, kz]
                if columns is not None:
                    source = source.at[:, pl.ds(columns[0], columns[1])]
                pltpu.make_async_copy(source, spot, sem).start()

        return carry

    lax.fori_loop(0, count, body, 0)


def end_load(target, sem):
    pltpu.make_async_copy(target, target, sem).wait()


def store_blocks(me, value_ref, keep_ref, send_ref, first_block, count, rows, column, width):
    def body(step, carry):
        own, first, second, kz = place_of(first_block + step, me)
        value = value_ref[pl.ds(pl.multiple_of(step * rows, 8), rows), :].astype(jnp.bfloat16)

        @pl.when(own)
        def _():
            keep_ref[first, second, kz, :, pl.ds(column, width)] = value

        @pl.when(jnp.logical_not(own))
        def _():
            send_ref[first, second, kz, :, pl.ds(column, width)] = value

        return carry

    lax.fori_loop(0, count, body, 0)


def lanes_of(shape):
    return lax.broadcasted_iota(jnp.int32, shape, len(shape) - 1)


def nn(a, b):
    return jnp.dot(a, b, preferred_element_type=jnp.float32)


def nt(a, b):
    return lax.dot_general(a, b, (((1,), (1,)), ((), ())), preferred_element_type=jnp.float32)


def tn(a, b):
    return lax.dot_general(a, b, (((0,), (0,)), ((), ())), preferred_element_type=jnp.float32)


def row_sum(values):
    return jnp.sum(values, axis=0, keepdims=True)


def pack_weights_kernel(wq_ref, wk_ref, wv_ref, *rest):
    vectors, inner_ref, out_ref = rest[:8], rest[8], rest[9]
    rows, width = wq_ref.shape
    out_ref[:, 0:width] = wq_ref[...]
    out_ref[:, width : 2 * width] = wk_ref[...]
    out_ref[:, 2 * width : 3 * width] = wv_ref[...]
    share = inner_ref.shape[1]
    lines = [ref[...].astype(jnp.float32) for ref in vectors]
    lines = [jnp.concatenate([line, jnp.zeros((1, SLAB - rows), jnp.float32)], axis=1) for line in lines]
    last = jnp.concatenate(
        [inner_ref[...].astype(jnp.float32), jnp.zeros((1, SLAB - share), jnp.float32)], axis=1
    )
    slab = jnp.concatenate(lines + [last, jnp.zeros((rows - 9, SLAB), jnp.float32)], axis=0)
    out_ref[:, 3 * width : 3 * width + SLAB] = slab.astype(jnp.bfloat16)


def pack_rows_kernel(me_ref, hidden_ref, segment_ref, cot_ref, near_ref, far_ref):
    x = me_ref[3]
    quarter, width = hidden_ref.shape[1], hidden_ref.shape[2]
    for ref, pick in ((near_ref, x), (far_ref, 1 - x)):
        ref[0:quarter, :] = hidden_ref[pick]
        both = segment_ref[...].astype(jnp.float32)
        line = jnp.where(pick == 0, both[0:1, :], both[1:2, :]).astype(jnp.bfloat16)
        ref[quarter : quarter + 8, 0:quarter] = jnp.broadcast_to(line, (8, quarter))
        ref[quarter : quarter + 8, quarter:width] = jnp.zeros((8, width - quarter), jnp.bfloat16)
        ref[quarter + 8 : 2 * quarter + 8, :] = cot_ref[pick]


def settle_kernel(me_ref, near_ref, far_ref, out_ref):
    x = me_ref[3]
    out_ref[x] = near_ref[...].astype(out_ref.dtype)
    out_ref[1 - x] = far_ref[...].astype(out_ref.dtype)


def spread_lanes(block, share, offset, tiles, tile):
    lane = lanes_of(block.shape)
    moved = pltpu.roll(block, offset, axis=1) if offset else block
    tiles[tile] = jnp.where(
        jnp.logical_and(lane >= offset, lane < offset + share), moved, tiles[tile]
    )
    if offset + share > 128:
        tiles[tile + 1] = jnp.where(lane < offset + share - 128, moved, tiles[tile + 1])


def project_kernel(
    me_ref, r0, r1, r2, r3, p0, p1, p2, p3,
    q_ref, k_ref, v_ref, vec_ref, bias_ref, x_ref, segrow_ref, segcol_ref, w_ref, slab_ref, sem,
):
    me = read_me(me_ref)
    tokens, width = q_ref.shape
    blocks = 32
    rows = width // blocks
    start_load(me, (p0, p1, p2, p3), None, w_ref, rows, blocks, sem)
    quarter = tokens // 2
    for number, ref in enumerate((r0, r1, r2, r3)):
        span = pl.ds(number * quarter, quarter)
        x_ref[span, :] = ref[0:quarter, :]
        line = ref[quarter : quarter + 8, 0:quarter].astype(jnp.float32)
        segrow_ref[:, span] = line
        segcol_ref[span, :] = jnp.broadcast_to(line[0:1, :], (128, quarter)).T
    end_load(w_ref, sem)
    slab_ref[...] = w_ref[:, 3 * width : 3 * width + SLAB].astype(jnp.float32)
    tiles = [jnp.zeros((8, 128), jnp.float32) for _ in range(width // 128 + 1)]
    for index in range(blocks):
        start = rows * index
        spread_lanes(slab_ref[start : start + 8, :], rows, start % 128, tiles, start // 128)
    vectors = jnp.concatenate(tiles[: width // 128], axis=1)
    vec_ref[...] = vectors
    share = bias_ref.shape[1] // blocks
    tiles = [jnp.zeros((8, 128), jnp.float32) for _ in range(4)]
    for turn in range(4):
        lines = slab_ref[pl.ds(rows * turn + 8, 8, stride=4 * rows), :]
        spread_lanes(lines, share, share * turn % 128, tiles, share * turn // 128)
    for group in range(8):
        for tile in range(3):
            bias_ref[0:1, pl.ds(group * 384 + tile * 128, 128)] = tiles[tile][group : group + 1, :]
    b_query, b_value = vectors[0:1, :], vectors[1:2, :]
    q_ref[...] = (nn(x_ref[0:tokens, :], w_ref[:, 0:width]) + b_query).astype(jnp.bfloat16)

    @pl.loop(0, 2)
    def _(part):
        span = pl.ds(pl.multiple_of(part * tokens, tokens), tokens)
        k_ref[span, :] = nn(x_ref[span, :], w_ref[:, width : 2 * width]).astype(jnp.bfloat16)
        v_ref[span, :] = (nn(x_ref[span, :], w_ref[:, 2 * width : 3 * width]) + b_value).astype(
            jnp.bfloat16
        )


def attend_kernel(q_ref, k_ref, v_ref, segcol_ref, segrow_ref, mixed_ref, lse_ref, bias_ref):
    tokens = q_ref.shape[0]
    keys = k_ref.shape[0]
    tile = 256

    @pl.when(pl.program_id(0) == 0)
    def _():
        visible = segcol_ref[0:tokens, 0:1] == segrow_ref[0:1, :]
        bias_ref[...] = jnp.where(visible, 0.0, HIDDEN_SCORE)

    low_half = lanes_of((1, 128)) < 64
    key_rows = k_ref[...]
    value_rows = v_ref[...]
    one = jnp.ones((), jnp.bfloat16)
    zero = jnp.zeros((), jnp.bfloat16)
    for part in range(tokens // tile):
        span = pl.ds(part * tile, tile)
        query = q_ref[span, :]
        bias = bias_ref[span, :]
        outs, sums = [], []
        for head in range(2):
            mine = low_half if head == 0 else jnp.logical_not(low_half)
            scores = nt(jnp.where(mine, query, zero), key_rows) + bias
            top = jnp.max(scores, axis=-1, keepdims=True)
            weights = jnp.exp2((scores - top) * SCORE_UNIT).astype(jnp.bfloat16)
            product = nn(weights, jnp.where(mine, value_rows, one))
            total = product[:, 64:65] if head == 0 else product[:, 0:1]
            outs.append(product / total)
            sums.append(top * SCORE_UNIT + jnp.log2(total))
        mixed_ref[span, :] = jnp.where(low_half, outs[0], outs[1])
        lane = lanes_of((tile, 128))
        both = jnp.where(lane == 0, sums[0], jnp.where(lane == 1, sums[1], 0.0))
        lse_ref[0, :, span] = both.T[0:8, :]


def attend_back_kernel(
    q_ref, k_ref, v_ref, gm_ref, mixed_ref, lse_ref, segcol_ref, segrow_ref,
    dq_ref, dk_ref, dv_ref, bias_ref,
):
    tokens = q_ref.shape[0]
    keys = k_ref.shape[0]
    tile = 256

    @pl.when(pl.program_id(0) == 0)
    def _():
        visible = segcol_ref[:, 0:1] == segrow_ref[0:1, 0:tokens]
        bias_ref[...] = jnp.where(visible, 0.0, HIDDEN_SCORE)

    low_half = lanes_of((1, 128)) < 64
    zero = jnp.zeros((), jnp.bfloat16)
    query = q_ref[...]
    grad = gm_ref[...]
    product = (grad.astype(jnp.float32) * mixed_ref[...]).T
    row_dots = [row_sum(product[0:64, :]), row_sum(product[64:128, :])]
    masks = (low_half, jnp.logical_not(low_half))
    queries = [jnp.where(mine, query, zero) for mine in masks]
    grads = [jnp.where(mine, grad, zero) for mine in masks]
    def body(turn, grad_query):
        for half in range(2):
            span = pl.ds(pl.multiple_of((2 * turn + half) * tile, tile), tile)
            key_rows = k_ref[span, :]
            value_rows = v_ref[span, :]
            bias = bias_ref[span, :]
            grad_key = jnp.zeros((tile, 128), jnp.float32)
            grad_value = jnp.zeros((tile, 128), jnp.float32)
            for head in range(2):
                scores = nt(key_rows, queries[head])
                probs = jnp.exp2(scores * SCORE_UNIT + (bias - lse_ref[0, head : head + 1, :]))
                grad_probs = nt(value_rows, grads[head])
                grad_scores = (probs * (grad_probs - row_dots[head])).astype(jnp.bfloat16)
                grad_key = grad_key + nn(grad_scores, queries[head])
                grad_value = grad_value + nn(probs.astype(jnp.bfloat16), grads[head])
                grad_query = grad_query + tn(grad_scores, jnp.where(masks[head], key_rows, zero))
            dk_ref[span, :] = (grad_key * 0.125).astype(jnp.bfloat16)
            dv_ref[span, :] = grad_value.astype(jnp.bfloat16)
        return grad_query

    grad_query = lax.fori_loop(0, keys // tile // 2, body, jnp.zeros((tokens, 128), jnp.float32))
    dq_ref[...] = (grad_query * 0.125).astype(jnp.bfloat16)


def normalize(values):
    average = jnp.mean(values, axis=-1, keepdims=True)
    centered = values - average
    spread = jnp.mean(centered * centered, axis=-1, keepdims=True)
    inverse = lax.rsqrt(spread + epsilon)
    return centered * inverse, inverse


def normalize_back(grad, unit, inverse, gain):
    scaled = grad * gain
    plain = jnp.mean(scaled, axis=-1, keepdims=True)
    cross = jnp.mean(scaled * unit, axis=-1, keepdims=True)
    return inverse * (scaled - plain - unit * cross)


def feed_in_kernel(
    me_ref, mixed_a_ref, mixed_b_ref, x_ref, vec_ref, bias_ref, a0, a1, a2, a3,
    low_ref, act_ref, slope_ref, unit_ref, inverse_ref, rest_ref, wo_ref, wi_ref, sem_o, sem_i,
):
    me = read_me(me_ref)
    tokens, width = low_ref.shape
    inner = wi_ref.shape[1]
    blocks = 32
    start_load(me, (a0, a1, a2, a3), (0, width), wo_ref, width // blocks, blocks, sem_o)
    start_load(me, (a0, a1, a2, a3), (width, inner), wi_ref, width // blocks, blocks, sem_i)
    b_output, attn_gain, attn_shift = vec_ref[2:3, :], vec_ref[3:4, :], vec_ref[4:5, :]
    b_outer = vec_ref[5:6, :]
    end_load(wo_ref, sem_o)
    part = mixed_a_ref.shape[1]
    branch = b_output + nn(mixed_a_ref[...].astype(jnp.bfloat16), wo_ref[0:part, :])
    branch = branch + nn(mixed_b_ref[...].astype(jnp.bfloat16), wo_ref[part:width, :])
    unit_one, inverse_one = normalize(x_ref[0:tokens, :].astype(jnp.float32) + branch)
    normed = unit_one * attn_gain + attn_shift
    unit_ref[...] = unit_one
    inverse_ref[...] = jnp.broadcast_to(inverse_one, inverse_ref.shape)
    low_ref[...] = normed.astype(jnp.bfloat16)
    rest_ref[...] = normed + b_outer
    end_load(wi_ref, sem_i)
    step = 512

    @pl.loop(0, inner // step)
    def _(turn):
        span = pl.ds(pl.multiple_of(turn * step, step), step)
        pre_act = nn(low_ref[...], wi_ref[:, span]) + bias_ref[0:1, span]
        normal_cdf = 0.5 * (1.0 + lax.erf(pre_act * root_half))
        density = jnp.exp(-0.5 * pre_act * pre_act) * inv_root_tau
        act_ref[:, span] = (pre_act * normal_cdf).astype(jnp.bfloat16)
        slope_ref[:, span] = (normal_cdf + pre_act * density).astype(jnp.bfloat16)


def feed_out_kernel(
    me_ref, act_ref, rest_ref, cot_near_ref, cot_far_ref, vec_ref, b0, b1, b2, b3,
    near_ref, far_ref, second_ref, outer_ref, sums_ref, keep_ref, send_ref,
    wu_ref, grad_ref, sem_u,
):
    me = read_me(me_ref)
    tokens, width = rest_ref.shape
    inner = act_ref.shape[1]
    blocks = 32
    rows = inner // blocks
    quarter = tokens // 2
    start_load(me, (b0, b1, b2, b3), None, wu_ref, rows, blocks, sem_u)
    ffn_gain, ffn_shift = vec_ref[6:7, :], vec_ref[7:8, :]
    end_load(wu_ref, sem_u)

    @pl.loop(0, 2)
    def _(part):
        span = pl.ds(pl.multiple_of(part * quarter, quarter), quarter)
        second_ref[span, :] = rest_ref[span, :] + nn(act_ref[span, :], wu_ref[...])

    sums = [jnp.zeros((1, width), jnp.float32) for _ in range(3)]
    for part in range(2):
        span = pl.ds(part * quarter, quarter)
        unit_two, inverse_two = normalize(second_ref[span, :])
        out_ref, packed_ref = ((near_ref, cot_near_ref), (far_ref, cot_far_ref))[part]
        out_ref[...] = (unit_two * ffn_gain + ffn_shift).astype(jnp.bfloat16)
        tangent = packed_ref[quarter + 8 : tokens + 8, :].astype(jnp.float32)
        second = normalize_back(tangent, unit_two, inverse_two, ffn_gain)
        second_ref[span, :] = second
        outer = second.astype(jnp.bfloat16)
        outer_ref[span, :] = outer
        sums[0] = sums[0] + row_sum(outer.astype(jnp.float32))
        sums[1] = sums[1] + row_sum(tangent * unit_two)
        sums[2] = sums[2] + row_sum(tangent)
    sums_ref[...] = jnp.concatenate(sums + [jnp.zeros((5, width), jnp.float32)], axis=0)
    half = width // 2

    @pl.loop(0, inner // half)
    def _(turn):
        cols = pl.ds(pl.multiple_of(turn * half, half), half)
        grad_ref[...] = tn(act_ref[:, cols], outer_ref[...])
        store_blocks(
            me, grad_ref, keep_ref, send_ref, turn * (half // rows), half // rows, rows, 0, width
        )


def slope_kernel(
    me_ref, slope_ref, outer_ref, b0, b1, b2, b3, pre_ref, bsum_ref, wu_ref, sem_u
):
    me = read_me(me_ref)
    inner = slope_ref.shape[1]
    blocks = 32
    start_load(me, (b0, b1, b2, b3), None, wu_ref, inner // blocks, blocks, sem_u)
    end_load(wu_ref, sem_u)
    step = 512

    @pl.loop(0, inner // step)
    def _(turn):
        span = pl.ds(pl.multiple_of(turn * step, step), step)
        grad_act = nt(outer_ref[...], wu_ref[span, :])
        grad_pre = (grad_act * slope_ref[:, span].astype(jnp.float32)).astype(jnp.bfloat16)
        bsum_ref[0:1, span] = row_sum(grad_pre.astype(jnp.float32))
        pre_ref[:, span] = grad_pre


def feed_back_kernel(
    me_ref, pre_ref, second_ref, low_ref, unit_ref, inverse_ref, mixed_a_ref, mixed_b_ref, vec_ref,
    a0, a1, a2, a3,
    mid_ref, gm_ref, sums_ref, keep_ref, send_ref,
    wo_ref, wi_ref, grad_ref, sem_o, sem_i,
):
    me = read_me(me_ref)
    tokens, width = second_ref.shape
    inner = wi_ref.shape[1]
    blocks = 32
    rows = width // blocks
    start_load(me, (a0, a1, a2, a3), (width, inner), wi_ref, rows, blocks, sem_i)
    start_load(me, (a0, a1, a2, a3), (0, width), wo_ref, rows, blocks, sem_o)
    step = 512

    @pl.loop(0, inner // step)
    def _(turn):
        first = pl.multiple_of(turn * step, step)
        grad_ref[:, 0:step] = tn(low_ref[...], pre_ref[:, pl.ds(first, step)])
        store_blocks(
            me, grad_ref.at[:, 0:step], keep_ref, send_ref, 0, blocks, rows,
            pl.multiple_of(width + first, 128), step,
        )

    end_load(wi_ref, sem_i)

    @pl.loop(0, 2)
    def _(part):
        span = pl.ds(pl.multiple_of(part * (tokens // 2), tokens // 2), tokens // 2)
        mid_ref[span, :] = second_ref[span, :] + nt(pre_ref[span, :], wi_ref[...])

    end_load(wo_ref, sem_o)
    attn_gain = vec_ref[3:4, :]
    grad_normed = mid_ref[...]
    unit = unit_ref[...]
    mid = normalize_back(grad_normed, unit, inverse_ref[:, 0:1], attn_gain)
    mid_ref[...] = mid
    branch = mid.astype(jnp.bfloat16)
    sums_ref[...] = jnp.zeros(sums_ref.shape, jnp.float32)
    sums_ref[0:1, :] = row_sum(branch.astype(jnp.float32))
    sums_ref[1:2, :] = row_sum(grad_normed * unit)
    sums_ref[2:3, :] = row_sum(grad_normed)
    gm_ref[...] = nt(branch, wo_ref[...]).astype(jnp.bfloat16)
    part = mixed_a_ref.shape[1]
    grad_ref[0:part, :] = tn(mixed_a_ref[...].astype(jnp.bfloat16), branch)
    grad_ref[part:width, :] = tn(mixed_b_ref[...].astype(jnp.bfloat16), branch)
    store_blocks(me, grad_ref, keep_ref, send_ref, 0, blocks, rows, 0, width)


def weight_kernel(
    me_ref, x_ref, dqa_ref, dka_ref, dva_ref, dqb_ref, dkb_ref, dvb_ref,
    sums_two_ref, sums_one_ref, bsum_ref, keep_ref, send_ref, grad_ref, slab_ref,
):
    me = read_me(me_ref)
    tokens, half = dqa_ref.shape
    width = 2 * half
    blocks = 32
    rows = width // blocks
    refs = (dqa_ref, dqb_ref, dka_ref, dkb_ref, dva_ref, dvb_ref)
    for number, ref in enumerate(refs):
        grad_ref[...] = tn(x_ref[0 : ref.shape[0], :], ref[...])
        store_blocks(me, grad_ref, keep_ref, send_ref, 0, blocks, rows, number * half, half)

    def sums(first, second):
        return jnp.concatenate(
            [row_sum(first[...].astype(jnp.float32)), row_sum(second[...].astype(jnp.float32))],
            axis=1,
        )

    vectors = jnp.concatenate(
        [
            sums(dqa_ref, dqb_ref),
            sums(dva_ref, dvb_ref),
            sums_one_ref[0:3, :],
            sums_two_ref[0:3, :],
        ],
        axis=0,
    )
    share = bsum_ref.shape[1] // blocks
    lane = lanes_of((8, 128))
    slab_ref[...] = jnp.zeros(slab_ref.shape, jnp.float32)
    for index in range(blocks):
        tile, offset = rows * index // 128, rows * index % 128
        piece = vectors[:, tile * 128 : tile * 128 + 128]
        if offset + rows > 128:
            piece = jnp.where(
                lane >= offset, piece, vectors[:, tile * 128 + 128 : tile * 128 + 256]
            )
        moved = pltpu.roll(piece, (128 - offset) % 128, axis=1) if offset else piece
        slab_ref[rows * index : rows * index + 8, :] = jnp.where(lane < rows, moved, 0.0)
    groups = jnp.concatenate([bsum_ref[0:1, pl.ds(384 * g, 384)] for g in range(8)], axis=0)
    for turn in range(4):
        tile, offset = share * turn // 128, share * turn % 128
        piece = groups[:, tile * 128 : tile * 128 + 128]
        if offset + share > 128:
            piece = jnp.where(lane >= offset, piece, groups[:, tile * 128 + 128 : tile * 128 + 256])
        moved = pltpu.roll(piece, (128 - offset) % 128, axis=1) if offset else piece
        slab_ref[pl.ds(rows * turn + 8, 8, stride=4 * rows), :] = jnp.where(lane < share, moved, 0.0)
    store_blocks(me, slab_ref, keep_ref, send_ref, 0, blocks, rows, 3 * width, SLAB)


def input_kernel(
    me_ref, mid_ref, dqa_ref, dka_ref, dva_ref, dqb_ref, dkb_ref, dvb_ref, other_ref,
    p0, p1, p2, p3, near_ref, far_ref, w_ref, sem,
):
    me = read_me(me_ref)
    tokens, width = mid_ref.shape
    half = width // 2
    blocks = 32
    start_load(me, (p0, p1, p2, p3), (0, 3 * width), w_ref, width // blocks, blocks, sem)
    own = []
    for number, ref in enumerate((dka_ref, dva_ref, dkb_ref, dvb_ref)):
        theirs = other_ref[:, number * half : (number + 1) * half].astype(jnp.float32)
        own.append((ref[0:tokens, :].astype(jnp.float32) + theirs).astype(jnp.bfloat16))
    end_load(w_ref, sem)
    total = mid_ref[...]
    for number, value in enumerate((dqa_ref[...], dqb_ref[...], own[0], own[2], own[1], own[3])):
        total = total + nt(value, w_ref[:, number * half : (number + 1) * half])
    low = total.astype(jnp.bfloat16)
    near_ref[...] = low[: tokens // 2]
    far_ref[...] = low[tokens // 2 :]


def shape_of(shape, dtype):
    return jax.ShapeDtypeStruct(shape, dtype)


def call(kernel, name, out_shape, kinds, scratch, flops, moved):
    spaces = {"s": pltpu.SMEM, "v": pltpu.VMEM, "a": pl.ANY}
    return pl.pallas_call(
        kernel,
        name=name,
        out_shape=out_shape,
        in_specs=[pl.BlockSpec(memory_space=spaces[kind]) for kind in kinds],
        scratch_shapes=scratch,
        compiler_params=pltpu.CompilerParams(vmem_limit_bytes=VMEM_BYTES),
        cost_estimate=pl.CostEstimate(
            flops=WEIGHT * flops, bytes_accessed=WEIGHT * moved, transcendentals=0
        ),
    )


def tie(*values):
    return lax.optimization_barrier(values)


def fast_device(depth, hidden, segment, cotangent, *weights):
    (
        w_query, b_query, w_key, w_value, b_value, w_output, b_output, attn_gain, attn_shift,
        w_inner, b_inner, w_outer, b_outer, ffn_gain, ffn_shift,
    ) = weights
    bf16, f32 = jnp.bfloat16, jnp.float32
    quarter, width = hidden.shape[1], hidden.shape[2]
    tokens = 2 * quarter
    keys = 2 * tokens
    rows = w_query.shape[0]
    inner = w_inner.shape[1]
    inner_rows = w_outer.shape[0]
    seq_index, ctx_index = lax.axis_index("seq"), lax.axis_index("ctx")
    me = jnp.stack([seq_index >> 1, seq_index & 1, ctx_index >> 1, ctx_index & 1]).astype(jnp.int32)

    def table(move):
        pairs = []
        for bz in range(depth):
            for bc in range(2):
                for by in range(2):
                    for bx in range(2):
                        tz, tc, ty, tx = move(bz, bc, by, bx)
                        pairs.append(
                            (((bz * 2 + bc) * 2 + by) * 2 + bx, ((tz * 2 + tc) * 2 + ty) * 2 + tx)
                        )
        return pairs

    along_z = [table(lambda a, b, d, e, k=k: (a ^ k, b, d, e)) for k in range(1, depth)]
    plane_one = table(lambda a, b, d, e: (a, b, d, 1 - e) if b == 0 else (a, b, 1 - d, e))
    plane_two = table(lambda a, b, d, e: (a, b, 1 - d, e) if b == 0 else (a, b, d, 1 - e))
    partner = table(lambda a, b, d, e: (a, 1 - b, d, e))
    home_near = table(lambda a, b, d, e: (a, d, b, e))
    home_far = table(lambda a, b, d, e: (a, d, b, 1 - e))

    def hop(value, pairs):
        return lax.ppermute(value, AXES, pairs)

    def levels_of(value):
        return jnp.stack([value] + [hop(value, pairs) for pairs in along_z])

    sem = pltpu.SemaphoreType.DMA
    flat = 2 * tokens * width
    slabbed = 3 * width + SLAB

    vectors_in = (
        b_query, b_value, b_output, attn_gain, attn_shift, b_outer, ffn_gain, ffn_shift, b_inner,
    )
    packed = call(
        pack_weights_kernel, "pack_weights", shape_of((rows, slabbed), bf16), "v" * 12, [], 1, 1 << 20
    )(w_query, w_key, w_value, *[vector[None, :] for vector in vectors_in])
    levels_one = levels_of(packed)

    packed_row = shape_of((tokens + 8, width), bf16)
    near, far = call(
        pack_rows_kernel, "pack_rows", (packed_row, packed_row), "svvv", [], 1, 1 << 20
    )(me, hidden, segment, cotangent)
    near, far = hop(near, home_near), hop(far, home_far)
    plain_row = shape_of((quarter, width), bf16)

    second_in = jnp.concatenate([w_output, w_inner], axis=1)
    levels_one, second_in = tie(levels_one, second_in)
    half_one = jnp.stack([levels_one, hop(levels_one, plane_one)])
    levels_two = levels_of(second_in)

    half_one, near, far = tie(half_one, near, far)
    other_one = hop(half_one, plane_two)
    half_one_p = hop(half_one, partner)
    near_other, far_other = hop(near, partner), hop(far, partner)
    other_one, levels_two, third_in = tie(other_one, levels_two, w_outer)
    other_one_p = hop(other_one, partner)
    got_two = hop(levels_two, plane_one)
    levels_three = levels_of(third_in)
    group_one = (half_one, other_one, half_one_p, other_one_p)

    q, k, v, vectors, bias, x_all, segrow, segcol = call(
        project_kernel,
        "project",
        (
            shape_of((tokens, width), bf16),
            shape_of((keys, width), bf16),
            shape_of((keys, width), bf16),
            shape_of((8, width), f32),
            shape_of((1, inner), f32),
            shape_of((keys, width), bf16),
            shape_of((8, keys), f32),
            shape_of((keys, 128), f32),
        ),
        "svvvvaaaa",
        [pltpu.VMEM((width, slabbed), bf16), pltpu.VMEM((width, SLAB), f32), sem],
        5 * flat * width,
        10 << 20,
    )(me, near, far, near_other, far_other, *group_one)

    half_two = jnp.stack([levels_two, got_two])
    q, half_two, levels_three = tie(q, half_two, levels_three)
    other_two = hop(half_two, plane_two)
    half_two_p = hop(half_two, partner)
    got_three = hop(levels_three, plane_one)

    parts = 2
    pairs_now = width // 128 // parts
    params = pltpu.CompilerParams(vmem_limit_bytes=VMEM_BYTES)

    def attend(part):
        def column(count):
            return pl.BlockSpec((count, 128), lambda i: (0, i + part * pairs_now))

        def column_out(count):
            return pl.BlockSpec((count, 128), lambda i: (0, i))

        def whole(shape):
            return pl.BlockSpec(shape, lambda i: (0, 0))

        return pl.pallas_call(
            attend_kernel,
            name="attend",
            grid=(pairs_now,),
            out_shape=(
                shape_of((tokens, pairs_now * 128), f32),
                shape_of((pairs_now, 8, tokens), f32),
            ),
            in_specs=[
                column(tokens), column(keys), column(keys), whole((keys, 128)), whole((8, keys)),
            ],
            out_specs=(column_out(tokens), pl.BlockSpec((1, 8, tokens), lambda i: (i, 0, 0))),
            scratch_shapes=[pltpu.VMEM((tokens, keys), f32)],
            compiler_params=params,
            cost_estimate=pl.CostEstimate(
                flops=WEIGHT * 8 * tokens * keys * width // parts, bytes_accessed=WEIGHT << 22, transcendentals=0
            ),
        )

    mixed_a, lse_a = attend(0)(q, k, v, segcol, segrow)
    half_three = jnp.stack([levels_three, got_three])
    q_b, mixed_a = tie(q, mixed_a)
    mixed_b, lse_b = attend(1)(q_b, k, v, segcol, segrow)
    mixed_b, other_two, half_three = tie(mixed_b, other_two, half_three)
    other_two_p = hop(other_two, partner)
    group_two = (half_two, other_two, half_two_p, other_two_p)
    other_three = hop(half_three, plane_two)
    half_three_p = hop(half_three, partner)

    low, act, slope, unit, inverse, rest = call(
        feed_in_kernel,
        "feed_in",
        (
            shape_of((tokens, width), bf16),
            shape_of((tokens, inner), bf16),
            shape_of((tokens, inner), bf16),
            shape_of((tokens, width), f32),
            shape_of((tokens, 128), f32),
            shape_of((tokens, width), f32),
        ),
        "svvvvvaaaa",
        [pltpu.VMEM((width, width), bf16), pltpu.VMEM((width, inner), bf16), sem, sem],
        flat * (width + inner),
        20 << 20,
    )(me, mixed_a, mixed_b, x_all, vectors, bias, *group_two)

    act, other_three = tie(act, other_three)
    other_three_p = hop(other_three, partner)
    group_three = (half_three, other_three, half_three_p, other_three_p)
    near_out, far_out, second, outer, sums_two, keep_three, send_three = call(
        feed_out_kernel,
        "feed_out",
        (
            plain_row,
            plain_row,
            shape_of((tokens, width), f32),
            shape_of((tokens, width), bf16),
            shape_of((8, width), f32),
            shape_of((2, 2, depth, inner_rows, width), bf16),
            shape_of((2, 2, depth, inner_rows, width), bf16),
        ),
        "svvvvvaaaa",
        [pltpu.VMEM((inner, width), bf16), pltpu.VMEM((width // 2, width), f32), sem],
        2 * flat * inner,
        20 << 20,
    )(me, act, rest, near, far, vectors, *group_three)

    got = hop(send_three, partner)
    near_out, far_out = hop(near_out, home_near), hop(far_out, home_far)

    grad_pre, bias_sums = call(
        slope_kernel,
        "slope",
        (shape_of((tokens, inner), bf16), shape_of((1, inner), f32)),
        "svvaaaa",
        [pltpu.VMEM((inner, width), bf16), sem],
        flat * inner,
        16 << 20,
    )(me, slope, outer, *group_three)

    def first_sum(keep, got):
        return keep[1] + got[1], keep[0] + got[0]

    def second_sum(kept, got):
        return kept[1] + got[1], kept[0] + got[0]

    def last_sum(levels, arrived):
        total = levels[0].astype(f32)
        for value in arrived:
            total = total + value.astype(f32)
        return total

    def climb(levels):
        return [hop(levels[k + 1], pairs) for k, pairs in enumerate(along_z)]

    three_send, three_kept = first_sum(keep_three, got)
    grad_pre, three_send, three_kept, near_out, far_out = tie(
        grad_pre, three_send, three_kept, near_out, far_out
    )
    three_got = hop(three_send, plane_one)

    mid, grad_mixed, sums_one, keep_two, send_two = call(
        feed_back_kernel,
        "feed_back",
        (
            shape_of((tokens, width), f32),
            shape_of((tokens, width), bf16),
            shape_of((8, width), f32),
            shape_of((2, 2, depth, rows, width + inner), bf16),
            shape_of((2, 2, depth, rows, width + inner), bf16),
        ),
        "svvvvvvvvaaaa",
        [
            pltpu.VMEM((width, width), bf16),
            pltpu.VMEM((width, inner), bf16),
            pltpu.VMEM((width, width), f32),
            sem, sem,
        ],
        flat * (2 * inner + 2 * width),
        30 << 20,
    )(me, grad_pre, second, low, unit, inverse, mixed_a, mixed_b, vectors, *group_two)

    two_got = hop(send_two, partner)
    three_send, three_kept = three_kept[1] + three_got[1], three_kept[0] + three_got[0]
    grad_mixed, three_send, three_kept = tie(grad_mixed, three_send, three_kept)
    three_got = hop(three_send, plane_two)

    def attend_back(part):
        def column(count):
            return pl.BlockSpec((count, 128), lambda i: (0, i + part * pairs_now))

        def column_out(count):
            return pl.BlockSpec((count, 128), lambda i: (0, i))

        def whole(shape):
            return pl.BlockSpec(shape, lambda i: (0, 0))

        return pl.pallas_call(
            attend_back_kernel,
            name="attend_back",
            grid=(pairs_now,),
            out_shape=(
                shape_of((tokens, pairs_now * 128), bf16),
                shape_of((keys, pairs_now * 128), bf16),
                shape_of((keys, pairs_now * 128), bf16),
            ),
            in_specs=[
                column(tokens), column(keys), column(keys), column(tokens), column_out(tokens),
                pl.BlockSpec((1, 8, tokens), lambda i: (i, 0, 0)),
                whole((keys, 128)), whole((8, keys)),
            ],
            out_specs=(column_out(tokens), column_out(keys), column_out(keys)),
            scratch_shapes=[pltpu.VMEM((keys, tokens), f32)],
            compiler_params=params,
            cost_estimate=pl.CostEstimate(
                flops=WEIGHT * 20 * tokens * keys * width // parts, bytes_accessed=WEIGHT << 22, transcendentals=0
            ),
        )

    back_a = attend_back(0)(q, k, v, grad_mixed, mixed_a, lse_a, segcol, segrow)

    three_levels = three_kept + three_got
    two_send, two_kept = first_sum(keep_two, two_got)
    back_a, three_levels, two_send, two_kept, grad_mixed_b = tie(
        back_a, three_levels, two_send, two_kept, grad_mixed
    )
    three_climb = climb(three_levels)
    two_got = hop(two_send, plane_one)

    back_b = attend_back(1)(q, k, v, grad_mixed_b, mixed_b, lse_b, segcol, segrow)

    total_three = last_sum(three_levels, three_climb)
    two_send, two_kept = second_sum(two_kept, two_got)
    back_b, total_three, two_send, two_kept = tie(back_b, total_three, two_send, two_kept)
    two_got = hop(two_send, plane_two)
    from_partner = hop(
        jnp.concatenate([value[tokens:] for value in back_a[1:] + back_b[1:]], axis=1), partner
    )

    keep_one, send_one = call(
        weight_kernel,
        "weight",
        (
            shape_of((2, 2, depth, rows, slabbed), bf16),
            shape_of((2, 2, depth, rows, slabbed), bf16),
        ),
        "svvvvvvvvvv",
        [pltpu.VMEM((width, width // 2), f32), pltpu.VMEM((width, SLAB), f32)],
        5 * flat * width,
        12 << 20,
    )(me, x_all, *back_a, *back_b, sums_two, sums_one, bias_sums)

    one_got = hop(send_one, partner)
    keep_one, two_levels = tie(keep_one, two_kept + two_got)
    two_climb = climb(two_levels)
    one_send, one_kept = first_sum(keep_one, one_got)
    mid, one_send, one_kept = tie(mid, one_send, one_kept)
    one_got = hop(one_send, plane_one)

    near_in, far_in = call(
        input_kernel,
        "input",
        (plain_row, plain_row),
        "svvvvvvvvaaaa",
        [pltpu.VMEM((width, 3 * width), bf16), sem],
        3 * flat * width,
        12 << 20,
    )(me, mid, *back_a, *back_b, from_partner, *group_one)

    one_got, near_in, far_in = tie(one_got, near_in, far_in)
    one_send, one_kept = second_sum(one_kept, one_got)
    one_got = hop(one_send, plane_two)
    total_two = last_sum(two_levels, two_climb)
    one_levels = one_kept + one_got
    one_levels, near_in, far_in, total_two = tie(one_levels, near_in, far_in, total_two)
    near_in, far_in = hop(near_in, home_near), hop(far_in, home_far)
    one_climb = climb(one_levels)

    def settle(first, second, dtype):
        return call(
            settle_kernel, "settle", shape_of((2, quarter, width), dtype), "svv", [], 1, 2 << 20
        )(me, first, second)

    result = settle(near_out, far_out, bf16)
    grad_input = settle(near_in, far_in, f32)
    total_one = last_sum(one_levels, one_climb)
    vector = [total_one[j, 3 * width : 3 * width + rows] for j in range(8)]
    grad_b_inner = total_one[8, 3 * width : 3 * width + inner_rows]
    return (
        result,
        grad_input,
        total_one[:, :width],
        vector[0],
        total_one[:, width : 2 * width],
        total_one[:, 2 * width : 3 * width],
        vector[1],
        total_two[:, :width],
        vector[2],
        vector[3],
        vector[4],
        total_two[:, width:],
        grad_b_inner,
        total_three,
        vector[5],
        vector[6],
        vector[7],
    )


def takes_fast(mesh):
    seq, ctx = mesh.shape["seq"], mesh.shape["ctx"]
    return ctx == 4 and seq == 8


def solution(mesh):
    return jax.shard_map(
        functools.partial(fast_device, mesh.shape["seq"] // 2) if takes_fast(mesh) else on_device,
        mesh=mesh,
        in_specs=(
            P("seq", "ctx", None),
            P("seq", "ctx"),
            P("seq", "ctx", None),
            P(("seq", "ctx"), None),
            P(("seq", "ctx")),
            P(("seq", "ctx"), None),
            P(("seq", "ctx"), None),
            P(("seq", "ctx")),
            P(("seq", "ctx"), None),
            P(("seq", "ctx")),
            P(("seq", "ctx")),
            P(("seq", "ctx")),
            P(("seq", "ctx"), None),
            P(("seq", "ctx")),
            P(("seq", "ctx"), None),
            P(("seq", "ctx")),
            P(("seq", "ctx")),
            P(("seq", "ctx")),
        ),
        out_specs=(
            P("seq", "ctx", None),
            P("seq", "ctx", None),
            P(("seq", "ctx"), None),
            P(("seq", "ctx")),
            P(("seq", "ctx"), None),
            P(("seq", "ctx"), None),
            P(("seq", "ctx")),
            P(("seq", "ctx"), None),
            P(("seq", "ctx")),
            P(("seq", "ctx")),
            P(("seq", "ctx")),
            P(("seq", "ctx"), None),
            P(("seq", "ctx")),
            P(("seq", "ctx"), None),
            P(("seq", "ctx")),
            P(("seq", "ctx")),
            P(("seq", "ctx")),
        ),
        check_vma=False,
    )
```

```python
import functools

import jax
import jax.numpy as jnp
from jax import lax
from jax.experimental import pallas as pl
from jax.experimental.pallas import tpu as pltpu
from jax.sharding import PartitionSpec as P

H = 12
DH = 64


epsilon = 1e-06
root_half = 0.7071067811865476
inv_root_tau = 0.3989422804014327


def matmul(left_side, right_side):
    return jnp.dot(left_side, right_side, preferred_element_type=jnp.float32)


def outer_dot(left_side, right_side):
    return lax.dot_general(
        left_side, right_side, (((0,), (0,)), ((), ())), preferred_element_type=jnp.float32
    )


def back_dot(left_side, right_side):
    return lax.dot_general(
        left_side, right_side, (((1,), (1,)), ((), ())), preferred_element_type=jnp.float32
    )


def forward_norm(values, gain_row, shift_row):
    average = jnp.mean(values, axis=-1, keepdims=True)
    centered = values - average
    spread = jnp.mean(centered * centered, axis=-1, keepdims=True)
    inv_scale = lax.rsqrt(spread + epsilon)
    unit_rows = centered * inv_scale
    return (unit_rows * gain_row + shift_row, unit_rows, inv_scale)


def backward_norm(grad_rows, unit_rows, inv_scale, gain_row):
    scaled = grad_rows * gain_row
    plain_mean = jnp.mean(scaled, axis=-1, keepdims=True)
    cross_mean = jnp.mean(scaled * unit_rows, axis=-1, keepdims=True)
    grad_values = inv_scale * (scaled - plain_mean - unit_rows * cross_mean)
    return (grad_values, jnp.sum(grad_rows * unit_rows, axis=0), jnp.sum(grad_rows, axis=0))


def as_float(weights):
    return tuple((item.astype(jnp.float32) if item.ndim == 1 else item for item in weights))


def forward_pass(token_rows, seg_ids, weights):
    (
        w_query,
        b_query,
        w_key,
        w_value,
        b_value,
        w_output,
        b_output,
        attn_gain,
        attn_shift,
        w_inner,
        b_inner,
        w_outer,
        b_outer,
        ffn_gain,
        ffn_shift,
    ) = as_float(weights)
    tokens = token_rows.shape[0]
    model_width = token_rows.shape[1]
    queries = (matmul(token_rows, w_query) + b_query).astype(jnp.bfloat16)
    key_rows = matmul(token_rows, w_key).astype(jnp.bfloat16)
    value_rows = (matmul(token_rows, w_value) + b_value).astype(jnp.bfloat16)
    seg_low = seg_ids.astype(jnp.bfloat16)
    query_heads = queries.reshape(tokens, H, DH)
    piece_keys = lax.all_gather(key_rows, "ctx", axis=0, tiled=True)
    piece_values = lax.all_gather(value_rows, "ctx", axis=0, tiled=True)
    piece_seg = lax.all_gather(seg_low, "ctx", axis=0, tiled=True)
    piece_len = piece_keys.shape[0]
    row_max = jnp.full((H, tokens), -1e30, jnp.float32)
    weighted = jnp.zeros((tokens, H, DH), jnp.float32)
    scores = (
        jnp.einsum(
            "qhd,khd->hqk",
            query_heads,
            piece_keys.reshape(piece_len, H, DH),
            preferred_element_type=jnp.float32,
        )
        * 0.125
    )
    visible = (seg_low[:, None] == piece_seg[None, :])[None]
    masked = jnp.where(visible, scores, -1e30)
    new_max = jnp.maximum(row_max, jnp.max(masked, axis=-1))
    weights_now = jnp.where(visible, jnp.exp(masked - new_max[:, :, None]), 0.0)
    rescale = jnp.exp(row_max - new_max)
    row_sum = jnp.sum(weights_now, axis=-1)
    added = jnp.einsum(
        "hqk,khd->qhd",
        weights_now.astype(jnp.bfloat16),
        piece_values.reshape(piece_len, H, DH),
        preferred_element_type=jnp.float32,
    )
    weighted = rescale.T[:, :, None] * weighted + added
    row_max, row_sum, weighted = (new_max, row_sum, weighted)
    mixed_full = (weighted / row_sum.T[:, :, None]).reshape(tokens, model_width)
    log_sum = row_max + jnp.log(row_sum)
    mixed = mixed_full.astype(jnp.bfloat16)
    branch = matmul(mixed, w_output) + b_output
    normed, unit_one, inv_one = forward_norm(
        token_rows.astype(jnp.float32) + branch, attn_gain, attn_shift
    )
    normed_low = normed.astype(jnp.bfloat16)
    pre_act = matmul(normed_low, w_inner) + b_inner
    activated = jax.nn.gelu(pre_act, approximate=False).astype(jnp.bfloat16)
    outer_sum = matmul(activated, w_outer) + b_outer
    result, unit_two, inv_two = forward_norm(normed + outer_sum, ffn_gain, ffn_shift)
    kept = (
        token_rows,
        seg_low,
        queries,
        key_rows,
        value_rows,
        mixed_full,
        mixed,
        log_sum,
        unit_one,
        inv_one,
        normed_low,
        pre_act,
        activated,
        unit_two,
        inv_two,
    )
    return (kept, result.astype(jnp.bfloat16))


def backward_pass(tangent, kept, weights):
    (
        w_query,
        b_query,
        w_key,
        w_value,
        b_value,
        w_output,
        b_output,
        attn_gain,
        attn_shift,
        w_inner,
        b_inner,
        w_outer,
        b_outer,
        ffn_gain,
        ffn_shift,
    ) = as_float(weights)
    (
        token_rows,
        seg_low,
        queries,
        key_rows,
        value_rows,
        mixed_full,
        mixed,
        log_sum,
        unit_one,
        inv_one,
        normed_low,
        pre_act,
        activated,
        unit_two,
        inv_two,
    ) = kept
    tokens = token_rows.shape[0]
    model_width = token_rows.shape[1]
    grad_second, grad_ffn_gain, grad_ffn_shift = backward_norm(
        tangent.astype(jnp.float32), unit_two, inv_two, ffn_gain
    )
    grad_outer = grad_second.astype(jnp.bfloat16)
    grad_b_outer = jnp.sum(grad_outer.astype(jnp.float32), axis=0)
    grad_w_outer = outer_dot(activated, grad_outer)
    grad_act = back_dot(grad_outer, w_outer)
    normal_cdf = 0.5 * (1.0 + lax.erf(pre_act * root_half))
    density = jnp.exp(-0.5 * pre_act * pre_act) * inv_root_tau
    grad_pre = (grad_act * (normal_cdf + pre_act * density)).astype(jnp.bfloat16)
    grad_b_inner = jnp.sum(grad_pre.astype(jnp.float32), axis=0)
    grad_w_inner = outer_dot(normed_low, grad_pre)
    grad_normed = grad_second + back_dot(grad_pre, w_inner)
    grad_mid, grad_attn_gain, grad_attn_shift = backward_norm(
        grad_normed, unit_one, inv_one, attn_gain
    )
    grad_branch = grad_mid.astype(jnp.bfloat16)
    grad_b_output = jnp.sum(grad_branch.astype(jnp.float32), axis=0)
    grad_w_output = outer_dot(mixed, grad_branch)
    grad_mixed = back_dot(grad_branch, w_output).astype(jnp.bfloat16)
    mixed_heads = grad_mixed.reshape(tokens, H, DH)
    query_heads = queries.reshape(tokens, H, DH)
    row_dot = jnp.sum(
        grad_mixed.astype(jnp.float32).reshape(tokens, H, DH) * mixed_full.reshape(tokens, H, DH),
        axis=-1,
    ).T
    whole_keys, whole_values, whole_seg = (
        lax.all_gather(key_rows, "ctx", axis=0, tiled=True),
        lax.all_gather(value_rows, "ctx", axis=0, tiled=True),
        lax.all_gather(seg_low, "ctx", axis=0, tiled=True),
    )
    length = whole_keys.shape[0]
    key_block = min(512, length)
    block_count = length // key_block

    def visit(block_index, carry_now):
        offset = block_index * key_block
        block_keys = lax.dynamic_slice_in_dim(whole_keys, offset, key_block, 0).reshape(
            key_block, H, DH
        )
        block_values = lax.dynamic_slice_in_dim(whole_values, offset, key_block, 0).reshape(
            key_block, H, DH
        )
        block_seg = lax.dynamic_slice_in_dim(whole_seg, offset, key_block, 0)
        grad_query_sum, key_terms, value_terms = carry_now
        scores = (
            jnp.einsum("qhd,khd->hqk", query_heads, block_keys, preferred_element_type=jnp.float32)
            * 0.125
        )
        visible = (seg_low[:, None] == block_seg[None, :])[None]
        probs = jnp.where(visible, jnp.exp(scores - log_sum[:, :, None]), 0.0)
        grad_probs = jnp.einsum(
            "qhd,khd->hqk", mixed_heads, block_values, preferred_element_type=jnp.float32
        )
        grad_scores = (probs * (grad_probs - row_dot[:, :, None])).astype(jnp.bfloat16)
        grad_query_sum = grad_query_sum + jnp.einsum(
            "hqk,khd->qhd", grad_scores, block_keys, preferred_element_type=jnp.float32
        )
        key_part = (
            jnp.einsum(
                "hqk,qhd->khd", grad_scores, query_heads, preferred_element_type=jnp.float32
            ).reshape(key_block, model_width)
            * 0.125
        )
        value_part = jnp.einsum(
            "hqk,qhd->khd",
            probs.astype(jnp.bfloat16),
            mixed_heads,
            preferred_element_type=jnp.float32,
        ).reshape(key_block, model_width)
        key_terms = lax.dynamic_update_slice_in_dim(key_terms, key_part, offset, 0)
        value_terms = lax.dynamic_update_slice_in_dim(value_terms, value_part, offset, 0)
        return (grad_query_sum, key_terms, value_terms)

    initial = (
        jnp.zeros((tokens, H, DH), jnp.float32),
        jnp.zeros((length, model_width), jnp.float32),
        jnp.zeros((length, model_width), jnp.float32),
    )
    grad_query_sum, key_terms, value_terms = lax.fori_loop(0, block_count, visit, initial)
    grad_key_sum, grad_value_sum = (
        lax.psum_scatter(
            key_terms.astype(jnp.bfloat16), "ctx", scatter_dimension=0, tiled=True
        ).astype(jnp.float32),
        lax.psum_scatter(
            value_terms.astype(jnp.bfloat16), "ctx", scatter_dimension=0, tiled=True
        ).astype(jnp.float32),
    )
    grad_queries = (grad_query_sum.reshape(tokens, model_width) * 0.125).astype(jnp.bfloat16)
    grad_keys = grad_key_sum.astype(jnp.bfloat16)
    grad_values = grad_value_sum.astype(jnp.bfloat16)
    grad_w_query = outer_dot(token_rows, grad_queries)
    grad_b_query = jnp.sum(grad_queries.astype(jnp.float32), axis=0)
    grad_w_key = outer_dot(token_rows, grad_keys)
    grad_w_value = outer_dot(token_rows, grad_values)
    grad_b_value = jnp.sum(grad_values.astype(jnp.float32), axis=0)
    grad_rows = (
        grad_mid
        + back_dot(grad_queries, w_query)
        + back_dot(grad_keys, w_key)
        + back_dot(grad_values, w_value)
    )
    grads = (
        grad_w_query,
        grad_b_query,
        grad_w_key,
        grad_w_value,
        grad_b_value,
        grad_w_output,
        grad_b_output,
        grad_attn_gain,
        grad_attn_shift,
        grad_w_inner,
        grad_b_inner,
        grad_w_outer,
        grad_b_outer,
        grad_ffn_gain,
        grad_ffn_shift,
    )
    return (grad_rows, grads)


def on_device(
    hidden,
    segment,
    cotangent,
    w_query,
    b_query,
    w_key,
    w_value,
    b_value,
    w_output,
    b_output,
    attn_gain,
    attn_shift,
    w_inner,
    b_inner,
    w_outer,
    b_outer,
    ffn_gain,
    ffn_shift,
):
    micro_count = hidden.shape[0]
    totals = None
    results = []
    input_grads = []
    for micro_index in range(micro_count):
        forward_weights = (
            lax.all_gather(w_query, ("seq", "ctx"), axis=0, tiled=True),
            lax.all_gather(b_query, ("seq", "ctx"), axis=0, tiled=True),
            lax.all_gather(w_key, ("seq", "ctx"), axis=0, tiled=True),
            lax.all_gather(w_value, ("seq", "ctx"), axis=0, tiled=True),
            lax.all_gather(b_value, ("seq", "ctx"), axis=0, tiled=True),
            lax.all_gather(w_output, ("seq", "ctx"), axis=0, tiled=True),
            lax.all_gather(b_output, ("seq", "ctx"), axis=0, tiled=True),
            lax.all_gather(attn_gain, ("seq", "ctx"), axis=0, tiled=True),
            lax.all_gather(attn_shift, ("seq", "ctx"), axis=0, tiled=True),
            lax.all_gather(w_inner, ("seq", "ctx"), axis=0, tiled=True),
            lax.all_gather(b_inner, ("seq", "ctx"), axis=0, tiled=True),
            lax.all_gather(w_outer, ("seq", "ctx"), axis=0, tiled=True),
            lax.all_gather(b_outer, ("seq", "ctx"), axis=0, tiled=True),
            lax.all_gather(ffn_gain, ("seq", "ctx"), axis=0, tiled=True),
            lax.all_gather(ffn_shift, ("seq", "ctx"), axis=0, tiled=True),
        )
        kept, result = forward_pass(hidden[micro_index], segment[micro_index], forward_weights)
        results.append(result)
        backward_weights = (
            lax.all_gather(w_query, ("seq", "ctx"), axis=0, tiled=True),
            lax.all_gather(b_query, ("seq", "ctx"), axis=0, tiled=True),
            lax.all_gather(w_key, ("seq", "ctx"), axis=0, tiled=True),
            lax.all_gather(w_value, ("seq", "ctx"), axis=0, tiled=True),
            lax.all_gather(b_value, ("seq", "ctx"), axis=0, tiled=True),
            lax.all_gather(w_output, ("seq", "ctx"), axis=0, tiled=True),
            lax.all_gather(b_output, ("seq", "ctx"), axis=0, tiled=True),
            lax.all_gather(attn_gain, ("seq", "ctx"), axis=0, tiled=True),
            lax.all_gather(attn_shift, ("seq", "ctx"), axis=0, tiled=True),
            lax.all_gather(w_inner, ("seq", "ctx"), axis=0, tiled=True),
            lax.all_gather(b_inner, ("seq", "ctx"), axis=0, tiled=True),
            lax.all_gather(w_outer, ("seq", "ctx"), axis=0, tiled=True),
            lax.all_gather(b_outer, ("seq", "ctx"), axis=0, tiled=True),
            lax.all_gather(ffn_gain, ("seq", "ctx"), axis=0, tiled=True),
            lax.all_gather(ffn_shift, ("seq", "ctx"), axis=0, tiled=True),
        )
        grad_rows, grads = backward_pass(cotangent[micro_index], kept, backward_weights)
        input_grads.append(grad_rows)
        if totals is None:
            totals = grads
        else:
            totals = jax.tree.map(jnp.add, totals, grads)
    owned = (
        lax.psum_scatter(totals[0], ("seq", "ctx"), scatter_dimension=0, tiled=True),
        lax.psum_scatter(totals[1], ("seq", "ctx"), scatter_dimension=0, tiled=True),
        lax.psum_scatter(totals[2], ("seq", "ctx"), scatter_dimension=0, tiled=True),
        lax.psum_scatter(totals[3], ("seq", "ctx"), scatter_dimension=0, tiled=True),
        lax.psum_scatter(totals[4], ("seq", "ctx"), scatter_dimension=0, tiled=True),
        lax.psum_scatter(totals[5], ("seq", "ctx"), scatter_dimension=0, tiled=True),
        lax.psum_scatter(totals[6], ("seq", "ctx"), scatter_dimension=0, tiled=True),
        lax.psum_scatter(totals[7], ("seq", "ctx"), scatter_dimension=0, tiled=True),
        lax.psum_scatter(totals[8], ("seq", "ctx"), scatter_dimension=0, tiled=True),
        lax.psum_scatter(totals[9], ("seq", "ctx"), scatter_dimension=0, tiled=True),
        lax.psum_scatter(totals[10], ("seq", "ctx"), scatter_dimension=0, tiled=True),
        lax.psum_scatter(totals[11], ("seq", "ctx"), scatter_dimension=0, tiled=True),
        lax.psum_scatter(totals[12], ("seq", "ctx"), scatter_dimension=0, tiled=True),
        lax.psum_scatter(totals[13], ("seq", "ctx"), scatter_dimension=0, tiled=True),
        lax.psum_scatter(totals[14], ("seq", "ctx"), scatter_dimension=0, tiled=True),
    )
    return (jnp.stack(results), jnp.stack(input_grads)) + tuple(owned)


AXES = ("seq", "ctx")
LOG2E = 1.4426950408889634
SCORE_UNIT = 0.125 * LOG2E
HIDDEN_SCORE = -1e30
VMEM_BYTES = 62 << 20
SLAB = 128
WEIGHT = 30


def place_of(index, me):
    mz, mc, my, mx = me
    bx, by, bc, bz = index & 1, (index >> 1) & 1, (index >> 2) & 1, index >> 3
    kx, ky, kz = bx ^ mx, by ^ my, bz ^ mz
    even = bc == 0
    first = jnp.where(even, kx, ky)
    second = jnp.where(even, ky, kx)
    return bc == mc, first, second, kz


def read_me(me_ref):
    return me_ref[0], me_ref[1], me_ref[2], me_ref[3]


def start_load(me, pieces, columns, target, rows, count, sem):
    def body(index, carry):
        own, first, second, kz = place_of(index, me)
        spot = target.at[pl.ds(pl.multiple_of(index * rows, 8), rows), :]
        for number, piece in enumerate(pieces):
            mine = own if number < 2 else jnp.logical_not(own)

            @pl.when(jnp.logical_and(mine, second == number % 2))
            def _(piece=piece):
                source = piece.at[first, kz]
                if columns is not None:
                    source = source.at[:, pl.ds(columns[0], columns[1])]
                pltpu.make_async_copy(source, spot, sem).start()

        return carry

    lax.fori_loop(0, count, body, 0)


def end_load(target, sem):
    pltpu.make_async_copy(target, target, sem).wait()


def store_blocks(me, value_ref, keep_ref, send_ref, first_block, count, rows, column, width):
    def body(step, carry):
        own, first, second, kz = place_of(first_block + step, me)
        value = value_ref[pl.ds(pl.multiple_of(step * rows, 8), rows), :].astype(jnp.bfloat16)

        @pl.when(own)
        def _():
            keep_ref[first, second, kz, :, pl.ds(column, width)] = value

        @pl.when(jnp.logical_not(own))
        def _():
            send_ref[first, second, kz, :, pl.ds(column, width)] = value

        return carry

    lax.fori_loop(0, count, body, 0)


def lanes_of(shape):
    return lax.broadcasted_iota(jnp.int32, shape, len(shape) - 1)


def nn(a, b):
    return jnp.dot(a, b, preferred_element_type=jnp.float32)


def nt(a, b):
    return lax.dot_general(a, b, (((1,), (1,)), ((), ())), preferred_element_type=jnp.float32)


def tn(a, b):
    return lax.dot_general(a, b, (((0,), (0,)), ((), ())), preferred_element_type=jnp.float32)


def row_sum(values):
    return jnp.sum(values, axis=0, keepdims=True)


def pack_kernel(me_ref, hidden_ref, segment_ref, cot_ref, wq_ref, wk_ref, wv_ref, *rest):
    vectors, inner_ref = rest[:8], rest[8]
    out_ref, near_ref, far_ref, cot_near_ref, cot_far_ref = rest[9:]
    rows, width = wq_ref.shape
    out_ref[:, 0:width] = wq_ref[...]
    out_ref[:, width : 2 * width] = wk_ref[...]
    out_ref[:, 2 * width : 3 * width] = wv_ref[...]
    share = inner_ref.shape[1]
    lines = [ref[...].astype(jnp.float32) for ref in vectors]
    lines = [jnp.concatenate([line, jnp.zeros((1, SLAB - rows), jnp.float32)], axis=1) for line in lines]
    last = jnp.concatenate(
        [inner_ref[...].astype(jnp.float32), jnp.zeros((1, SLAB - share), jnp.float32)], axis=1
    )
    slab = jnp.concatenate(lines + [last, jnp.zeros((rows - 9, SLAB), jnp.float32)], axis=0)
    out_ref[:, 3 * width : 3 * width + SLAB] = slab.astype(jnp.bfloat16)
    x = me_ref[3]
    quarter = hidden_ref.shape[1]
    for ref, cotangent, pick in ((near_ref, cot_near_ref, x), (far_ref, cot_far_ref, 1 - x)):
        ref[0:quarter, :] = hidden_ref[pick]
        cotangent[...] = cot_ref[pick]
        both = segment_ref[...].astype(jnp.float32)
        line = jnp.where(pick == 0, both[0:1, :], both[1:2, :]).astype(jnp.bfloat16)
        ref[quarter : quarter + 8, 0:quarter] = jnp.broadcast_to(line, (8, quarter))
        ref[quarter : quarter + 8, quarter:width] = jnp.zeros((8, width - quarter), jnp.bfloat16)


def settle_kernel(me_ref, near_ref, far_ref, out_ref):
    x = me_ref[3]
    out_ref[x] = near_ref[...].astype(out_ref.dtype)
    out_ref[1 - x] = far_ref[...].astype(out_ref.dtype)


def spread_lanes(block, share, offset, tiles, tile):
    lane = lanes_of(block.shape)
    moved = pltpu.roll(block, offset, axis=1) if offset else block
    tiles[tile] = jnp.where(
        jnp.logical_and(lane >= offset, lane < offset + share), moved, tiles[tile]
    )
    if offset + share > 128:
        tiles[tile + 1] = jnp.where(lane < offset + share - 128, moved, tiles[tile + 1])


def project_kernel(
    me_ref, r0, r1, r2, r3, p0, p1, p2, p3,
    q_ref, k_ref, v_ref, vec_ref, bias_ref, x_ref, segrow_ref, segcol_ref, w_ref, slab_ref, sem,
):
    me = read_me(me_ref)
    tokens, width = q_ref.shape
    blocks = 32
    rows = width // blocks
    start_load(me, (p0, p1, p2, p3), None, w_ref, rows, blocks, sem)
    quarter = tokens // 2
    for number, ref in enumerate((r0, r1, r2, r3)):
        span = pl.ds(number * quarter, quarter)
        x_ref[span, :] = ref[0:quarter, :]
        line = ref[quarter : quarter + 8, 0:quarter].astype(jnp.float32)
        segrow_ref[:, span] = line
        segcol_ref[span, :] = jnp.broadcast_to(line[0:1, :], (128, quarter)).T
    end_load(w_ref, sem)
    slab_ref[...] = w_ref[:, 3 * width : 3 * width + SLAB].astype(jnp.float32)
    tiles = [jnp.zeros((8, 128), jnp.float32) for _ in range(width // 128 + 1)]
    for index in range(blocks):
        start = rows * index
        spread_lanes(slab_ref[start : start + 8, :], rows, start % 128, tiles, start // 128)
    vectors = jnp.concatenate(tiles[: width // 128], axis=1)
    vec_ref[...] = vectors
    share = bias_ref.shape[1] // blocks
    tiles = [jnp.zeros((8, 128), jnp.float32) for _ in range(4)]
    for turn in range(4):
        lines = slab_ref[pl.ds(rows * turn + 8, 8, stride=4 * rows), :]
        spread_lanes(lines, share, share * turn % 128, tiles, share * turn // 128)
    for group in range(8):
        for tile in range(3):
            bias_ref[0:1, pl.ds(group * 384 + tile * 128, 128)] = tiles[tile][group : group + 1, :]
    b_query, b_value = vectors[0:1, :], vectors[1:2, :]
    q_ref[...] = (nn(x_ref[0:tokens, :], w_ref[:, 0:width]) + b_query).astype(jnp.bfloat16)

    @pl.loop(0, 2)
    def _(part):
        span = pl.ds(pl.multiple_of(part * tokens, tokens), tokens)
        k_ref[span, :] = nn(x_ref[span, :], w_ref[:, width : 2 * width]).astype(jnp.bfloat16)
        v_ref[span, :] = (nn(x_ref[span, :], w_ref[:, 2 * width : 3 * width]) + b_value).astype(
            jnp.bfloat16
        )


def attend_kernel(q_ref, k_ref, v_ref, segcol_ref, segrow_ref, mixed_ref, lse_ref, bias_ref):
    tokens = q_ref.shape[0]
    keys = k_ref.shape[0]
    tile = 256

    @pl.when(pl.program_id(0) == 0)
    def _():
        visible = segcol_ref[0:tokens, 0:1] == segrow_ref[0:1, :]
        bias_ref[...] = jnp.where(visible, 0.0, HIDDEN_SCORE)

    low_half = lanes_of((1, 128)) < 64
    key_rows = k_ref[...]
    value_rows = v_ref[...]
    one = jnp.ones((), jnp.bfloat16)
    zero = jnp.zeros((), jnp.bfloat16)
    for part in range(tokens // tile):
        span = pl.ds(part * tile, tile)
        query = q_ref[span, :]
        bias = bias_ref[span, :]
        outs, sums = [], []
        for head in range(2):
            mine = low_half if head == 0 else jnp.logical_not(low_half)
            scores = nt(jnp.where(mine, query, zero), key_rows) + bias
            top = jnp.max(scores, axis=-1, keepdims=True)
            weights = jnp.exp2((scores - top) * SCORE_UNIT).astype(jnp.bfloat16)
            product = nn(weights, jnp.where(mine, value_rows, one))
            total = product[:, 64:65] if head == 0 else product[:, 0:1]
            outs.append(product / total)
            sums.append(top * SCORE_UNIT + jnp.log2(total))
        mixed_ref[span, :] = jnp.where(low_half, outs[0], outs[1])
        lane = lanes_of((tile, 128))
        both = jnp.where(lane == 0, sums[0], jnp.where(lane == 1, sums[1], 0.0))
        lse_ref[0, :, span] = both.T[0:8, :]


def attend_back_kernel(
    q_ref, k_ref, v_ref, gm_ref, mixed_ref, lse_ref, segcol_ref, segrow_ref,
    dq_ref, dk_ref, dv_ref, bias_ref,
):
    tokens = q_ref.shape[0]
    keys = k_ref.shape[0]
    tile = 256

    @pl.when(pl.program_id(0) == 0)
    def _():
        visible = segcol_ref[:, 0:1] == segrow_ref[0:1, 0:tokens]
        bias_ref[...] = jnp.where(visible, 0.0, HIDDEN_SCORE)

    low_half = lanes_of((1, 128)) < 64
    zero = jnp.zeros((), jnp.bfloat16)
    query = q_ref[...]
    grad = gm_ref[...]
    product = (grad.astype(jnp.float32) * mixed_ref[...]).T
    row_dots = [row_sum(product[0:64, :]), row_sum(product[64:128, :])]
    masks = (low_half, jnp.logical_not(low_half))
    queries = [jnp.where(mine, query, zero) for mine in masks]
    grads = [jnp.where(mine, grad, zero) for mine in masks]
    def body(turn, grad_query):
        for half in range(2):
            span = pl.ds(pl.multiple_of((2 * turn + half) * tile, tile), tile)
            key_rows = k_ref[span, :]
            value_rows = v_ref[span, :]
            bias = bias_ref[span, :]
            grad_key = jnp.zeros((tile, 128), jnp.float32)
            grad_value = jnp.zeros((tile, 128), jnp.float32)
            for head in range(2):
                scores = nt(key_rows, queries[head])
                probs = jnp.exp2(scores * SCORE_UNIT + (bias - lse_ref[0, head : head + 1, :]))
                grad_probs = nt(value_rows, grads[head])
                grad_scores = (probs * (grad_probs - row_dots[head])).astype(jnp.bfloat16)
                grad_key = grad_key + nn(grad_scores, queries[head])
                grad_value = grad_value + nn(probs.astype(jnp.bfloat16), grads[head])
                grad_query = grad_query + tn(grad_scores, jnp.where(masks[head], key_rows, zero))
            dk_ref[span, :] = (grad_key * 0.125).astype(jnp.bfloat16)
            dv_ref[span, :] = grad_value.astype(jnp.bfloat16)
        return grad_query

    grad_query = lax.fori_loop(0, keys // tile // 2, body, jnp.zeros((tokens, 128), jnp.float32))
    dq_ref[...] = (grad_query * 0.125).astype(jnp.bfloat16)


def normalize(values):
    average = jnp.mean(values, axis=-1, keepdims=True)
    centered = values - average
    spread = jnp.mean(centered * centered, axis=-1, keepdims=True)
    inverse = lax.rsqrt(spread + epsilon)
    return centered * inverse, inverse


def normalize_back(grad, unit, inverse, gain):
    scaled = grad * gain
    plain = jnp.mean(scaled, axis=-1, keepdims=True)
    cross = jnp.mean(scaled * unit, axis=-1, keepdims=True)
    return inverse * (scaled - plain - unit * cross)


def feed_in_kernel(
    me_ref, mixed_a_ref, mixed_b_ref, x_ref, vec_ref, bias_ref, a0, a1, a2, a3,
    low_ref, act_ref, slope_ref, unit_ref, inverse_ref, rest_ref, wo_ref, wi_ref, sem_o, sem_i,
):
    me = read_me(me_ref)
    tokens, width = low_ref.shape
    inner = wi_ref.shape[1]
    blocks = 32
    start_load(me, (a0, a1, a2, a3), (0, width), wo_ref, width // blocks, blocks, sem_o)
    start_load(me, (a0, a1, a2, a3), (width, inner), wi_ref, width // blocks, blocks, sem_i)
    b_output, attn_gain, attn_shift = vec_ref[2:3, :], vec_ref[3:4, :], vec_ref[4:5, :]
    b_outer = vec_ref[5:6, :]
    end_load(wo_ref, sem_o)
    part = mixed_a_ref.shape[1]
    branch = b_output + nn(mixed_a_ref[...].astype(jnp.bfloat16), wo_ref[0:part, :])
    branch = branch + nn(mixed_b_ref[...].astype(jnp.bfloat16), wo_ref[part:width, :])
    unit_one, inverse_one = normalize(x_ref[0:tokens, :].astype(jnp.float32) + branch)
    normed = unit_one * attn_gain + attn_shift
    unit_ref[...] = unit_one
    inverse_ref[...] = jnp.broadcast_to(inverse_one, inverse_ref.shape)
    low_ref[...] = normed.astype(jnp.bfloat16)
    rest_ref[...] = normed + b_outer
    end_load(wi_ref, sem_i)
    step = 512

    @pl.loop(0, inner // step)
    def _(turn):
        span = pl.ds(pl.multiple_of(turn * step, step), step)
        pre_act = nn(low_ref[...], wi_ref[:, span]) + bias_ref[0:1, span]
        normal_cdf = 0.5 * (1.0 + lax.erf(pre_act * root_half))
        density = jnp.exp(-0.5 * pre_act * pre_act) * inv_root_tau
        act_ref[:, span] = (pre_act * normal_cdf).astype(jnp.bfloat16)
        slope_ref[:, span] = (normal_cdf + pre_act * density).astype(jnp.bfloat16)


def feed_out_kernel(
    me_ref, act_ref, rest_ref, cot_near_ref, cot_far_ref, vec_ref, b0, b1, b2, b3,
    near_ref, far_ref, second_ref, outer_ref, sums_ref, keep_ref, send_ref,
    wu_ref, grad_ref, sem_u,
):
    me = read_me(me_ref)
    tokens, width = rest_ref.shape
    inner = act_ref.shape[1]
    blocks = 32
    rows = inner // blocks
    quarter = tokens // 2
    start_load(me, (b0, b1, b2, b3), None, wu_ref, rows, blocks, sem_u)
    ffn_gain, ffn_shift = vec_ref[6:7, :], vec_ref[7:8, :]
    end_load(wu_ref, sem_u)

    @pl.loop(0, 2)
    def _(part):
        span = pl.ds(pl.multiple_of(part * quarter, quarter), quarter)
        second_ref[span, :] = rest_ref[span, :] + nn(act_ref[span, :], wu_ref[...])

    sums = [jnp.zeros((1, width), jnp.float32) for _ in range(3)]
    for part in range(2):
        span = pl.ds(part * quarter, quarter)
        unit_two, inverse_two = normalize(second_ref[span, :])
        out_ref, cot_ref = ((near_ref, cot_near_ref), (far_ref, cot_far_ref))[part]
        out_ref[...] = (unit_two * ffn_gain + ffn_shift).astype(jnp.bfloat16)
        tangent = cot_ref[...].astype(jnp.float32)
        second = normalize_back(tangent, unit_two, inverse_two, ffn_gain)
        second_ref[span, :] = second
        outer = second.astype(jnp.bfloat16)
        outer_ref[span, :] = outer
        sums[0] = sums[0] + row_sum(outer.astype(jnp.float32))
        sums[1] = sums[1] + row_sum(tangent * unit_two)
        sums[2] = sums[2] + row_sum(tangent)
    sums_ref[...] = jnp.concatenate(sums + [jnp.zeros((5, width), jnp.float32)], axis=0)
    half = width // 2

    @pl.loop(0, inner // half)
    def _(turn):
        cols = pl.ds(pl.multiple_of(turn * half, half), half)
        grad_ref[...] = tn(act_ref[:, cols], outer_ref[...])
        store_blocks(
            me, grad_ref, keep_ref, send_ref, turn * (half // rows), half // rows, rows, 0, width
        )


def slope_kernel(
    me_ref, slope_ref, outer_ref, b0, b1, b2, b3, pre_ref, bsum_ref, wu_ref, sem_u
):
    me = read_me(me_ref)
    inner = slope_ref.shape[1]
    blocks = 32
    start_load(me, (b0, b1, b2, b3), None, wu_ref, inner // blocks, blocks, sem_u)
    end_load(wu_ref, sem_u)
    step = 512

    @pl.loop(0, inner // step)
    def _(turn):
        span = pl.ds(pl.multiple_of(turn * step, step), step)
        grad_act = nt(outer_ref[...], wu_ref[span, :])
        grad_pre = (grad_act * slope_ref[:, span].astype(jnp.float32)).astype(jnp.bfloat16)
        bsum_ref[0:1, span] = row_sum(grad_pre.astype(jnp.float32))
        pre_ref[:, span] = grad_pre


def feed_back_kernel(
    me_ref, pre_ref, second_ref, low_ref, unit_ref, inverse_ref, mixed_a_ref, mixed_b_ref, vec_ref,
    a0, a1, a2, a3,
    mid_ref, gm_ref, sums_ref, keep_ref, send_ref,
    wo_ref, wi_ref, grad_ref, sem_o, sem_i,
):
    me = read_me(me_ref)
    tokens, width = second_ref.shape
    inner = wi_ref.shape[1]
    blocks = 32
    rows = width // blocks
    start_load(me, (a0, a1, a2, a3), (width, inner), wi_ref, rows, blocks, sem_i)
    start_load(me, (a0, a1, a2, a3), (0, width), wo_ref, rows, blocks, sem_o)
    step = 512

    @pl.loop(0, inner // step)
    def _(turn):
        first = pl.multiple_of(turn * step, step)
        grad_ref[:, 0:step] = tn(low_ref[...], pre_ref[:, pl.ds(first, step)])
        store_blocks(
            me, grad_ref.at[:, 0:step], keep_ref, send_ref, 0, blocks, rows,
            pl.multiple_of(width + first, 128), step,
        )

    end_load(wi_ref, sem_i)

    @pl.loop(0, 2)
    def _(part):
        span = pl.ds(pl.multiple_of(part * (tokens // 2), tokens // 2), tokens // 2)
        mid_ref[span, :] = second_ref[span, :] + nt(pre_ref[span, :], wi_ref[...])

    end_load(wo_ref, sem_o)
    attn_gain = vec_ref[3:4, :]
    grad_normed = mid_ref[...]
    unit = unit_ref[...]
    mid = normalize_back(grad_normed, unit, inverse_ref[:, 0:1], attn_gain)
    mid_ref[...] = mid
    branch = mid.astype(jnp.bfloat16)
    sums_ref[...] = jnp.zeros(sums_ref.shape, jnp.float32)
    sums_ref[0:1, :] = row_sum(branch.astype(jnp.float32))
    sums_ref[1:2, :] = row_sum(grad_normed * unit)
    sums_ref[2:3, :] = row_sum(grad_normed)
    gm_ref[...] = nt(branch, wo_ref[...]).astype(jnp.bfloat16)
    part = mixed_a_ref.shape[1]
    grad_ref[0:part, :] = tn(mixed_a_ref[...].astype(jnp.bfloat16), branch)
    grad_ref[part:width, :] = tn(mixed_b_ref[...].astype(jnp.bfloat16), branch)
    store_blocks(me, grad_ref, keep_ref, send_ref, 0, blocks, rows, 0, width)


def weight_kernel(
    me_ref, x_ref, dqa_ref, dka_ref, dva_ref, dqb_ref, dkb_ref, dvb_ref,
    sums_two_ref, sums_one_ref, bsum_ref, keep_ref, send_ref, grad_ref, slab_ref,
):
    me = read_me(me_ref)
    tokens, half = dqa_ref.shape
    width = 2 * half
    blocks = 32
    rows = width // blocks
    refs = (dqa_ref, dqb_ref, dka_ref, dkb_ref, dva_ref, dvb_ref)
    for number, ref in enumerate(refs):
        grad_ref[...] = tn(x_ref[0 : ref.shape[0], :], ref[...])
        store_blocks(me, grad_ref, keep_ref, send_ref, 0, blocks, rows, number * half, half)

    def sums(first, second):
        return jnp.concatenate(
            [row_sum(first[...].astype(jnp.float32)), row_sum(second[...].astype(jnp.float32))],
            axis=1,
        )

    vectors = jnp.concatenate(
        [
            sums(dqa_ref, dqb_ref),
            sums(dva_ref, dvb_ref),
            sums_one_ref[0:3, :],
            sums_two_ref[0:3, :],
        ],
        axis=0,
    )
    share = bsum_ref.shape[1] // blocks
    lane = lanes_of((8, 128))
    slab_ref[...] = jnp.zeros(slab_ref.shape, jnp.float32)
    for index in range(blocks):
        tile, offset = rows * index // 128, rows * index % 128
        piece = vectors[:, tile * 128 : tile * 128 + 128]
        if offset + rows > 128:
            piece = jnp.where(
                lane >= offset, piece, vectors[:, tile * 128 + 128 : tile * 128 + 256]
            )
        moved = pltpu.roll(piece, (128 - offset) % 128, axis=1) if offset else piece
        slab_ref[rows * index : rows * index + 8, :] = jnp.where(lane < rows, moved, 0.0)
    groups = jnp.concatenate([bsum_ref[0:1, pl.ds(384 * g, 384)] for g in range(8)], axis=0)
    for turn in range(4):
        tile, offset = share * turn // 128, share * turn % 128
        piece = groups[:, tile * 128 : tile * 128 + 128]
        if offset + share > 128:
            piece = jnp.where(lane >= offset, piece, groups[:, tile * 128 + 128 : tile * 128 + 256])
        moved = pltpu.roll(piece, (128 - offset) % 128, axis=1) if offset else piece
        slab_ref[pl.ds(rows * turn + 8, 8, stride=4 * rows), :] = jnp.where(lane < share, moved, 0.0)
    store_blocks(me, slab_ref, keep_ref, send_ref, 0, blocks, rows, 3 * width, SLAB)


def input_kernel(
    me_ref, mid_ref, dqa_ref, dka_ref, dva_ref, dqb_ref, dkb_ref, dvb_ref, other_ref,
    p0, p1, p2, p3, near_ref, far_ref, w_ref, sem,
):
    me = read_me(me_ref)
    tokens, width = mid_ref.shape
    half = width // 2
    blocks = 32
    start_load(me, (p0, p1, p2, p3), (0, 3 * width), w_ref, width // blocks, blocks, sem)
    own = []
    for number, ref in enumerate((dka_ref, dva_ref, dkb_ref, dvb_ref)):
        theirs = other_ref[:, number * half : (number + 1) * half].astype(jnp.float32)
        own.append((ref[0:tokens, :].astype(jnp.float32) + theirs).astype(jnp.bfloat16))
    end_load(w_ref, sem)
    total = mid_ref[...]
    for number, value in enumerate((dqa_ref[...], dqb_ref[...], own[0], own[2], own[1], own[3])):
        total = total + nt(value, w_ref[:, number * half : (number + 1) * half])
    low = total.astype(jnp.bfloat16)
    near_ref[...] = low[: tokens // 2]
    far_ref[...] = low[tokens // 2 :]


def shape_of(shape, dtype):
    return jax.ShapeDtypeStruct(shape, dtype)


def call(kernel, name, out_shape, kinds, scratch, flops, moved):
    spaces = {"s": pltpu.SMEM, "v": pltpu.VMEM, "a": pl.ANY}
    return pl.pallas_call(
        kernel,
        name=name,
        out_shape=out_shape,
        in_specs=[pl.BlockSpec(memory_space=spaces[kind]) for kind in kinds],
        scratch_shapes=scratch,
        compiler_params=pltpu.CompilerParams(vmem_limit_bytes=VMEM_BYTES),
        cost_estimate=pl.CostEstimate(
            flops=WEIGHT * flops, bytes_accessed=WEIGHT * moved, transcendentals=0
        ),
    )


def tie(*values):
    return lax.optimization_barrier(values)


def fast_device(depth, hidden, segment, cotangent, *weights):
    (
        w_query, b_query, w_key, w_value, b_value, w_output, b_output, attn_gain, attn_shift,
        w_inner, b_inner, w_outer, b_outer, ffn_gain, ffn_shift,
    ) = weights
    bf16, f32 = jnp.bfloat16, jnp.float32
    quarter, width = hidden.shape[1], hidden.shape[2]
    tokens = 2 * quarter
    keys = 2 * tokens
    rows = w_query.shape[0]
    inner = w_inner.shape[1]
    inner_rows = w_outer.shape[0]
    seq_index, ctx_index = lax.axis_index("seq"), lax.axis_index("ctx")
    me = jnp.stack([seq_index >> 1, seq_index & 1, ctx_index >> 1, ctx_index & 1]).astype(jnp.int32)

    def table(move):
        pairs = []
        for bz in range(depth):
            for bc in range(2):
                for by in range(2):
                    for bx in range(2):
                        tz, tc, ty, tx = move(bz, bc, by, bx)
                        pairs.append(
                            (((bz * 2 + bc) * 2 + by) * 2 + bx, ((tz * 2 + tc) * 2 + ty) * 2 + tx)
                        )
        return pairs

    along_z = [table(lambda a, b, d, e, k=k: (a ^ k, b, d, e)) for k in range(1, depth)]
    plane_one = table(lambda a, b, d, e: (a, b, d, 1 - e) if b == 0 else (a, b, 1 - d, e))
    plane_two = table(lambda a, b, d, e: (a, b, 1 - d, e) if b == 0 else (a, b, d, 1 - e))
    partner = table(lambda a, b, d, e: (a, 1 - b, d, e))
    home_near = table(lambda a, b, d, e: (a, d, b, e))
    home_far = table(lambda a, b, d, e: (a, d, b, 1 - e))

    def hop(value, pairs):
        return lax.ppermute(value, AXES, pairs)

    def hops_z(value):
        return [hop(value, pairs) for pairs in along_z]

    sem = pltpu.SemaphoreType.DMA
    flat = 2 * tokens * width
    slabbed = 3 * width + SLAB

    vectors_in = (
        b_query, b_value, b_output, attn_gain, attn_shift, b_outer, ffn_gain, ffn_shift, b_inner,
    )
    packed_row = shape_of((quarter + 8, width), bf16)
    plain_row = shape_of((quarter, width), bf16)
    first_in, near, far, cot_near, cot_far = call(
        pack_kernel,
        "pack",
        (shape_of((rows, slabbed), bf16), packed_row, packed_row, plain_row, plain_row),
        "s" + "v" * 15,
        [],
        1,
        1 << 20,
    )(
        me, hidden, segment, cotangent, w_query, w_key, w_value,
        *[vector[None, :] for vector in vectors_in],
    )
    near, far = hop(near, home_near), hop(far, home_far)
    second_in = jnp.concatenate([w_output, w_inner], axis=1)
    climbed, near, far, second_in = tie(hops_z(first_in), near, far, second_in)
    levels_one = jnp.stack([first_in, *climbed])
    got_one = hop(levels_one, plane_one)
    near_other, far_other = hop(near, partner), hop(far, partner)
    second_one = hop(second_in, along_z[0])
    got_one, near_other, far_other, second_one, second_in = tie(
        got_one, near_other, far_other, second_one, second_in
    )
    half_one = jnp.stack([levels_one, got_one])
    other_one = hop(half_one, plane_two)
    half_one_p = hop(half_one, partner)
    second_two = hop(second_in, along_z[1])
    other_one, half_one_p, second_two, second_in, third_in, cot_near, cot_far = tie(
        other_one, half_one_p, second_two, second_in, w_outer, cot_near, cot_far
    )
    other_one_p = hop(other_one, partner)
    cot_near, cot_far = hop(cot_near, home_near), hop(cot_far, home_far)
    second_three = hop(second_in, along_z[2])
    third_one, third_two = hop(third_in, along_z[0]), hop(third_in, along_z[1])
    group_one = (half_one, other_one, half_one_p, other_one_p)

    q, k, v, vectors, bias, x_all, segrow, segcol = call(
        project_kernel,
        "project",
        (
            shape_of((tokens, width), bf16),
            shape_of((keys, width), bf16),
            shape_of((keys, width), bf16),
            shape_of((8, width), f32),
            shape_of((1, inner), f32),
            shape_of((keys, width), bf16),
            shape_of((8, keys), f32),
            shape_of((keys, 128), f32),
        ),
        "svvvvaaaa",
        [pltpu.VMEM((width, slabbed), bf16), pltpu.VMEM((width, SLAB), f32), sem],
        5 * flat * width,
        10 << 20,
    )(me, near, far, near_other, far_other, *group_one)

    q, second_three, third_one, third_two, cot_near, cot_far, third_in = tie(
        q, second_three, third_one, third_two, cot_near, cot_far, third_in
    )
    levels_two = jnp.stack([second_in, second_one, second_two, second_three])
    got_two = hop(levels_two, plane_one)
    third_three = hop(third_in, along_z[2])

    parts = 2
    pairs_now = width // 128 // parts
    params = pltpu.CompilerParams(vmem_limit_bytes=VMEM_BYTES)

    def attend(part):
        def column(count):
            return pl.BlockSpec((count, 128), lambda i: (0, i + part * pairs_now))

        def column_out(count):
            return pl.BlockSpec((count, 128), lambda i: (0, i))

        def whole(shape):
            return pl.BlockSpec(shape, lambda i: (0, 0))

        return pl.pallas_call(
            attend_kernel,
            name="attend",
            grid=(pairs_now,),
            out_shape=(
                shape_of((tokens, pairs_now * 128), f32),
                shape_of((pairs_now, 8, tokens), f32),
            ),
            in_specs=[
                column(tokens), column(keys), column(keys), whole((keys, 128)), whole((8, keys)),
            ],
            out_specs=(column_out(tokens), pl.BlockSpec((1, 8, tokens), lambda i: (i, 0, 0))),
            scratch_shapes=[pltpu.VMEM((tokens, keys), f32)],
            compiler_params=params,
            cost_estimate=pl.CostEstimate(
                flops=WEIGHT * 8 * tokens * keys * width // parts, bytes_accessed=WEIGHT << 22, transcendentals=0
            ),
        )

    mixed_a, lse_a = attend(0)(q, k, v, segcol, segrow)
    levels_three = jnp.stack([third_in, third_one, third_two, third_three])
    half_two = jnp.stack([levels_two, got_two])
    q_b, mixed_a, half_two, levels_three = tie(q, mixed_a, half_two, levels_three)
    other_two = hop(half_two, plane_two)
    half_two_p = hop(half_two, partner)
    got_three = hop(levels_three, plane_one)
    mixed_b, lse_b = attend(1)(q_b, k, v, segcol, segrow)
    half_three = jnp.stack([levels_three, got_three])
    mixed_b, other_two, half_three = tie(mixed_b, other_two, half_three)
    other_two_p = hop(other_two, partner)
    group_two = (half_two, other_two, half_two_p, other_two_p)
    other_three = hop(half_three, plane_two)
    half_three_p = hop(half_three, partner)

    low, act, slope, unit, inverse, rest = call(
        feed_in_kernel,
        "feed_in",
        (
            shape_of((tokens, width), bf16),
            shape_of((tokens, inner), bf16),
            shape_of((tokens, inner), bf16),
            shape_of((tokens, width), f32),
            shape_of((tokens, 128), f32),
            shape_of((tokens, width), f32),
        ),
        "svvvvvaaaa",
        [pltpu.VMEM((width, width), bf16), pltpu.VMEM((width, inner), bf16), sem, sem],
        flat * (width + inner),
        20 << 20,
    )(me, mixed_a, mixed_b, x_all, vectors, bias, *group_two)

    act, other_three = tie(act, other_three)
    other_three_p = hop(other_three, partner)
    group_three = (half_three, other_three, half_three_p, other_three_p)
    near_out, far_out, second, outer, sums_two, keep_three, send_three = call(
        feed_out_kernel,
        "feed_out",
        (
            plain_row,
            plain_row,
            shape_of((tokens, width), f32),
            shape_of((tokens, width), bf16),
            shape_of((8, width), f32),
            shape_of((2, 2, depth, inner_rows, width), bf16),
            shape_of((2, 2, depth, inner_rows, width), bf16),
        ),
        "svvvvvaaaa",
        [pltpu.VMEM((inner, width), bf16), pltpu.VMEM((width // 2, width), f32), sem],
        2 * flat * inner,
        20 << 20,
    )(me, act, rest, cot_near, cot_far, vectors, *group_three)

    got = hop(send_three, partner)
    near_out, far_out = hop(near_out, home_near), hop(far_out, home_far)

    grad_pre, bias_sums = call(
        slope_kernel,
        "slope",
        (shape_of((tokens, inner), bf16), shape_of((1, inner), f32)),
        "svvaaaa",
        [pltpu.VMEM((inner, width), bf16), sem],
        flat * inner,
        16 << 20,
    )(me, slope, outer, *group_three)

    def first_sum(keep, got):
        return keep[1] + got[1], keep[0] + got[0]

    def second_sum(kept, got):
        return kept[1] + got[1], kept[0] + got[0]

    def last_sum(levels, arrived):
        total = levels[0].astype(f32)
        for value in arrived:
            total = total + value.astype(f32)
        return total

    def climb(levels):
        return [hop(levels[k + 1], pairs) for k, pairs in enumerate(along_z)]

    three_send, three_kept = first_sum(keep_three, got)
    grad_pre, three_send, three_kept, near_out, far_out = tie(
        grad_pre, three_send, three_kept, near_out, far_out
    )
    three_got = hop(three_send, plane_one)

    mid, grad_mixed, sums_one, keep_two, send_two = call(
        feed_back_kernel,
        "feed_back",
        (
            shape_of((tokens, width), f32),
            shape_of((tokens, width), bf16),
            shape_of((8, width), f32),
            shape_of((2, 2, depth, rows, width + inner), bf16),
            shape_of((2, 2, depth, rows, width + inner), bf16),
        ),
        "svvvvvvvvaaaa",
        [
            pltpu.VMEM((width, width), bf16),
            pltpu.VMEM((width, inner), bf16),
            pltpu.VMEM((width, width), f32),
            sem, sem,
        ],
        flat * (2 * inner + 2 * width),
        30 << 20,
    )(me, grad_pre, second, low, unit, inverse, mixed_a, mixed_b, vectors, *group_two)

    two_got = hop(send_two, partner)
    three_send, three_kept = three_kept[1] + three_got[1], three_kept[0] + three_got[0]
    grad_mixed, three_send, three_kept = tie(grad_mixed, three_send, three_kept)
    three_got = hop(three_send, plane_two)

    def attend_back(part):
        def column(count):
            return pl.BlockSpec((count, 128), lambda i: (0, i + part * pairs_now))

        def column_out(count):
            return pl.BlockSpec((count, 128), lambda i: (0, i))

        def whole(shape):
            return pl.BlockSpec(shape, lambda i: (0, 0))

        return pl.pallas_call(
            attend_back_kernel,
            name="attend_back",
            grid=(pairs_now,),
            out_shape=(
                shape_of((tokens, pairs_now * 128), bf16),
                shape_of((keys, pairs_now * 128), bf16),
                shape_of((keys, pairs_now * 128), bf16),
            ),
            in_specs=[
                column(tokens), column(keys), column(keys), column(tokens), column_out(tokens),
                pl.BlockSpec((1, 8, tokens), lambda i: (i, 0, 0)),
                whole((keys, 128)), whole((8, keys)),
            ],
            out_specs=(column_out(tokens), column_out(keys), column_out(keys)),
            scratch_shapes=[pltpu.VMEM((keys, tokens), f32)],
            compiler_params=params,
            cost_estimate=pl.CostEstimate(
                flops=WEIGHT * 20 * tokens * keys * width // parts, bytes_accessed=WEIGHT << 22, transcendentals=0
            ),
        )

    back_a = attend_back(0)(q, k, v, grad_mixed, mixed_a, lse_a, segcol, segrow)

    three_levels = three_kept + three_got
    two_send, two_kept = first_sum(keep_two, two_got)
    back_a, three_levels, two_send, two_kept, grad_mixed_b = tie(
        back_a, three_levels, two_send, two_kept, grad_mixed
    )
    three_climb = climb(three_levels)
    two_got = hop(two_send, plane_one)

    back_b = attend_back(1)(q, k, v, grad_mixed_b, mixed_b, lse_b, segcol, segrow)

    total_three = last_sum(three_levels, three_climb)
    two_send, two_kept = second_sum(two_kept, two_got)
    back_b, total_three, two_send, two_kept = tie(back_b, total_three, two_send, two_kept)
    two_got = hop(two_send, plane_two)
    from_partner = hop(
        jnp.concatenate([value[tokens:] for value in back_a[1:] + back_b[1:]], axis=1), partner
    )

    keep_one, send_one = call(
        weight_kernel,
        "weight",
        (
            shape_of((2, 2, depth, rows, slabbed), bf16),
            shape_of((2, 2, depth, rows, slabbed), bf16),
        ),
        "svvvvvvvvvv",
        [pltpu.VMEM((width, width // 2), f32), pltpu.VMEM((width, SLAB), f32)],
        5 * flat * width,
        12 << 20,
    )(me, x_all, *back_a, *back_b, sums_two, sums_one, bias_sums)

    one_got = hop(send_one, partner)
    keep_one, two_levels = tie(keep_one, two_kept + two_got)
    two_climb = climb(two_levels)
    one_send, one_kept = first_sum(keep_one, one_got)
    mid, one_send, one_kept = tie(mid, one_send, one_kept)
    one_got = hop(one_send, plane_one)

    near_in, far_in = call(
        input_kernel,
        "input",
        (plain_row, plain_row),
        "svvvvvvvvaaaa",
        [pltpu.VMEM((width, 3 * width), bf16), sem],
        3 * flat * width,
        12 << 20,
    )(me, mid, *back_a, *back_b, from_partner, *group_one)

    one_got, near_in, far_in = tie(one_got, near_in, far_in)
    one_send, one_kept = second_sum(one_kept, one_got)
    one_got = hop(one_send, plane_two)
    near_in, far_in = hop(near_in, home_near), hop(far_in, home_far)
    total_two = last_sum(two_levels, two_climb)
    one_levels = one_kept + one_got
    one_levels, near_in, far_in, total_two = tie(one_levels, near_in, far_in, total_two)
    one_climb = climb(one_levels)

    def settle(first, second, dtype):
        return call(
            settle_kernel, "settle", shape_of((2, quarter, width), dtype), "svv", [], 1, 2 << 20
        )(me, first, second)

    result = settle(near_out, far_out, bf16)
    grad_input = settle(near_in, far_in, f32)
    total_one = last_sum(one_levels, one_climb)
    vector = [total_one[j, 3 * width : 3 * width + rows] for j in range(8)]
    grad_b_inner = total_one[8, 3 * width : 3 * width + inner_rows]
    return (
        result,
        grad_input,
        total_one[:, :width],
        vector[0],
        total_one[:, width : 2 * width],
        total_one[:, 2 * width : 3 * width],
        vector[1],
        total_two[:, :width],
        vector[2],
        vector[3],
        vector[4],
        total_two[:, width:],
        grad_b_inner,
        total_three,
        vector[5],
        vector[6],
        vector[7],
    )


def takes_fast(mesh):
    seq, ctx = mesh.shape["seq"], mesh.shape["ctx"]
    return ctx == 4 and seq == 8


def solution(mesh):
    return jax.shard_map(
        functools.partial(fast_device, mesh.shape["seq"] // 2) if takes_fast(mesh) else on_device,
        mesh=mesh,
        in_specs=(
            P("seq", "ctx", None),
            P("seq", "ctx"),
            P("seq", "ctx", None),
            P(("seq", "ctx"), None),
            P(("seq", "ctx")),
            P(("seq", "ctx"), None),
            P(("seq", "ctx"), None),
            P(("seq", "ctx")),
            P(("seq", "ctx"), None),
            P(("seq", "ctx")),
            P(("seq", "ctx")),
            P(("seq", "ctx")),
            P(("seq", "ctx"), None),
            P(("seq", "ctx")),
            P(("seq", "ctx"), None),
            P(("seq", "ctx")),
            P(("seq", "ctx")),
            P(("seq", "ctx")),
        ),
        out_specs=(
            P("seq", "ctx", None),
            P("seq", "ctx", None),
            P(("seq", "ctx"), None),
            P(("seq", "ctx")),
            P(("seq", "ctx"), None),
            P(("seq", "ctx"), None),
            P(("seq", "ctx")),
            P(("seq", "ctx"), None),
            P(("seq", "ctx")),
            P(("seq", "ctx")),
            P(("seq", "ctx")),
            P(("seq", "ctx"), None),
            P(("seq", "ctx")),
            P(("seq", "ctx"), None),
            P(("seq", "ctx")),
            P(("seq", "ctx")),
            P(("seq", "ctx")),
        ),
        check_vma=False,
    )
```

```python
import functools

import jax
import jax.numpy as jnp
from jax import lax
from jax.experimental import pallas as pl
from jax.experimental.pallas import tpu as pltpu
from jax.sharding import PartitionSpec as P

H = 12
DH = 64


epsilon = 1e-06
root_half = 0.7071067811865476
inv_root_tau = 0.3989422804014327


def matmul(left_side, right_side):
    return jnp.dot(left_side, right_side, preferred_element_type=jnp.float32)


def outer_dot(left_side, right_side):
    return lax.dot_general(
        left_side, right_side, (((0,), (0,)), ((), ())), preferred_element_type=jnp.float32
    )


def back_dot(left_side, right_side):
    return lax.dot_general(
        left_side, right_side, (((1,), (1,)), ((), ())), preferred_element_type=jnp.float32
    )


def forward_norm(values, gain_row, shift_row):
    average = jnp.mean(values, axis=-1, keepdims=True)
    centered = values - average
    spread = jnp.mean(centered * centered, axis=-1, keepdims=True)
    inv_scale = lax.rsqrt(spread + epsilon)
    unit_rows = centered * inv_scale
    return (unit_rows * gain_row + shift_row, unit_rows, inv_scale)


def backward_norm(grad_rows, unit_rows, inv_scale, gain_row):
    scaled = grad_rows * gain_row
    plain_mean = jnp.mean(scaled, axis=-1, keepdims=True)
    cross_mean = jnp.mean(scaled * unit_rows, axis=-1, keepdims=True)
    grad_values = inv_scale * (scaled - plain_mean - unit_rows * cross_mean)
    return (grad_values, jnp.sum(grad_rows * unit_rows, axis=0), jnp.sum(grad_rows, axis=0))


def as_float(weights):
    return tuple((item.astype(jnp.float32) if item.ndim == 1 else item for item in weights))


def forward_pass(token_rows, seg_ids, weights):
    (
        w_query,
        b_query,
        w_key,
        w_value,
        b_value,
        w_output,
        b_output,
        attn_gain,
        attn_shift,
        w_inner,
        b_inner,
        w_outer,
        b_outer,
        ffn_gain,
        ffn_shift,
    ) = as_float(weights)
    tokens = token_rows.shape[0]
    model_width = token_rows.shape[1]
    queries = (matmul(token_rows, w_query) + b_query).astype(jnp.bfloat16)
    key_rows = matmul(token_rows, w_key).astype(jnp.bfloat16)
    value_rows = (matmul(token_rows, w_value) + b_value).astype(jnp.bfloat16)
    seg_low = seg_ids.astype(jnp.bfloat16)
    query_heads = queries.reshape(tokens, H, DH)
    piece_keys = lax.all_gather(key_rows, "ctx", axis=0, tiled=True)
    piece_values = lax.all_gather(value_rows, "ctx", axis=0, tiled=True)
    piece_seg = lax.all_gather(seg_low, "ctx", axis=0, tiled=True)
    piece_len = piece_keys.shape[0]
    row_max = jnp.full((H, tokens), -1e30, jnp.float32)
    weighted = jnp.zeros((tokens, H, DH), jnp.float32)
    scores = (
        jnp.einsum(
            "qhd,khd->hqk",
            query_heads,
            piece_keys.reshape(piece_len, H, DH),
            preferred_element_type=jnp.float32,
        )
        * 0.125
    )
    visible = (seg_low[:, None] == piece_seg[None, :])[None]
    masked = jnp.where(visible, scores, -1e30)
    new_max = jnp.maximum(row_max, jnp.max(masked, axis=-1))
    weights_now = jnp.where(visible, jnp.exp(masked - new_max[:, :, None]), 0.0)
    rescale = jnp.exp(row_max - new_max)
    row_sum = jnp.sum(weights_now, axis=-1)
    added = jnp.einsum(
        "hqk,khd->qhd",
        weights_now.astype(jnp.bfloat16),
        piece_values.reshape(piece_len, H, DH),
        preferred_element_type=jnp.float32,
    )
    weighted = rescale.T[:, :, None] * weighted + added
    row_max, row_sum, weighted = (new_max, row_sum, weighted)
    mixed_full = (weighted / row_sum.T[:, :, None]).reshape(tokens, model_width)
    log_sum = row_max + jnp.log(row_sum)
    mixed = mixed_full.astype(jnp.bfloat16)
    branch = matmul(mixed, w_output) + b_output
    normed, unit_one, inv_one = forward_norm(
        token_rows.astype(jnp.float32) + branch, attn_gain, attn_shift
    )
    normed_low = normed.astype(jnp.bfloat16)
    pre_act = matmul(normed_low, w_inner) + b_inner
    activated = jax.nn.gelu(pre_act, approximate=False).astype(jnp.bfloat16)
    outer_sum = matmul(activated, w_outer) + b_outer
    result, unit_two, inv_two = forward_norm(normed + outer_sum, ffn_gain, ffn_shift)
    kept = (
        token_rows,
        seg_low,
        queries,
        key_rows,
        value_rows,
        mixed_full,
        mixed,
        log_sum,
        unit_one,
        inv_one,
        normed_low,
        pre_act,
        activated,
        unit_two,
        inv_two,
    )
    return (kept, result.astype(jnp.bfloat16))


def backward_pass(tangent, kept, weights):
    (
        w_query,
        b_query,
        w_key,
        w_value,
        b_value,
        w_output,
        b_output,
        attn_gain,
        attn_shift,
        w_inner,
        b_inner,
        w_outer,
        b_outer,
        ffn_gain,
        ffn_shift,
    ) = as_float(weights)
    (
        token_rows,
        seg_low,
        queries,
        key_rows,
        value_rows,
        mixed_full,
        mixed,
        log_sum,
        unit_one,
        inv_one,
        normed_low,
        pre_act,
        activated,
        unit_two,
        inv_two,
    ) = kept
    tokens = token_rows.shape[0]
    model_width = token_rows.shape[1]
    grad_second, grad_ffn_gain, grad_ffn_shift = backward_norm(
        tangent.astype(jnp.float32), unit_two, inv_two, ffn_gain
    )
    grad_outer = grad_second.astype(jnp.bfloat16)
    grad_b_outer = jnp.sum(grad_outer.astype(jnp.float32), axis=0)
    grad_w_outer = outer_dot(activated, grad_outer)
    grad_act = back_dot(grad_outer, w_outer)
    normal_cdf = 0.5 * (1.0 + lax.erf(pre_act * root_half))
    density = jnp.exp(-0.5 * pre_act * pre_act) * inv_root_tau
    grad_pre = (grad_act * (normal_cdf + pre_act * density)).astype(jnp.bfloat16)
    grad_b_inner = jnp.sum(grad_pre.astype(jnp.float32), axis=0)
    grad_w_inner = outer_dot(normed_low, grad_pre)
    grad_normed = grad_second + back_dot(grad_pre, w_inner)
    grad_mid, grad_attn_gain, grad_attn_shift = backward_norm(
        grad_normed, unit_one, inv_one, attn_gain
    )
    grad_branch = grad_mid.astype(jnp.bfloat16)
    grad_b_output = jnp.sum(grad_branch.astype(jnp.float32), axis=0)
    grad_w_output = outer_dot(mixed, grad_branch)
    grad_mixed = back_dot(grad_branch, w_output).astype(jnp.bfloat16)
    mixed_heads = grad_mixed.reshape(tokens, H, DH)
    query_heads = queries.reshape(tokens, H, DH)
    row_dot = jnp.sum(
        grad_mixed.astype(jnp.float32).reshape(tokens, H, DH) * mixed_full.reshape(tokens, H, DH),
        axis=-1,
    ).T
    whole_keys, whole_values, whole_seg = (
        lax.all_gather(key_rows, "ctx", axis=0, tiled=True),
        lax.all_gather(value_rows, "ctx", axis=0, tiled=True),
        lax.all_gather(seg_low, "ctx", axis=0, tiled=True),
    )
    length = whole_keys.shape[0]
    key_block = min(512, length)
    block_count = length // key_block

    def visit(block_index, carry_now):
        offset = block_index * key_block
        block_keys = lax.dynamic_slice_in_dim(whole_keys, offset, key_block, 0).reshape(
            key_block, H, DH
        )
        block_values = lax.dynamic_slice_in_dim(whole_values, offset, key_block, 0).reshape(
            key_block, H, DH
        )
        block_seg = lax.dynamic_slice_in_dim(whole_seg, offset, key_block, 0)
        grad_query_sum, key_terms, value_terms = carry_now
        scores = (
            jnp.einsum("qhd,khd->hqk", query_heads, block_keys, preferred_element_type=jnp.float32)
            * 0.125
        )
        visible = (seg_low[:, None] == block_seg[None, :])[None]
        probs = jnp.where(visible, jnp.exp(scores - log_sum[:, :, None]), 0.0)
        grad_probs = jnp.einsum(
            "qhd,khd->hqk", mixed_heads, block_values, preferred_element_type=jnp.float32
        )
        grad_scores = (probs * (grad_probs - row_dot[:, :, None])).astype(jnp.bfloat16)
        grad_query_sum = grad_query_sum + jnp.einsum(
            "hqk,khd->qhd", grad_scores, block_keys, preferred_element_type=jnp.float32
        )
        key_part = (
            jnp.einsum(
                "hqk,qhd->khd", grad_scores, query_heads, preferred_element_type=jnp.float32
            ).reshape(key_block, model_width)
            * 0.125
        )
        value_part = jnp.einsum(
            "hqk,qhd->khd",
            probs.astype(jnp.bfloat16),
            mixed_heads,
            preferred_element_type=jnp.float32,
        ).reshape(key_block, model_width)
        key_terms = lax.dynamic_update_slice_in_dim(key_terms, key_part, offset, 0)
        value_terms = lax.dynamic_update_slice_in_dim(value_terms, value_part, offset, 0)
        return (grad_query_sum, key_terms, value_terms)

    initial = (
        jnp.zeros((tokens, H, DH), jnp.float32),
        jnp.zeros((length, model_width), jnp.float32),
        jnp.zeros((length, model_width), jnp.float32),
    )
    grad_query_sum, key_terms, value_terms = lax.fori_loop(0, block_count, visit, initial)
    grad_key_sum, grad_value_sum = (
        lax.psum_scatter(
            key_terms.astype(jnp.bfloat16), "ctx", scatter_dimension=0, tiled=True
        ).astype(jnp.float32),
        lax.psum_scatter(
            value_terms.astype(jnp.bfloat16), "ctx", scatter_dimension=0, tiled=True
        ).astype(jnp.float32),
    )
    grad_queries = (grad_query_sum.reshape(tokens, model_width) * 0.125).astype(jnp.bfloat16)
    grad_keys = grad_key_sum.astype(jnp.bfloat16)
    grad_values = grad_value_sum.astype(jnp.bfloat16)
    grad_w_query = outer_dot(token_rows, grad_queries)
    grad_b_query = jnp.sum(grad_queries.astype(jnp.float32), axis=0)
    grad_w_key = outer_dot(token_rows, grad_keys)
    grad_w_value = outer_dot(token_rows, grad_values)
    grad_b_value = jnp.sum(grad_values.astype(jnp.float32), axis=0)
    grad_rows = (
        grad_mid
        + back_dot(grad_queries, w_query)
        + back_dot(grad_keys, w_key)
        + back_dot(grad_values, w_value)
    )
    grads = (
        grad_w_query,
        grad_b_query,
        grad_w_key,
        grad_w_value,
        grad_b_value,
        grad_w_output,
        grad_b_output,
        grad_attn_gain,
        grad_attn_shift,
        grad_w_inner,
        grad_b_inner,
        grad_w_outer,
        grad_b_outer,
        grad_ffn_gain,
        grad_ffn_shift,
    )
    return (grad_rows, grads)


def on_device(
    hidden,
    segment,
    cotangent,
    w_query,
    b_query,
    w_key,
    w_value,
    b_value,
    w_output,
    b_output,
    attn_gain,
    attn_shift,
    w_inner,
    b_inner,
    w_outer,
    b_outer,
    ffn_gain,
    ffn_shift,
):
    micro_count = hidden.shape[0]
    totals = None
    results = []
    input_grads = []
    for micro_index in range(micro_count):
        forward_weights = (
            lax.all_gather(w_query, ("seq", "ctx"), axis=0, tiled=True),
            lax.all_gather(b_query, ("seq", "ctx"), axis=0, tiled=True),
            lax.all_gather(w_key, ("seq", "ctx"), axis=0, tiled=True),
            lax.all_gather(w_value, ("seq", "ctx"), axis=0, tiled=True),
            lax.all_gather(b_value, ("seq", "ctx"), axis=0, tiled=True),
            lax.all_gather(w_output, ("seq", "ctx"), axis=0, tiled=True),
            lax.all_gather(b_output, ("seq", "ctx"), axis=0, tiled=True),
            lax.all_gather(attn_gain, ("seq", "ctx"), axis=0, tiled=True),
            lax.all_gather(attn_shift, ("seq", "ctx"), axis=0, tiled=True),
            lax.all_gather(w_inner, ("seq", "ctx"), axis=0, tiled=True),
            lax.all_gather(b_inner, ("seq", "ctx"), axis=0, tiled=True),
            lax.all_gather(w_outer, ("seq", "ctx"), axis=0, tiled=True),
            lax.all_gather(b_outer, ("seq", "ctx"), axis=0, tiled=True),
            lax.all_gather(ffn_gain, ("seq", "ctx"), axis=0, tiled=True),
            lax.all_gather(ffn_shift, ("seq", "ctx"), axis=0, tiled=True),
        )
        kept, result = forward_pass(hidden[micro_index], segment[micro_index], forward_weights)
        results.append(result)
        backward_weights = (
            lax.all_gather(w_query, ("seq", "ctx"), axis=0, tiled=True),
            lax.all_gather(b_query, ("seq", "ctx"), axis=0, tiled=True),
            lax.all_gather(w_key, ("seq", "ctx"), axis=0, tiled=True),
            lax.all_gather(w_value, ("seq", "ctx"), axis=0, tiled=True),
            lax.all_gather(b_value, ("seq", "ctx"), axis=0, tiled=True),
            lax.all_gather(w_output, ("seq", "ctx"), axis=0, tiled=True),
            lax.all_gather(b_output, ("seq", "ctx"), axis=0, tiled=True),
            lax.all_gather(attn_gain, ("seq", "ctx"), axis=0, tiled=True),
            lax.all_gather(attn_shift, ("seq", "ctx"), axis=0, tiled=True),
            lax.all_gather(w_inner, ("seq", "ctx"), axis=0, tiled=True),
            lax.all_gather(b_inner, ("seq", "ctx"), axis=0, tiled=True),
            lax.all_gather(w_outer, ("seq", "ctx"), axis=0, tiled=True),
            lax.all_gather(b_outer, ("seq", "ctx"), axis=0, tiled=True),
            lax.all_gather(ffn_gain, ("seq", "ctx"), axis=0, tiled=True),
            lax.all_gather(ffn_shift, ("seq", "ctx"), axis=0, tiled=True),
        )
        grad_rows, grads = backward_pass(cotangent[micro_index], kept, backward_weights)
        input_grads.append(grad_rows)
        if totals is None:
            totals = grads
        else:
            totals = jax.tree.map(jnp.add, totals, grads)
    owned = (
        lax.psum_scatter(totals[0], ("seq", "ctx"), scatter_dimension=0, tiled=True),
        lax.psum_scatter(totals[1], ("seq", "ctx"), scatter_dimension=0, tiled=True),
        lax.psum_scatter(totals[2], ("seq", "ctx"), scatter_dimension=0, tiled=True),
        lax.psum_scatter(totals[3], ("seq", "ctx"), scatter_dimension=0, tiled=True),
        lax.psum_scatter(totals[4], ("seq", "ctx"), scatter_dimension=0, tiled=True),
        lax.psum_scatter(totals[5], ("seq", "ctx"), scatter_dimension=0, tiled=True),
        lax.psum_scatter(totals[6], ("seq", "ctx"), scatter_dimension=0, tiled=True),
        lax.psum_scatter(totals[7], ("seq", "ctx"), scatter_dimension=0, tiled=True),
        lax.psum_scatter(totals[8], ("seq", "ctx"), scatter_dimension=0, tiled=True),
        lax.psum_scatter(totals[9], ("seq", "ctx"), scatter_dimension=0, tiled=True),
        lax.psum_scatter(totals[10], ("seq", "ctx"), scatter_dimension=0, tiled=True),
        lax.psum_scatter(totals[11], ("seq", "ctx"), scatter_dimension=0, tiled=True),
        lax.psum_scatter(totals[12], ("seq", "ctx"), scatter_dimension=0, tiled=True),
        lax.psum_scatter(totals[13], ("seq", "ctx"), scatter_dimension=0, tiled=True),
        lax.psum_scatter(totals[14], ("seq", "ctx"), scatter_dimension=0, tiled=True),
    )
    return (jnp.stack(results), jnp.stack(input_grads)) + tuple(owned)


AXES = ("seq", "ctx")
LOG2E = 1.4426950408889634
SCORE_UNIT = 0.125 * LOG2E
HIDDEN_SCORE = -1e30
VMEM_BYTES = 62 << 20
SLAB = 128
WEIGHT = 30


def place_of(index, me):
    mz, mc, my, mx = me
    bx, by, bc, bz = index & 1, (index >> 1) & 1, (index >> 2) & 1, index >> 3
    kx, ky, kz = bx ^ mx, by ^ my, bz ^ mz
    even = bc == 0
    first = jnp.where(even, kx, ky)
    second = jnp.where(even, ky, kx)
    return bc == mc, first, second, kz


def read_me(me_ref):
    return me_ref[0], me_ref[1], me_ref[2], me_ref[3]


def start_load(me, pieces, columns, target, rows, count, sem):
    def body(index, carry):
        own, first, second, kz = place_of(index, me)
        spot = target.at[pl.ds(pl.multiple_of(index * rows, 8), rows), :]
        for number, piece in enumerate(pieces):
            mine = own if number < 2 else jnp.logical_not(own)

            @pl.when(jnp.logical_and(mine, second == number % 2))
            def _(piece=piece):
                source = piece.at[first, kz]
                if columns is not None:
                    source = source.at[:, pl.ds(columns[0], columns[1])]
                pltpu.make_async_copy(source, spot, sem).start()

        return carry

    lax.fori_loop(0, count, body, 0)


def end_load(target, sem):
    pltpu.make_async_copy(target, target, sem).wait()


def store_blocks(me, value_ref, keep_ref, send_ref, first_block, count, rows, column, width):
    def body(step, carry):
        own, first, second, kz = place_of(first_block + step, me)
        value = value_ref[pl.ds(pl.multiple_of(step * rows, 8), rows), :].astype(jnp.bfloat16)

        @pl.when(own)
        def _():
            keep_ref[first, second, kz, :, pl.ds(column, width)] = value

        @pl.when(jnp.logical_not(own))
        def _():
            send_ref[first, second, kz, :, pl.ds(column, width)] = value

        return carry

    lax.fori_loop(0, count, body, 0)


def lanes_of(shape):
    return lax.broadcasted_iota(jnp.int32, shape, len(shape) - 1)


def nn(a, b):
    return jnp.dot(a, b, preferred_element_type=jnp.float32)


def nt(a, b):
    return lax.dot_general(a, b, (((1,), (1,)), ((), ())), preferred_element_type=jnp.float32)


def tn(a, b):
    return lax.dot_general(a, b, (((0,), (0,)), ((), ())), preferred_element_type=jnp.float32)


def row_sum(values):
    return jnp.sum(values, axis=0, keepdims=True)


def pack_kernel(me_ref, hidden_ref, segment_ref, cot_ref, wq_ref, wk_ref, wv_ref, *rest):
    vectors, inner_ref = rest[:8], rest[8]
    out_ref, near_ref, far_ref, cot_near_ref, cot_far_ref = rest[9:]
    rows, width = wq_ref.shape
    out_ref[:, 0:width] = wq_ref[...]
    out_ref[:, width : 2 * width] = wk_ref[...]
    out_ref[:, 2 * width : 3 * width] = wv_ref[...]
    share = inner_ref.shape[1]
    lines = [ref[...].astype(jnp.float32) for ref in vectors]
    lines = [jnp.concatenate([line, jnp.zeros((1, SLAB - rows), jnp.float32)], axis=1) for line in lines]
    last = jnp.concatenate(
        [inner_ref[...].astype(jnp.float32), jnp.zeros((1, SLAB - share), jnp.float32)], axis=1
    )
    slab = jnp.concatenate(lines + [last, jnp.zeros((rows - 9, SLAB), jnp.float32)], axis=0)
    out_ref[:, 3 * width : 3 * width + SLAB] = slab.astype(jnp.bfloat16)
    x = me_ref[3]
    quarter = hidden_ref.shape[1]
    for ref, cotangent, pick in ((near_ref, cot_near_ref, x), (far_ref, cot_far_ref, 1 - x)):
        ref[0:quarter, :] = hidden_ref[pick]
        cotangent[...] = cot_ref[pick]
        both = segment_ref[...].astype(jnp.float32)
        line = jnp.where(pick == 0, both[0:1, :], both[1:2, :]).astype(jnp.bfloat16)
        ref[quarter : quarter + 8, 0:quarter] = jnp.broadcast_to(line, (8, quarter))
        ref[quarter : quarter + 8, quarter:width] = jnp.zeros((8, width - quarter), jnp.bfloat16)


def settle_kernel(me_ref, near_ref, far_ref, out_ref):
    x = me_ref[3]
    out_ref[x] = near_ref[...].astype(out_ref.dtype)
    out_ref[1 - x] = far_ref[...].astype(out_ref.dtype)


def spread_lanes(block, share, offset, tiles, tile):
    lane = lanes_of(block.shape)
    moved = pltpu.roll(block, offset, axis=1) if offset else block
    tiles[tile] = jnp.where(
        jnp.logical_and(lane >= offset, lane < offset + share), moved, tiles[tile]
    )
    if offset + share > 128:
        tiles[tile + 1] = jnp.where(lane < offset + share - 128, moved, tiles[tile + 1])


def project_kernel(
    me_ref, r0, r1, r2, r3, p0, p1, p2, p3,
    q_ref, k_ref, v_ref, vec_ref, bias_ref, x_ref, segrow_ref, segcol_ref, w_ref, slab_ref, sem,
):
    me = read_me(me_ref)
    tokens, width = q_ref.shape
    blocks = 32
    rows = width // blocks
    start_load(me, (p0, p1, p2, p3), None, w_ref, rows, blocks, sem)
    quarter = tokens // 2
    for number, ref in enumerate((r0, r1, r2, r3)):
        span = pl.ds(number * quarter, quarter)
        x_ref[span, :] = ref[0:quarter, :]
        line = ref[quarter : quarter + 8, 0:quarter].astype(jnp.float32)
        segrow_ref[:, span] = line
        segcol_ref[span, :] = jnp.broadcast_to(line[0:1, :], (128, quarter)).T
    end_load(w_ref, sem)
    slab_ref[...] = w_ref[:, 3 * width : 3 * width + SLAB].astype(jnp.float32)
    tiles = [jnp.zeros((8, 128), jnp.float32) for _ in range(width // 128 + 1)]
    for index in range(blocks):
        start = rows * index
        spread_lanes(slab_ref[start : start + 8, :], rows, start % 128, tiles, start // 128)
    vectors = jnp.concatenate(tiles[: width // 128], axis=1)
    vec_ref[...] = vectors
    share = bias_ref.shape[1] // blocks
    tiles = [jnp.zeros((8, 128), jnp.float32) for _ in range(4)]
    for turn in range(4):
        lines = slab_ref[pl.ds(rows * turn + 8, 8, stride=4 * rows), :]
        spread_lanes(lines, share, share * turn % 128, tiles, share * turn // 128)
    for group in range(8):
        for tile in range(3):
            bias_ref[0:1, pl.ds(group * 384 + tile * 128, 128)] = tiles[tile][group : group + 1, :]
    b_query, b_value = vectors[0:1, :], vectors[1:2, :]
    q_ref[...] = (nn(x_ref[0:tokens, :], w_ref[:, 0:width]) + b_query).astype(jnp.bfloat16)

    @pl.loop(0, 2)
    def _(part):
        span = pl.ds(pl.multiple_of(part * tokens, tokens), tokens)
        k_ref[span, :] = nn(x_ref[span, :], w_ref[:, width : 2 * width]).astype(jnp.bfloat16)
        v_ref[span, :] = (nn(x_ref[span, :], w_ref[:, 2 * width : 3 * width]) + b_value).astype(
            jnp.bfloat16
        )


def attend_kernel(q_ref, k_ref, v_ref, segcol_ref, segrow_ref, mixed_ref, lse_ref, bias_ref):
    tokens = q_ref.shape[0]
    keys = k_ref.shape[0]
    tile = 256

    @pl.when(pl.program_id(0) == 0)
    def _():
        visible = segcol_ref[0:tokens, 0:1] == segrow_ref[0:1, :]
        bias_ref[...] = jnp.where(visible, 0.0, HIDDEN_SCORE)

    low_half = lanes_of((1, 128)) < 64
    key_rows = k_ref[...]
    value_rows = v_ref[...]
    one = jnp.ones((), jnp.bfloat16)
    zero = jnp.zeros((), jnp.bfloat16)
    for part in range(tokens // tile):
        span = pl.ds(part * tile, tile)
        query = q_ref[span, :]
        bias = bias_ref[span, :]
        outs, sums = [], []
        for head in range(2):
            mine = low_half if head == 0 else jnp.logical_not(low_half)
            scores = nt(jnp.where(mine, query, zero), key_rows) + bias
            top = jnp.max(scores, axis=-1, keepdims=True)
            weights = jnp.exp2((scores - top) * SCORE_UNIT).astype(jnp.bfloat16)
            product = nn(weights, jnp.where(mine, value_rows, one))
            total = product[:, 64:65] if head == 0 else product[:, 0:1]
            outs.append(product / total)
            sums.append(top * SCORE_UNIT + jnp.log2(total))
        mixed_ref[span, :] = jnp.where(low_half, outs[0], outs[1])
        lane = lanes_of((tile, 128))
        both = jnp.where(lane == 0, sums[0], jnp.where(lane == 1, sums[1], 0.0))
        lse_ref[0, :, span] = both.T[0:8, :]


def attend_back_kernel(
    together, q_ref, k_ref, v_ref, gm_ref, mixed_ref, lse_ref, segcol_ref, segrow_ref,
    dq_ref, dk_ref, dv_ref, bias_ref,
):
    tokens = q_ref.shape[0]
    keys = k_ref.shape[0]
    tile = 256

    @pl.when(pl.program_id(0) == 0)
    def _():
        visible = segcol_ref[:, 0:1] == segrow_ref[0:1, 0:tokens]
        bias_ref[...] = jnp.where(visible, 0.0, HIDDEN_SCORE)

    low_half = lanes_of((1, 128)) < 64
    zero = jnp.zeros((), jnp.bfloat16)
    query = q_ref[...]
    grad = gm_ref[...]
    product = (grad.astype(jnp.float32) * mixed_ref[...]).T
    row_dots = [row_sum(product[0:64, :]), row_sum(product[64:128, :])]
    masks = (low_half, jnp.logical_not(low_half))
    queries = [jnp.where(mine, query, zero) for mine in masks]
    grads = [jnp.where(mine, grad, zero) for mine in masks]
    def body(turn, grad_query):
        for step in range(together):
            span = pl.ds(pl.multiple_of((together * turn + step) * tile, tile), tile)
            key_rows = k_ref[span, :]
            value_rows = v_ref[span, :]
            bias = bias_ref[span, :]
            grad_key = jnp.zeros((tile, 128), jnp.float32)
            grad_value = jnp.zeros((tile, 128), jnp.float32)
            for head in range(2):
                scores = nt(key_rows, queries[head])
                probs = jnp.exp2(scores * SCORE_UNIT + (bias - lse_ref[0, head : head + 1, :]))
                grad_probs = nt(value_rows, grads[head])
                grad_scores = (probs * (grad_probs - row_dots[head])).astype(jnp.bfloat16)
                grad_key = grad_key + nn(grad_scores, queries[head])
                grad_value = grad_value + nn(probs.astype(jnp.bfloat16), grads[head])
                grad_query = grad_query + tn(grad_scores, jnp.where(masks[head], key_rows, zero))
            dk_ref[span, :] = (grad_key * 0.125).astype(jnp.bfloat16)
            dv_ref[span, :] = grad_value.astype(jnp.bfloat16)
        return grad_query

    grad_query = jnp.zeros((tokens, 128), jnp.float32)
    turns = keys // tile // together
    grad_query = body(0, grad_query) if turns == 1 else lax.fori_loop(0, turns, body, grad_query)
    dq_ref[...] = (grad_query * 0.125).astype(jnp.bfloat16)


def normalize(values):
    average = jnp.mean(values, axis=-1, keepdims=True)
    centered = values - average
    spread = jnp.mean(centered * centered, axis=-1, keepdims=True)
    inverse = lax.rsqrt(spread + epsilon)
    return centered * inverse, inverse


def normalize_back(grad, unit, inverse, gain):
    scaled = grad * gain
    plain = jnp.mean(scaled, axis=-1, keepdims=True)
    cross = jnp.mean(scaled * unit, axis=-1, keepdims=True)
    return inverse * (scaled - plain - unit * cross)


def feed_in_kernel(
    me_ref, mixed_a_ref, mixed_b_ref, x_ref, vec_ref, bias_ref, a0, a1, a2, a3,
    low_ref, act_ref, slope_ref, unit_ref, inverse_ref, rest_ref, wo_ref, wi_ref, sem_o, sem_i,
):
    me = read_me(me_ref)
    tokens, width = low_ref.shape
    inner = wi_ref.shape[1]
    blocks = 32
    start_load(me, (a0, a1, a2, a3), (0, width), wo_ref, width // blocks, blocks, sem_o)
    start_load(me, (a0, a1, a2, a3), (width, inner), wi_ref, width // blocks, blocks, sem_i)
    b_output, attn_gain, attn_shift = vec_ref[2:3, :], vec_ref[3:4, :], vec_ref[4:5, :]
    b_outer = vec_ref[5:6, :]
    end_load(wo_ref, sem_o)
    part = mixed_a_ref.shape[1]
    branch = b_output + nn(mixed_a_ref[...].astype(jnp.bfloat16), wo_ref[0:part, :])
    branch = branch + nn(mixed_b_ref[...].astype(jnp.bfloat16), wo_ref[part:width, :])
    unit_one, inverse_one = normalize(x_ref[0:tokens, :].astype(jnp.float32) + branch)
    normed = unit_one * attn_gain + attn_shift
    unit_ref[...] = unit_one
    inverse_ref[...] = jnp.broadcast_to(inverse_one, inverse_ref.shape)
    low_ref[...] = normed.astype(jnp.bfloat16)
    rest_ref[...] = normed + b_outer
    end_load(wi_ref, sem_i)
    step = 512

    @pl.loop(0, inner // step)
    def _(turn):
        span = pl.ds(pl.multiple_of(turn * step, step), step)
        pre_act = nn(low_ref[...], wi_ref[:, span]) + bias_ref[0:1, span]
        normal_cdf = 0.5 * (1.0 + lax.erf(pre_act * root_half))
        density = jnp.exp(-0.5 * pre_act * pre_act) * inv_root_tau
        act_ref[:, span] = (pre_act * normal_cdf).astype(jnp.bfloat16)
        slope_ref[:, span] = (normal_cdf + pre_act * density).astype(jnp.bfloat16)


def feed_out_kernel(
    me_ref, act_ref, rest_ref, cot_near_ref, cot_far_ref, vec_ref, b0, b1, b2, b3,
    near_ref, far_ref, second_ref, outer_ref, sums_ref, keep_ref, send_ref,
    wu_ref, grad_ref, sem_u,
):
    me = read_me(me_ref)
    tokens, width = rest_ref.shape
    inner = act_ref.shape[1]
    blocks = 32
    rows = inner // blocks
    quarter = tokens // 2
    start_load(me, (b0, b1, b2, b3), None, wu_ref, rows, blocks, sem_u)
    ffn_gain, ffn_shift = vec_ref[6:7, :], vec_ref[7:8, :]
    end_load(wu_ref, sem_u)

    @pl.loop(0, 2)
    def _(part):
        span = pl.ds(pl.multiple_of(part * quarter, quarter), quarter)
        second_ref[span, :] = rest_ref[span, :] + nn(act_ref[span, :], wu_ref[...])

    sums = [jnp.zeros((1, width), jnp.float32) for _ in range(3)]
    for part in range(2):
        span = pl.ds(part * quarter, quarter)
        unit_two, inverse_two = normalize(second_ref[span, :])
        out_ref, cot_ref = ((near_ref, cot_near_ref), (far_ref, cot_far_ref))[part]
        out_ref[...] = (unit_two * ffn_gain + ffn_shift).astype(jnp.bfloat16)
        tangent = cot_ref[...].astype(jnp.float32)
        second = normalize_back(tangent, unit_two, inverse_two, ffn_gain)
        second_ref[span, :] = second
        outer = second.astype(jnp.bfloat16)
        outer_ref[span, :] = outer
        sums[0] = sums[0] + row_sum(outer.astype(jnp.float32))
        sums[1] = sums[1] + row_sum(tangent * unit_two)
        sums[2] = sums[2] + row_sum(tangent)
    sums_ref[...] = jnp.concatenate(sums + [jnp.zeros((5, width), jnp.float32)], axis=0)
    half = width // 2

    @pl.loop(0, inner // half)
    def _(turn):
        cols = pl.ds(pl.multiple_of(turn * half, half), half)
        grad_ref[...] = tn(act_ref[:, cols], outer_ref[...])
        store_blocks(
            me, grad_ref, keep_ref, send_ref, turn * (half // rows), half // rows, rows, 0, width
        )


def slope_kernel(
    me_ref, slope_ref, outer_ref, b0, b1, b2, b3, pre_ref, bsum_ref, wu_ref, sem_u
):
    me = read_me(me_ref)
    inner = slope_ref.shape[1]
    blocks = 32
    start_load(me, (b0, b1, b2, b3), None, wu_ref, inner // blocks, blocks, sem_u)
    end_load(wu_ref, sem_u)
    step = 512

    @pl.loop(0, inner // step)
    def _(turn):
        span = pl.ds(pl.multiple_of(turn * step, step), step)
        grad_act = nt(outer_ref[...], wu_ref[span, :])
        grad_pre = (grad_act * slope_ref[:, span].astype(jnp.float32)).astype(jnp.bfloat16)
        bsum_ref[0:1, span] = row_sum(grad_pre.astype(jnp.float32))
        pre_ref[:, span] = grad_pre


def feed_back_kernel(
    me_ref, pre_ref, second_ref, low_ref, unit_ref, inverse_ref, mixed_a_ref, mixed_b_ref, vec_ref,
    a0, a1, a2, a3,
    mid_ref, gm_ref, sums_ref, keep_ref, send_ref,
    wo_ref, wi_ref, grad_ref, sem_o, sem_i,
):
    me = read_me(me_ref)
    tokens, width = second_ref.shape
    inner = wi_ref.shape[1]
    blocks = 32
    rows = width // blocks
    start_load(me, (a0, a1, a2, a3), (width, inner), wi_ref, rows, blocks, sem_i)
    start_load(me, (a0, a1, a2, a3), (0, width), wo_ref, rows, blocks, sem_o)
    step = 512

    @pl.loop(0, inner // step)
    def _(turn):
        first = pl.multiple_of(turn * step, step)
        grad_ref[:, 0:step] = tn(low_ref[...], pre_ref[:, pl.ds(first, step)])
        store_blocks(
            me, grad_ref.at[:, 0:step], keep_ref, send_ref, 0, blocks, rows,
            pl.multiple_of(width + first, 128), step,
        )

    end_load(wi_ref, sem_i)

    @pl.loop(0, 2)
    def _(part):
        span = pl.ds(pl.multiple_of(part * (tokens // 2), tokens // 2), tokens // 2)
        mid_ref[span, :] = second_ref[span, :] + nt(pre_ref[span, :], wi_ref[...])

    end_load(wo_ref, sem_o)
    attn_gain = vec_ref[3:4, :]
    grad_normed = mid_ref[...]
    unit = unit_ref[...]
    mid = normalize_back(grad_normed, unit, inverse_ref[:, 0:1], attn_gain)
    mid_ref[...] = mid
    branch = mid.astype(jnp.bfloat16)
    sums_ref[...] = jnp.zeros(sums_ref.shape, jnp.float32)
    sums_ref[0:1, :] = row_sum(branch.astype(jnp.float32))
    sums_ref[1:2, :] = row_sum(grad_normed * unit)
    sums_ref[2:3, :] = row_sum(grad_normed)
    gm_ref[...] = nt(branch, wo_ref[...]).astype(jnp.bfloat16)
    part = mixed_a_ref.shape[1]
    grad_ref[0:part, :] = tn(mixed_a_ref[...].astype(jnp.bfloat16), branch)
    grad_ref[part:width, :] = tn(mixed_b_ref[...].astype(jnp.bfloat16), branch)
    store_blocks(me, grad_ref, keep_ref, send_ref, 0, blocks, rows, 0, width)


def weight_kernel(
    me_ref, x_ref, dqa_ref, dka_ref, dva_ref, dqb_ref, dkb_ref, dvb_ref,
    sums_two_ref, sums_one_ref, bsum_ref, keep_ref, send_ref, grad_ref, slab_ref,
):
    me = read_me(me_ref)
    tokens, half = dqa_ref.shape
    width = 2 * half
    blocks = 32
    rows = width // blocks
    refs = (dqa_ref, dqb_ref, dka_ref, dkb_ref, dva_ref, dvb_ref)
    for number, ref in enumerate(refs):
        grad_ref[...] = tn(x_ref[0 : ref.shape[0], :], ref[...])
        store_blocks(me, grad_ref, keep_ref, send_ref, 0, blocks, rows, number * half, half)

    def sums(first, second):
        return jnp.concatenate(
            [row_sum(first[...].astype(jnp.float32)), row_sum(second[...].astype(jnp.float32))],
            axis=1,
        )

    vectors = jnp.concatenate(
        [
            sums(dqa_ref, dqb_ref),
            sums(dva_ref, dvb_ref),
            sums_one_ref[0:3, :],
            sums_two_ref[0:3, :],
        ],
        axis=0,
    )
    share = bsum_ref.shape[1] // blocks
    lane = lanes_of((8, 128))
    slab_ref[...] = jnp.zeros(slab_ref.shape, jnp.float32)
    for index in range(blocks):
        tile, offset = rows * index // 128, rows * index % 128
        piece = vectors[:, tile * 128 : tile * 128 + 128]
        if offset + rows > 128:
            piece = jnp.where(
                lane >= offset, piece, vectors[:, tile * 128 + 128 : tile * 128 + 256]
            )
        moved = pltpu.roll(piece, (128 - offset) % 128, axis=1) if offset else piece
        slab_ref[rows * index : rows * index + 8, :] = jnp.where(lane < rows, moved, 0.0)
    groups = jnp.concatenate([bsum_ref[0:1, pl.ds(384 * g, 384)] for g in range(8)], axis=0)
    for turn in range(4):
        tile, offset = share * turn // 128, share * turn % 128
        piece = groups[:, tile * 128 : tile * 128 + 128]
        if offset + share > 128:
            piece = jnp.where(lane >= offset, piece, groups[:, tile * 128 + 128 : tile * 128 + 256])
        moved = pltpu.roll(piece, (128 - offset) % 128, axis=1) if offset else piece
        slab_ref[pl.ds(rows * turn + 8, 8, stride=4 * rows), :] = jnp.where(lane < share, moved, 0.0)
    store_blocks(me, slab_ref, keep_ref, send_ref, 0, blocks, rows, 3 * width, SLAB)


def input_kernel(
    me_ref, mid_ref, dqa_ref, dka_ref, dva_ref, dqb_ref, dkb_ref, dvb_ref, other_ref,
    p0, p1, p2, p3, near_ref, far_ref, w_ref, sem,
):
    me = read_me(me_ref)
    tokens, width = mid_ref.shape
    half = width // 2
    blocks = 32
    start_load(me, (p0, p1, p2, p3), (0, 3 * width), w_ref, width // blocks, blocks, sem)
    own = []
    for number, ref in enumerate((dka_ref, dva_ref, dkb_ref, dvb_ref)):
        theirs = other_ref[:, number * half : (number + 1) * half].astype(jnp.float32)
        own.append((ref[0:tokens, :].astype(jnp.float32) + theirs).astype(jnp.bfloat16))
    end_load(w_ref, sem)
    total = mid_ref[...]
    for number, value in enumerate((dqa_ref[...], dqb_ref[...], own[0], own[2], own[1], own[3])):
        total = total + nt(value, w_ref[:, number * half : (number + 1) * half])
    low = total.astype(jnp.bfloat16)
    near_ref[...] = low[: tokens // 2]
    far_ref[...] = low[tokens // 2 :]


def shape_of(shape, dtype):
    return jax.ShapeDtypeStruct(shape, dtype)


def call(kernel, name, out_shape, kinds, scratch, flops, moved):
    spaces = {"s": pltpu.SMEM, "v": pltpu.VMEM, "a": pl.ANY}
    return pl.pallas_call(
        kernel,
        name=name,
        out_shape=out_shape,
        in_specs=[pl.BlockSpec(memory_space=spaces[kind]) for kind in kinds],
        scratch_shapes=scratch,
        compiler_params=pltpu.CompilerParams(vmem_limit_bytes=VMEM_BYTES),
        cost_estimate=pl.CostEstimate(
            flops=WEIGHT * flops, bytes_accessed=WEIGHT * moved, transcendentals=0
        ),
    )


def tie(*values):
    return lax.optimization_barrier(values)


def fast_device(depth, hidden, segment, cotangent, *weights):
    (
        w_query, b_query, w_key, w_value, b_value, w_output, b_output, attn_gain, attn_shift,
        w_inner, b_inner, w_outer, b_outer, ffn_gain, ffn_shift,
    ) = weights
    bf16, f32 = jnp.bfloat16, jnp.float32
    quarter, width = hidden.shape[1], hidden.shape[2]
    tokens = 2 * quarter
    keys = 2 * tokens
    rows = w_query.shape[0]
    inner = w_inner.shape[1]
    inner_rows = w_outer.shape[0]
    seq_index, ctx_index = lax.axis_index("seq"), lax.axis_index("ctx")
    me = jnp.stack([seq_index >> 1, seq_index & 1, ctx_index >> 1, ctx_index & 1]).astype(jnp.int32)

    def table(move):
        pairs = []
        for bz in range(depth):
            for bc in range(2):
                for by in range(2):
                    for bx in range(2):
                        tz, tc, ty, tx = move(bz, bc, by, bx)
                        pairs.append(
                            (((bz * 2 + bc) * 2 + by) * 2 + bx, ((tz * 2 + tc) * 2 + ty) * 2 + tx)
                        )
        return pairs

    along_z = [table(lambda a, b, d, e, k=k: (a ^ k, b, d, e)) for k in range(1, depth)]
    plane_one = table(lambda a, b, d, e: (a, b, d, 1 - e) if b == 0 else (a, b, 1 - d, e))
    plane_two = table(lambda a, b, d, e: (a, b, 1 - d, e) if b == 0 else (a, b, d, 1 - e))
    partner = table(lambda a, b, d, e: (a, 1 - b, d, e))
    home_near = table(lambda a, b, d, e: (a, d, b, e))
    home_far = table(lambda a, b, d, e: (a, d, b, 1 - e))

    def hop(value, pairs):
        return lax.ppermute(value, AXES, pairs)

    def hops_z(value):
        return [hop(value, pairs) for pairs in along_z]

    sem = pltpu.SemaphoreType.DMA
    flat = 2 * tokens * width
    slabbed = 3 * width + SLAB

    vectors_in = (
        b_query, b_value, b_output, attn_gain, attn_shift, b_outer, ffn_gain, ffn_shift, b_inner,
    )
    packed_row = shape_of((quarter + 8, width), bf16)
    plain_row = shape_of((quarter, width), bf16)
    first_in, near, far, cot_near, cot_far = call(
        pack_kernel,
        "pack",
        (shape_of((rows, slabbed), bf16), packed_row, packed_row, plain_row, plain_row),
        "s" + "v" * 15,
        [],
        1,
        1 << 20,
    )(
        me, hidden, segment, cotangent, w_query, w_key, w_value,
        *[vector[None, :] for vector in vectors_in],
    )
    near, far = hop(near, home_near), hop(far, home_far)
    second_in = jnp.concatenate([w_output, w_inner], axis=1)
    climbed, near, far, second_in = tie(hops_z(first_in), near, far, second_in)
    levels_one = jnp.stack([first_in, *climbed])
    got_one = hop(levels_one, plane_one)
    near_other, far_other = hop(near, partner), hop(far, partner)
    second_one = hop(second_in, along_z[0])
    got_one, near_other, far_other, second_one, second_in = tie(
        got_one, near_other, far_other, second_one, second_in
    )
    half_one = jnp.stack([levels_one, got_one])
    other_one = hop(half_one, plane_two)
    half_one_p = hop(half_one, partner)
    second_two = hop(second_in, along_z[1])
    other_one, half_one_p, second_two, second_in, third_in, cot_near, cot_far = tie(
        other_one, half_one_p, second_two, second_in, w_outer, cot_near, cot_far
    )
    other_one_p = hop(other_one, partner)
    cot_near, cot_far = hop(cot_near, home_near), hop(cot_far, home_far)
    second_three = hop(second_in, along_z[2])
    third_one, third_two = hop(third_in, along_z[0]), hop(third_in, along_z[1])
    group_one = (half_one, other_one, half_one_p, other_one_p)

    q, k, v, vectors, bias, x_all, segrow, segcol = call(
        project_kernel,
        "project",
        (
            shape_of((tokens, width), bf16),
            shape_of((keys, width), bf16),
            shape_of((keys, width), bf16),
            shape_of((8, width), f32),
            shape_of((1, inner), f32),
            shape_of((keys, width), bf16),
            shape_of((8, keys), f32),
            shape_of((keys, 128), f32),
        ),
        "svvvvaaaa",
        [pltpu.VMEM((width, slabbed), bf16), pltpu.VMEM((width, SLAB), f32), sem],
        5 * flat * width,
        10 << 20,
    )(me, near, far, near_other, far_other, *group_one)

    q, second_three, third_one, third_two, cot_near, cot_far, third_in = tie(
        q, second_three, third_one, third_two, cot_near, cot_far, third_in
    )
    levels_two = jnp.stack([second_in, second_one, second_two, second_three])
    got_two = hop(levels_two, plane_one)
    third_three = hop(third_in, along_z[2])

    parts = 2
    pairs_now = width // 128 // parts
    params = pltpu.CompilerParams(vmem_limit_bytes=VMEM_BYTES)

    def attend(part):
        def column(count):
            return pl.BlockSpec((count, 128), lambda i: (0, i + part * pairs_now))

        def column_out(count):
            return pl.BlockSpec((count, 128), lambda i: (0, i))

        def whole(shape):
            return pl.BlockSpec(shape, lambda i: (0, 0))

        return pl.pallas_call(
            attend_kernel,
            name="attend",
            grid=(pairs_now,),
            out_shape=(
                shape_of((tokens, pairs_now * 128), f32),
                shape_of((pairs_now, 8, tokens), f32),
            ),
            in_specs=[
                column(tokens), column(keys), column(keys), whole((keys, 128)), whole((8, keys)),
            ],
            out_specs=(column_out(tokens), pl.BlockSpec((1, 8, tokens), lambda i: (i, 0, 0))),
            scratch_shapes=[pltpu.VMEM((tokens, keys), f32)],
            compiler_params=params,
            cost_estimate=pl.CostEstimate(
                flops=WEIGHT * 8 * tokens * keys * width // parts, bytes_accessed=WEIGHT << 22, transcendentals=0
            ),
        )

    mixed_a, lse_a = attend(0)(q, k, v, segcol, segrow)
    levels_three = jnp.stack([third_in, third_one, third_two, third_three])
    half_two = jnp.stack([levels_two, got_two])
    q_b, mixed_a, half_two, levels_three = tie(q, mixed_a, half_two, levels_three)
    other_two = hop(half_two, plane_two)
    half_two_p = hop(half_two, partner)
    got_three = hop(levels_three, plane_one)
    mixed_b, lse_b = attend(1)(q_b, k, v, segcol, segrow)
    half_three = jnp.stack([levels_three, got_three])
    mixed_b, other_two, half_three = tie(mixed_b, other_two, half_three)
    other_two_p = hop(other_two, partner)
    group_two = (half_two, other_two, half_two_p, other_two_p)
    other_three = hop(half_three, plane_two)
    half_three_p = hop(half_three, partner)

    low, act, slope, unit, inverse, rest = call(
        feed_in_kernel,
        "feed_in",
        (
            shape_of((tokens, width), bf16),
            shape_of((tokens, inner), bf16),
            shape_of((tokens, inner), bf16),
            shape_of((tokens, width), f32),
            shape_of((tokens, 128), f32),
            shape_of((tokens, width), f32),
        ),
        "svvvvvaaaa",
        [pltpu.VMEM((width, width), bf16), pltpu.VMEM((width, inner), bf16), sem, sem],
        flat * (width + inner),
        20 << 20,
    )(me, mixed_a, mixed_b, x_all, vectors, bias, *group_two)

    act, other_three = tie(act, other_three)
    other_three_p = hop(other_three, partner)
    group_three = (half_three, other_three, half_three_p, other_three_p)
    near_out, far_out, second, outer, sums_two, keep_three, send_three = call(
        feed_out_kernel,
        "feed_out",
        (
            plain_row,
            plain_row,
            shape_of((tokens, width), f32),
            shape_of((tokens, width), bf16),
            shape_of((8, width), f32),
            shape_of((2, 2, depth, inner_rows, width), bf16),
            shape_of((2, 2, depth, inner_rows, width), bf16),
        ),
        "svvvvvaaaa",
        [pltpu.VMEM((inner, width), bf16), pltpu.VMEM((width // 2, width), f32), sem],
        2 * flat * inner,
        20 << 20,
    )(me, act, rest, cot_near, cot_far, vectors, *group_three)

    got = hop(send_three, partner)
    near_out, far_out = hop(near_out, home_near), hop(far_out, home_far)

    grad_pre, bias_sums = call(
        slope_kernel,
        "slope",
        (shape_of((tokens, inner), bf16), shape_of((1, inner), f32)),
        "svvaaaa",
        [pltpu.VMEM((inner, width), bf16), sem],
        flat * inner,
        16 << 20,
    )(me, slope, outer, *group_three)

    def first_sum(keep, got):
        return keep[1] + got[1], keep[0] + got[0]

    def second_sum(kept, got):
        return kept[1] + got[1], kept[0] + got[0]

    def last_sum(levels, arrived):
        total = levels[0].astype(f32)
        for value in arrived:
            total = total + value.astype(f32)
        return total

    def climb(levels):
        return [hop(levels[k + 1], pairs) for k, pairs in enumerate(along_z)]

    three_send, three_kept = first_sum(keep_three, got)
    grad_pre, three_send, three_kept, near_out, far_out = tie(
        grad_pre, three_send, three_kept, near_out, far_out
    )
    three_got = hop(three_send, plane_one)

    mid, grad_mixed, sums_one, keep_two, send_two = call(
        feed_back_kernel,
        "feed_back",
        (
            shape_of((tokens, width), f32),
            shape_of((tokens, width), bf16),
            shape_of((8, width), f32),
            shape_of((2, 2, depth, rows, width + inner), bf16),
            shape_of((2, 2, depth, rows, width + inner), bf16),
        ),
        "svvvvvvvvaaaa",
        [
            pltpu.VMEM((width, width), bf16),
            pltpu.VMEM((width, inner), bf16),
            pltpu.VMEM((width, width), f32),
            sem, sem,
        ],
        flat * (2 * inner + 2 * width),
        30 << 20,
    )(me, grad_pre, second, low, unit, inverse, mixed_a, mixed_b, vectors, *group_two)

    two_got = hop(send_two, partner)
    three_send, three_kept = three_kept[1] + three_got[1], three_kept[0] + three_got[0]
    grad_mixed, three_send, three_kept = tie(grad_mixed, three_send, three_kept)
    three_got = hop(three_send, plane_two)

    def attend_back(part):
        def column(count):
            return pl.BlockSpec((count, 128), lambda i: (0, i + part * pairs_now))

        def column_out(count):
            return pl.BlockSpec((count, 128), lambda i: (0, i))

        def whole(shape):
            return pl.BlockSpec(shape, lambda i: (0, 0))

        return pl.pallas_call(
            functools.partial(attend_back_kernel, 2 + 2 * part),
            name="attend_back",
            grid=(pairs_now,),
            out_shape=(
                shape_of((tokens, pairs_now * 128), bf16),
                shape_of((keys, pairs_now * 128), bf16),
                shape_of((keys, pairs_now * 128), bf16),
            ),
            in_specs=[
                column(tokens), column(keys), column(keys), column(tokens), column_out(tokens),
                pl.BlockSpec((1, 8, tokens), lambda i: (i, 0, 0)),
                whole((keys, 128)), whole((8, keys)),
            ],
            out_specs=(column_out(tokens), column_out(keys), column_out(keys)),
            scratch_shapes=[pltpu.VMEM((keys, tokens), f32)],
            compiler_params=params,
            cost_estimate=pl.CostEstimate(
                flops=WEIGHT * 20 * tokens * keys * width // parts, bytes_accessed=WEIGHT << 22, transcendentals=0
            ),
        )

    back_a = attend_back(0)(q, k, v, grad_mixed, mixed_a, lse_a, segcol, segrow)

    three_levels = three_kept + three_got
    two_send, two_kept = first_sum(keep_two, two_got)
    back_a, three_levels, two_send, two_kept, grad_mixed_b = tie(
        back_a, three_levels, two_send, two_kept, grad_mixed
    )
    three_climb = climb(three_levels)
    two_got = hop(two_send, plane_one)

    back_b = attend_back(1)(q, k, v, grad_mixed_b, mixed_b, lse_b, segcol, segrow)

    total_three = last_sum(three_levels, three_climb)
    two_send, two_kept = second_sum(two_kept, two_got)
    back_b, total_three, two_send, two_kept = tie(back_b, total_three, two_send, two_kept)
    two_got = hop(two_send, plane_two)
    from_partner = hop(
        jnp.concatenate([value[tokens:] for value in back_a[1:] + back_b[1:]], axis=1), partner
    )

    keep_one, send_one = call(
        weight_kernel,
        "weight",
        (
            shape_of((2, 2, depth, rows, slabbed), bf16),
            shape_of((2, 2, depth, rows, slabbed), bf16),
        ),
        "svvvvvvvvvv",
        [pltpu.VMEM((width, width // 2), f32), pltpu.VMEM((width, SLAB), f32)],
        5 * flat * width,
        12 << 20,
    )(me, x_all, *back_a, *back_b, sums_two, sums_one, bias_sums)

    one_got = hop(send_one, partner)
    keep_one, two_levels = tie(keep_one, two_kept + two_got)
    two_climb = climb(two_levels)
    one_send, one_kept = first_sum(keep_one, one_got)
    mid, one_send, one_kept = tie(mid, one_send, one_kept)
    one_got = hop(one_send, plane_one)

    near_in, far_in = call(
        input_kernel,
        "input",
        (plain_row, plain_row),
        "svvvvvvvvaaaa",
        [pltpu.VMEM((width, 3 * width), bf16), sem],
        3 * flat * width,
        12 << 20,
    )(me, mid, *back_a, *back_b, from_partner, *group_one)

    one_got, near_in, far_in = tie(one_got, near_in, far_in)
    one_send, one_kept = second_sum(one_kept, one_got)
    one_got = hop(one_send, plane_two)
    near_in = hop(near_in, home_near)
    total_two = last_sum(two_levels, two_climb)
    one_levels = one_kept + one_got
    one_levels, near_in, far_in, total_two, near_out, far_out = tie(
        one_levels, near_in, far_in, total_two, near_out, far_out
    )
    far_in = hop(far_in, home_far)
    one_climb = climb(one_levels)

    def settle(first, second, dtype):
        return call(
            settle_kernel, "settle", shape_of((2, quarter, width), dtype), "svv", [], 1, 2 << 20
        )(me, first, second)

    result = settle(near_out, far_out, bf16)
    far_in, result = tie(far_in, result)
    grad_input = settle(near_in, far_in, f32)
    total_one = last_sum(one_levels, one_climb)
    vector = [total_one[j, 3 * width : 3 * width + rows] for j in range(8)]
    grad_b_inner = total_one[8, 3 * width : 3 * width + inner_rows]
    return (
        result,
        grad_input,
        total_one[:, :width],
        vector[0],
        total_one[:, width : 2 * width],
        total_one[:, 2 * width : 3 * width],
        vector[1],
        total_two[:, :width],
        vector[2],
        vector[3],
        vector[4],
        total_two[:, width:],
        grad_b_inner,
        total_three,
        vector[5],
        vector[6],
        vector[7],
    )


def takes_fast(mesh):
    seq, ctx = mesh.shape["seq"], mesh.shape["ctx"]
    return ctx == 4 and seq == 8


def solution(mesh):
    return jax.shard_map(
        functools.partial(fast_device, mesh.shape["seq"] // 2) if takes_fast(mesh) else on_device,
        mesh=mesh,
        in_specs=(
            P("seq", "ctx", None),
            P("seq", "ctx"),
            P("seq", "ctx", None),
            P(("seq", "ctx"), None),
            P(("seq", "ctx")),
            P(("seq", "ctx"), None),
            P(("seq", "ctx"), None),
            P(("seq", "ctx")),
            P(("seq", "ctx"), None),
            P(("seq", "ctx")),
            P(("seq", "ctx")),
            P(("seq", "ctx")),
            P(("seq", "ctx"), None),
            P(("seq", "ctx")),
            P(("seq", "ctx"), None),
            P(("seq", "ctx")),
            P(("seq", "ctx")),
            P(("seq", "ctx")),
        ),
        out_specs=(
            P("seq", "ctx", None),
            P("seq", "ctx", None),
            P(("seq", "ctx"), None),
            P(("seq", "ctx")),
            P(("seq", "ctx"), None),
            P(("seq", "ctx"), None),
            P(("seq", "ctx")),
            P(("seq", "ctx"), None),
            P(("seq", "ctx")),
            P(("seq", "ctx")),
            P(("seq", "ctx")),
            P(("seq", "ctx"), None),
            P(("seq", "ctx")),
            P(("seq", "ctx"), None),
            P(("seq", "ctx")),
            P(("seq", "ctx")),
            P(("seq", "ctx")),
        ),
        check_vma=False,
    )
```
